256 devices in a mesh: pool: 2 (over core), ep: 64 (over x_hi, z, y), tp: 2 (over x_lo).
Axes of the slice: x: 4 (x_hi: 2, x_lo: 2; x = x_hi * 2 + x_lo), y: 4, z: 8, core: 2. Of those that a mesh axis runs over, the one named last changes fastest.
Arguments:
- latent_pages: bfloat16 [16384, 16, 576], P(('pool', 'ep')), may hold values from -6.1 to 6.1
- page_table: int32 [4096, 4], P(('pool', 'ep')), may hold values from 0 to 127, as said below
- lengths: int32 [4096], P(('pool', 'ep')), may hold values from 1 to 63, as said below
- new_place: int32 [4096], P(('pool', 'ep')), may hold values from 0 to 2047, as said below
- queries: bfloat16 [4096, 64, 576], P(('pool', 'ep'), 'tp'), may hold values from -90 to 90
- fresh_latent: bfloat16 [4096, 576], P(('pool', 'ep')), may hold values from -6 to 6
- hidden_states: bfloat16 [4096, 3584], P(('pool', 'ep')), may hold values from -6 to 6
- routing: int32 [4096, 8], P(('pool', 'ep')), may hold values from 0 to 63, all different within a row; in each aligned block of 32 rows (0 to 31, 32 to 63, ...) at most 8 rows name the same one
- route_weight: float32 [4096, 8], P(('pool', 'ep')), may hold values from 0.05 to 0.5
- gate_value: bfloat16 [64, 3584, 1024], P('ep', None, ('pool', 'tp')), may hold values from -0.09375 to 0.09375
- gate_scale: bfloat16 [64, 28, 8], P('ep', None, ('pool', 'tp')), may hold values from 0.5 to 2
- up_value: bfloat16 [64, 3584, 1024], P('ep', None, ('pool', 'tp')), may hold values from -0.09375 to 0.09375
- up_scale: bfloat16 [64, 28, 8], P('ep', None, ('pool', 'tp')), may hold values from 0.5 to 2
- down_value: bfloat16 [64, 1024, 3584], P('ep', ('pool', 'tp')), may hold values from -0.1875 to 0.1875
- down_scale: bfloat16 [64, 8, 28], P('ep', ('pool', 'tp')), may hold values from 0.5 to 2
Outputs:
- new_cache: bfloat16 [4096, 64, 576], P(('pool', 'ep'))
- latent_attention_output: bfloat16 [4096, 64, 512], P(('pool', 'ep'), 'tp')
- expert_mix: bfloat16 [4096, 3584], P(('pool', 'ep'), 'tp')
The draws below stay inside these ranges and needn't reach their ends.
Inputs may be any that keep to these rules, and one draw needn't show every extreme that they name: `page_table`: the rows of each device's 32 trajectories name every index of that device's 32 * 4 pages exactly once. `lengths`: no trajectory fills its cache; every device holds one trajectory of length 63. Within each group of 2048 trajectories along pool, new_place is a permutation; the new owner along ep is new_place // 32. Each device hands at most 1 trajectories to any one device, and exactly 1 to some device. `routing`: each token names 8 different experts; among the 32 rows of one device no expert is named more than 8 times, a bound that some block reaches.
All inputs are finite; a program needn't handle non-finite values.
Results may differ from the reference program's by a relative error of at most 0.0076.
Values may be sent and summed in bfloat16 or wider, within the bound.
No kernel may reach another device: no remote copies, remote signals or barrier semaphores. Data moves between devices by JAX's collectives and lax.ppermute only.
A program may use at most 128 MiB of HBM per device.

```python
import math
import jax
import jax.numpy as jnp
import numpy as np
from jax import lax

D = 3584
FF = 1024
ATTENTION_HEADS = 64
LATENT_WIDTH = 512
BLOCK = 128
MAXLEN = 64
PAGE = 16
TRAJ = 32
LATENT = 576
PAGES_PER = 4
TOPK = 8
EXPERTS = 64
CAP = 8
PAIR = 1
HALF = 2048
TOTAL_TOKENS = 4096


def draw_latent_pages(key, part):
    shape = (TOTAL_TOKENS * PAGES_PER, PAGE, LATENT)
    base_offset = jnp.clip(jax.random.normal(jax.random.fold_in(key, 11), shape, jnp.float32), -6.0, 6.0)
    return base_offset.astype(jnp.bfloat16)


def draw_queries(key, part):
    shape = (TOTAL_TOKENS, ATTENTION_HEADS, LATENT)
    base_offset = jnp.clip(jax.random.normal(jax.random.fold_in(key, 21), shape, jnp.float32), -6.0, 6.0)
    return base_offset.astype(jnp.bfloat16)


def draw_page_table(key, part):
    blocks = TOTAL_TOKENS // TRAJ
    block_keys = jax.random.split(jax.random.fold_in(key, 31), blocks)
    orders = jax.vmap(lambda block_key: jax.random.permutation(block_key, TRAJ * PAGES_PER))(block_keys)
    return orders.reshape(TOTAL_TOKENS, PAGES_PER).astype(jnp.int32)


def draw_lengths(key, part):
    blocks = TOTAL_TOKENS // TRAJ
    base_offset = jax.random.randint(jax.random.fold_in(key, 41), (TOTAL_TOKENS,), 1, MAXLEN)
    chosen = jax.random.randint(jax.random.fold_in(key, 42), (blocks, 1), 0, TRAJ)
    local_index = lax.broadcasted_iota(jnp.int32, (blocks, TRAJ), 1)
    longest = (local_index == chosen).reshape(TOTAL_TOKENS)
    return jnp.where(longest, MAXLEN - 1, base_offset).astype(jnp.int32)


def place_group(group_key):
    device_count = HALF // TRAJ
    pair_cap = PAIR
    key_a, key_b, key_c, key_d, key_e = jax.random.split(group_key, 5)
    relabel_send = jax.random.permutation(key_a, device_count)
    relabel_take = jax.random.permutation(key_b, device_count)
    slot_scores = jax.random.permutation(key_c, device_count * pair_cap)
    forced = jax.random.randint(key_d, (), 0, device_count)
    slot_offset = jnp.arange(device_count * pair_cap, dtype=jnp.int32) // pair_cap
    slot_scores = jnp.where(slot_offset == forced, slot_scores - device_count * pair_cap, slot_scores)
    ordering = jnp.argsort(slot_scores)
    offsets = (ordering[:TRAJ] // pair_cap).astype(jnp.int32)
    local_keys = jax.random.split(key_e, device_count)
    local_slots = jax.vmap(lambda local_key: jax.random.permutation(local_key, TRAJ))(local_keys).astype(jnp.int32)
    sender = jnp.arange(device_count, dtype=jnp.int32)[:, None]
    new_owner = relabel_take[(relabel_send[sender] + offsets[local_slots]) % device_count]
    return (new_owner * TRAJ + local_slots).reshape(HALF).astype(jnp.int32)


def draw_new_place(key, part):
    groups = [place_group(jax.random.fold_in(key, 50 + group)) for group in range(TOTAL_TOKENS // HALF)]
    return jnp.concatenate(groups, axis=0)


def block_scale(own_key, shape, shards, smallest, top_value):
    def one(dim, shards_of):
        steps = jax.random.uniform(jax.random.fold_in(jax.random.fold_in(own_key, 6), dim), (shards_of,), jnp.float32, smallest / len(shards), top_value / len(shards))
        return jnp.repeat(jnp.exp(steps), shape[dim] // shards_of).reshape((-1,) + (1,) * (len(shape) - dim - 1))

    gain = one(*shards[0])
    for cut in shards[1:]:
        gain = gain * one(*cut)
    return gain


def shared_out(rng, own, number, rows, number_of, top, reach, slope):
    sequence = jax.random.permutation(rng, number_of)
    heavy_load, usual = portions_of(number_of, rows * top, reach, slope, True), portions_of(number_of, rows * top, reach, slope, False)
    places = jnp.arange(number_of)

    def named(tallies, offset_by):
        used = int((tallies > 0).sum())
        fixed = max(1, used // 4)
        shifted = fixed + (places - fixed + offset_by * (used - fixed)) % max(1, number_of - fixed)
        return jnp.zeros((number_of,), jnp.int32).at[sequence[jnp.where(places < fixed, places, shifted)]].set(jnp.asarray(tallies, jnp.int32))

    tallies = jnp.where(number % 4 == 0, named(heavy_load, number // 4), named(usual, number - number // 4 - 1))
    mixed = jax.random.permutation(jax.random.fold_in(own, 3), number_of)
    giver, receiver = mixed[0:number_of // 2 * 2:2], mixed[1:number_of // 2 * 2:2]
    margin = jnp.minimum(tallies[giver] - 1, reach - tallies[receiver]) // 2
    margin = jnp.where((giver == sequence[0]) | (receiver == sequence[0]) | (tallies[receiver] == 0), 0, jnp.maximum(margin, 0))
    shifted = jax.random.randint(jax.random.fold_in(own, 4), (number_of // 2,), 0, 1 << 20) % (margin + 1)
    tallies = tallies.at[giver].add(-shifted).at[receiver].add(shifted)
    items = jnp.searchsorted(jnp.cumsum(tallies), jnp.arange(rows * top), side="right").astype(jnp.int32)
    listing = items.reshape(top, rows).T
    listing = listing[jax.random.permutation(jax.random.fold_in(own, 1), rows)]
    offset_by = jax.random.randint(jax.random.fold_in(own, 2), (rows, 1), 0, top)
    return jnp.take_along_axis(listing, (jnp.arange(top)[None, :] + offset_by) % top, axis=1)


def portions_of(count, total, limit, slope, full):
    portions = [(1 << 20) // math.isqrt(standing ** slope) + 1 for standing in range(1, count + 1)]
    largest = limit if full else min(limit, max(-(-total // count), total * portions[0] // sum(portions)))
    least = 1 if total - largest >= count - 1 else 0
    counts, surplus = [largest] + [least] * (count - 1), total - largest - least * (count - 1)
    while surplus > 0:
        candidates = [i for i in range(1, count) if counts[i] < largest] or [i for i in range(1, count) if counts[i] < limit]
        pool, budget = sum([portions[i] for i in candidates]), surplus
        for i in candidates:
            more = min(limit - counts[i], max(1, budget * portions[i] // pool), surplus)
            counts[i] = counts[i] + more
            surplus = surplus - more
    return np.array(counts)


def noise(key, extent, width, most, pieces=(), kind=jnp.bfloat16):
    entries = width * jax.random.normal(key, extent, jnp.float32)
    if pieces:
        entries = entries * block_scale(key, extent, pieces, -0.22, 0.18)
    return jnp.clip(entries, -most, most).astype(kind)


def setup_inputs(seed: int = 0) -> dict:
    keys = jax.random.split(jax.random.key(seed), 16)
    latent_pages = draw_latent_pages(jax.random.fold_in(keys[15], 71), 0)
    page_table = draw_page_table(jax.random.fold_in(keys[15], 71), 0)
    lengths = draw_lengths(jax.random.fold_in(keys[15], 71), 0)
    new_place = draw_new_place(jax.random.fold_in(keys[15], 71), 0)
    queries = draw_queries(jax.random.fold_in(keys[15], 71), 0)
    fresh_latent = noise(keys[5], (TOTAL_TOKENS, LATENT), 1.0, 6.0, ((0, 128),))
    hidden_states = noise(keys[6], (TOTAL_TOKENS, D), 1.0, 6.0, ((0, 128),))
    routing_keys = jax.random.split(jax.random.fold_in(keys[7], 1), TOTAL_TOKENS // TRAJ)
    routing_turns = jax.random.permutation(jax.random.fold_in(keys[7], 3), TOTAL_TOKENS // TRAJ)
    routing = jax.vmap(lambda own, number: shared_out(jax.random.fold_in(keys[7], 2), own, number, TRAJ, EXPERTS, TOPK, CAP, 2))(routing_keys, routing_turns).reshape((TOTAL_TOKENS, TOPK))
    route_weight = jnp.clip(0.05 + 0.45 * jax.random.uniform(keys[8], (TOTAL_TOKENS, TOPK), jnp.float32) ** block_scale(keys[8], (TOTAL_TOKENS, TOPK), ((0, 128),), -0.2, 0.2), 0.05, 0.5)
    gate_value = noise(keys[9], (EXPERTS, D, FF), D ** -0.5, 0.09375, ((0, 64), (2, 4)))
    gate_scale = jnp.clip(jnp.exp(math.log(2.0) - 1.3862944 * jax.random.uniform(keys[10], (EXPERTS, D // BLOCK, FF // BLOCK), jnp.float32) ** block_scale(keys[10], (EXPERTS, D // BLOCK, FF // BLOCK), ((0, 64), (2, 4)), -0.2, 0.2)), 0.5, 2.0).astype(jnp.bfloat16)
    up_value = noise(keys[11], (EXPERTS, D, FF), D ** -0.5, 0.09375, ((0, 64), (2, 4)))
    up_scale = jnp.clip(jnp.exp(math.log(2.0) - 1.3862944 * jax.random.uniform(keys[12], (EXPERTS, D // BLOCK, FF // BLOCK), jnp.float32) ** block_scale(keys[12], (EXPERTS, D // BLOCK, FF // BLOCK), ((0, 64), (2, 4)), -0.2, 0.2)), 0.5, 2.0).astype(jnp.bfloat16)
    down_value = noise(keys[13], (EXPERTS, FF, D), FF ** -0.5, 0.1875, ((0, 64), (1, 4)))
    down_scale = jnp.clip(jnp.exp(math.log(2.0) - 1.3862944 * jax.random.uniform(keys[14], (EXPERTS, FF // BLOCK, D // BLOCK), jnp.float32) ** block_scale(keys[14], (EXPERTS, FF // BLOCK, D // BLOCK), ((0, 64), (1, 4)), -0.2, 0.2)), 0.5, 2.0).astype(jnp.bfloat16)
    return dict(latent_pages=latent_pages, page_table=page_table, lengths=lengths, new_place=new_place, queries=queries, fresh_latent=fresh_latent, hidden_states=hidden_states, routing=routing, route_weight=route_weight, gate_value=gate_value, gate_scale=gate_scale, up_value=up_value, up_scale=up_scale, down_value=down_value, down_scale=down_scale)


score_scale = 192.0 ** -0.5


def dequant(value_rows, scales):
    scale_wide = jnp.repeat(jnp.repeat(scales.astype(jnp.float32), BLOCK, axis=0), BLOCK, axis=1)
    return (value_rows.astype(jnp.float32) * scale_wide).astype(jnp.bfloat16)


def attend(query_block, compressed_latent_cache, length_block):
    scores = jnp.einsum("rhc,rtc->rht", query_block.astype(jnp.float32), compressed_latent_cache.astype(jnp.float32)) * score_scale
    positions = jnp.arange(compressed_latent_cache.shape[1], dtype=jnp.int32)
    valid = positions[None, None, :] <= length_block[:, None, None]
    scores = jnp.where(valid, scores, -jnp.inf)
    attention_weights = jax.nn.softmax(scores, axis=-1).astype(jnp.bfloat16)
    value_rows = compressed_latent_cache[:, :, :LATENT_WIDTH].astype(jnp.float32)
    return jnp.einsum("djm,dmc->djc", attention_weights.astype(jnp.float32), value_rows).astype(jnp.bfloat16)


def reference(latent_pages, page_table, lengths, new_place, queries, fresh_latent, hidden_states, routing, route_weight, gate_value, gate_scale, up_value, up_scale, down_value, down_scale):
    blocks = TOTAL_TOKENS // TRAJ
    page_blocks = latent_pages.reshape(blocks, TRAJ * PAGES_PER, PAGE, LATENT)
    table_blocks = page_table.reshape(blocks, TRAJ * PAGES_PER)
    old_cache = jax.vmap(lambda page_block, table_block: page_block[table_block])(page_blocks, table_blocks)
    old_cache = old_cache.reshape(TOTAL_TOKENS, MAXLEN, LATENT)
    group_index = jnp.arange(TOTAL_TOKENS, dtype=jnp.int32) // HALF
    new_slot = group_index * HALF + new_place
    source = jnp.zeros((TOTAL_TOKENS,), jnp.int32).at[new_slot].set(jnp.arange(TOTAL_TOKENS, dtype=jnp.int32))
    moved = old_cache[source]
    new_length = lengths[source]
    positions = jnp.arange(MAXLEN, dtype=jnp.int32)[None, :, None]
    fill_len = new_length[:, None, None]
    new_cache = jnp.where(positions < fill_len, moved, jnp.where(positions == fill_len, fresh_latent[:, None, :], jnp.zeros((), jnp.bfloat16)))

    packed = (queries.reshape(blocks, TRAJ, ATTENTION_HEADS, LATENT), new_cache.reshape(blocks, TRAJ, MAXLEN, LATENT), new_length.reshape(blocks, TRAJ))
    attended_value = lax.map(lambda group: attend(group[0], group[1], group[2]), packed)
    latent_attention_output = attended_value.reshape(TOTAL_TOKENS, ATTENTION_HEADS, LATENT_WIDTH)

    row_bound = CAP * blocks

    def expert_step(summed, expert):
        routed = routing == expert
        picked = jnp.any(routed, axis=1)
        rows_at = jnp.nonzero(picked, size=row_bound, fill_value=0)[0].astype(jnp.int32)
        filled_row = jnp.arange(row_bound, dtype=jnp.int32) < jnp.sum(picked.astype(jnp.int32))
        token_share = jnp.sum(jnp.where(routed, route_weight, jnp.zeros((), jnp.float32)), axis=1)[rows_at]
        token_share = jnp.where(filled_row, token_share, jnp.zeros((), jnp.float32))
        slot_rows = hidden_states[rows_at]
        gate_w = dequant(gate_value[expert], gate_scale[expert])
        up_w = dequant(up_value[expert], up_scale[expert])
        down_w = dequant(down_value[expert], down_scale[expert])
        gate_act = jnp.dot(slot_rows, gate_w, preferred_element_type=jnp.float32)
        up_act = jnp.dot(slot_rows, up_w, preferred_element_type=jnp.float32)
        hidden_act = (jax.nn.silu(gate_act) * up_act).astype(jnp.bfloat16)
        expert_out = jnp.dot(hidden_act, down_w, preferred_element_type=jnp.float32).astype(jnp.bfloat16)
        expert_out = lax.optimization_barrier(expert_out).astype(jnp.float32)
        return summed.at[rows_at].add(token_share[:, None] * expert_out), None

    summed, _ = lax.scan(expert_step, jnp.zeros((TOTAL_TOKENS, D), jnp.float32), jnp.arange(EXPERTS, dtype=jnp.int32))
    expert_mix = summed.astype(jnp.bfloat16)
    return new_cache, latent_attention_output, expert_mix
```

```python
import functools

import jax
import jax.numpy as jnp
from jax import lax
from jax.experimental import pallas as pl
from jax.experimental.pallas import tpu as pltpu
from jax.sharding import Mesh, PartitionSpec as P

F32, BF16, I32 = jnp.float32, jnp.bfloat16, jnp.int32
LATENT_WIDTH = 512
BLOCK = 128
MAXLEN = 64
LATENT = 576
LANES = 640
D = 3584
HALF_D = 1792
TRAJ = 32
CAP = 8
NZ, NY, NX = 8, 4, 2
EP = NZ * NY * NX
SCORE_SCALE = 192.0 ** (-0.5)
MB = 1024 * 1024

SMEM = pltpu.SMEM


def whole(shape):
    return pl.BlockSpec(shape, lambda *_: (0,) * len(shape))


def smem():
    return pl.BlockSpec(memory_space=SMEM)


def params(mb):
    return pltpu.CompilerParams(vmem_limit_bytes=mb * MB)


def cost(flops, nbytes):
    return pl.CostEstimate(flops=int(flops), bytes_accessed=int(nbytes), transcendentals=0)


def panel_kernel(tp_ref, gs, us, ds, gv, uv, dv, g_out, u_out, keep_out, send_out):
    step = pl.program_id(0)
    for a in range(2):
        for f in range(2):
            rows, cols = slice(a * BLOCK, (a + 1) * BLOCK), slice(f * BLOCK, (f + 1) * BLOCK)
            at = (step * 2 + a) * 2 + f
            g_out[rows, cols] = (gv[0, rows, cols].astype(F32) * gs[at]).astype(BF16)
            u_out[rows, cols] = (uv[0, rows, cols].astype(F32) * us[at]).astype(BF16)
    half = jnp.where(step < 7, tp_ref[0], 1 - tp_ref[0])
    column = half * 14 + jnp.where(step < 7, step, step - 7) * 2

    def down(out):
        for a in range(2):
            for f in range(2):
                rows, cols = slice(a * BLOCK, (a + 1) * BLOCK), slice(f * BLOCK, (f + 1) * BLOCK)
                out[rows, cols] = (
                    dv[0, rows, cols].astype(F32) * ds[a * 28 + column + f]
                ).astype(BF16)

    @pl.when(step < 7)
    def _():
        down(keep_out)

    @pl.when(step >= 7)
    def _():
        down(send_out)


def scale_panels(tp_index, gate_value, gate_scale, up_value, up_scale, down_value, down_scale):
    def flat(scale):
        return scale.astype(F32).reshape(-1)

    def down_at(i, t):
        return (0, 0, jnp.where(i < 7, t[0] * 7 + i, (1 - t[0]) * 7 + i - 7))

    return pl.pallas_call(
        panel_kernel,
        grid_spec=pltpu.PrefetchScalarGridSpec(
            num_scalar_prefetch=1,
            grid=(14,),
            in_specs=[
                smem(),
                smem(),
                smem(),
                pl.BlockSpec((1, 256, 256), lambda i, t: (0, i, 0)),
                pl.BlockSpec((1, 256, 256), lambda i, t: (0, i, 0)),
                pl.BlockSpec((1, 256, 256), down_at),
            ],
            out_specs=[
                pl.BlockSpec((256, 256), lambda i, t: (i, 0)),
                pl.BlockSpec((256, 256), lambda i, t: (i, 0)),
                pl.BlockSpec((256, 256), lambda i, t: (0, jnp.minimum(i, 6))),
                pl.BlockSpec((256, 256), lambda i, t: (0, jnp.maximum(i - 7, 0))),
            ],
        ),
        out_shape=[
            jax.ShapeDtypeStruct((D, 256), BF16),
            jax.ShapeDtypeStruct((D, 256), BF16),
            jax.ShapeDtypeStruct((256, HALF_D), BF16),
            jax.ShapeDtypeStruct((256, HALF_D), BF16),
        ],
        compiler_params=params(16),
        cost_estimate=cost(3e6, 11e6),
        name="scale_panels",
    )(
        tp_index,
        flat(gate_scale),
        flat(up_scale),
        flat(down_scale),
        gate_value,
        up_value,
        down_value,
    )


def named_by(routing, experts):
    marks = jnp.zeros((routing.shape[0], experts.shape[1]), F32)
    for k in range(routing.shape[1]):
        marks = marks + (routing[:, k : k + 1] == experts).astype(F32)
    return marks


def earlier(marks):
    n = marks.shape[0]
    lower = (
        lax.broadcasted_iota(I32, (n, n), 0) > lax.broadcasted_iota(I32, (n, n), 1)
    ).astype(BF16)
    return jnp.dot(lower, marks.astype(BF16), preferred_element_type=F32)


def pick_kernel(place_ref, *refs):
    blocks, outs = refs[:NZ], refs[NZ:]
    xh, z, y = place_ref[0], place_ref[1], place_ref[2]
    column = lax.broadcasted_iota(I32, (1, EP), 1)
    peer, slot = column >> 3, column & 7
    experts = (((peer >> 2) ^ xh) * NZ + z) * NY + (((peer & 3) + y) & 3)
    for b, block in enumerate(blocks):
        routing = block[:, D : D + 8].astype(F32).astype(I32)
        marks = named_by(routing, experts)
        chosen = jnp.where(earlier(marks) == slot.astype(F32), marks, 0.0).astype(BF16)
        rows = lax.dot_general(
            chosen,
            block[:, :D],
            (((0,), (0,)), ((), ())),
            preferred_element_type=F32,
        ).astype(BF16)
        for r, out in enumerate(outs):
            out[b * CAP : (b + 1) * CAP, :] = rows[r * CAP : (r + 1) * CAP, :]


def pick_rows(place, blocks):
    return pl.pallas_call(
        pick_kernel,
        in_specs=[smem()] + [pl.BlockSpec(memory_space=pltpu.VMEM)] * NZ,
        out_specs=[pl.BlockSpec(memory_space=pltpu.VMEM)] * 8,
        out_shape=[jax.ShapeDtypeStruct((NZ * CAP, D), BF16)] * 8,
        compiler_params=params(24),
        cost_estimate=cost(1e9, 6e6),
        name="pick_rows",
    )(place, *blocks)


def hidden_kernel(*refs):
    tokens, (g0, g1, u0, u1, out), (acc_g, acc_u) = refs[:8], refs[8:13], refs[13:]
    step = pl.program_id(0)

    @pl.when(step == 0)
    def _():
        acc_g[...] = jnp.zeros_like(acc_g)
        acc_u[...] = jnp.zeros_like(acc_u)

    x = jnp.concatenate([t[...] for t in tokens], axis=0)
    acc_g[:, :256] += jnp.dot(x, g0[...], preferred_element_type=F32)
    acc_u[:, :256] += jnp.dot(x, u0[...], preferred_element_type=F32)
    acc_g[:, 256:] += jnp.dot(x, g1[...], preferred_element_type=F32)
    acc_u[:, 256:] += jnp.dot(x, u1[...], preferred_element_type=F32)

    @pl.when(step == pl.num_programs(0) - 1)
    def _():
        g = acc_g[...]
        out[...] = (g / (1.0 + jnp.exp(-g)) * acc_u[...]).astype(BF16)


def hidden_units(tokens, g0, g1, u0, u1):
    depth = 512
    return pl.pallas_call(
        hidden_kernel,
        grid=(D // depth,),
        in_specs=[pl.BlockSpec((64, depth), lambda k: (0, k))] * 8
        + [pl.BlockSpec((depth, 256), lambda k: (k, 0))] * 4,
        out_specs=whole((512, 512)),
        out_shape=jax.ShapeDtypeStruct((512, 512), BF16),
        scratch_shapes=[pltpu.VMEM((512, 512), F32)] * 2,
        compiler_params=params(24),
        cost_estimate=cost(3.8e9, 12e6),
        name="hidden_units",
    )(*tokens, g0, g1, u0, u1)


def down_kernel(order_ref, h0, h1, w0, w1, w2, w3, out):
    h = jnp.concatenate([h0[...], h1[...]], axis=1)
    w = jnp.concatenate([w0[...], w1[...], w2[...], w3[...]], axis=0)
    rows = jnp.dot(h, w, preferred_element_type=F32)
    for group in range(EP):
        out[order_ref[group]] = rows[group * CAP : (group + 1) * CAP, :].astype(BF16)


def down_rows(order, h0, h1, weights):
    wide = 256
    return pl.pallas_call(
        down_kernel,
        grid=(HALF_D // wide,),
        in_specs=[smem(), whole((512, 512)), whole((512, 512))]
        + [pl.BlockSpec((256, wide), lambda i: (0, i))] * 4,
        out_specs=pl.BlockSpec((EP, CAP, wide), lambda i: (0, 0, i)),
        out_shape=jax.ShapeDtypeStruct((EP, CAP, HALF_D), BF16),
        compiler_params=params(24),
        cost_estimate=cost(1.9e9, 7e6),
        name="down_rows",
    )(order, h0, h1, *weights)


def blend_kernel(routing_ref, weight_ref, rows_ref, out):
    column = lax.broadcasted_iota(I32, (1, EP * CAP), 1)
    experts, slot = column >> 3, column & 7
    routing, weight = routing_ref[...], weight_ref[...]
    marks = jnp.zeros((TRAJ, EP * CAP), F32)
    share = jnp.zeros((TRAJ, EP * CAP), F32)
    for k in range(8):
        hit = routing[:, k : k + 1] == experts
        marks = marks + hit.astype(F32)
        share = share + jnp.where(hit, weight[:, k : k + 1], 0.0)
    share = jnp.where(earlier(marks) == slot.astype(F32), share, 0.0)
    high = share.astype(BF16)
    low = (share - high.astype(F32)).astype(BF16)
    rows = rows_ref[...].reshape(EP * CAP, rows_ref.shape[2])
    out[...] = (
        jnp.dot(high, rows, preferred_element_type=F32)
        + jnp.dot(low, rows, preferred_element_type=F32)
    ).astype(BF16)


def blend(routing, weight, rows):
    wide = 896
    return pl.pallas_call(
        blend_kernel,
        grid=(HALF_D // wide,),
        in_specs=[
            whole((TRAJ, 8)),
            whole((TRAJ, 8)),
            pl.BlockSpec((EP, CAP, wide), lambda i: (0, 0, i)),
        ],
        out_specs=pl.BlockSpec((TRAJ, wide), lambda i: (0, i)),
        out_shape=jax.ShapeDtypeStruct((TRAJ, HALF_D), BF16),
        compiler_params=params(16),
        cost_estimate=cost(1e8, 2e6),
        name="blend",
    )(routing, weight, rows)


def collect_kernel(index_ref, pages, out):
    lane = lax.broadcasted_iota(I32, (32, LANES - 512), 1)

    def body(j, carry):
        first, second = index_ref[j, 0], index_ref[j, 1]
        slot, length = index_ref[j, 2].astype(F32), index_ref[j, 3].astype(F32)
        out[j, 0:16, 0:LATENT] = pages[first]
        out[j, 16:32, 0:LATENT] = pages[second]
        label = jnp.where(lane[:, 64:] == 64, slot, length).astype(BF16)
        out[j, :, LATENT:LANES] = label
        return carry

    lax.fori_loop(0, EP, body, 0)


def collect(index, pages):
    return pl.pallas_call(
        collect_kernel,
        in_specs=[smem(), pl.BlockSpec(memory_space=pltpu.VMEM)],
        out_specs=pl.BlockSpec(memory_space=pltpu.VMEM),
        out_shape=jax.ShapeDtypeStruct((EP, 32, LANES), BF16),
        compiler_params=params(16),
        cost_estimate=cost(1e6, 6e6),
        name="collect",
    )(index, pages)


def compact_kernel(source_ref, arrived, out, sem):
    copies = [
        pltpu.make_async_copy(arrived.at[source_ref[s]], out.at[s], sem.at[s])
        for s in range(TRAJ)
    ]
    for copy in copies:
        copy.start()
    for copy in copies:
        copy.wait()


def compact(source, arrived):
    return pl.pallas_call(
        compact_kernel,
        in_specs=[smem(), pl.BlockSpec(memory_space=pl.ANY)],
        out_specs=pl.BlockSpec(memory_space=pl.ANY),
        out_shape=jax.ShapeDtypeStruct((TRAJ, 32, LANES), BF16),
        scratch_shapes=[pltpu.SemaphoreType.DMA((TRAJ,))],
        cost_estimate=cost(1e6, 3e6),
        name="compact",
    )(source, arrived)


ATTEND_STEP = 4


def attend_kernel(tp_ref, length_ref, mine, other, queries, fresh, cache_out, out):
    step = pl.program_id(0)
    first = tp_ref[0] == 0
    row = lax.broadcasted_iota(I32, (MAXLEN, LATENT), 0)
    column = lax.broadcasted_iota(I32, (TRAJ, MAXLEN), 1)
    for i in range(ATTEND_STEP):
        length = length_ref[step * ATTEND_STEP + i]
        a, b = mine[i, :, :LATENT], other[i, :, :LATENT]
        old = jnp.concatenate([jnp.where(first, a, b), jnp.where(first, b, a)], axis=0)
        new = jnp.broadcast_to(fresh[i], (MAXLEN, LATENT))
        cache = jnp.where(
            row < length,
            old.astype(F32),
            jnp.where(row == length, new.astype(F32), 0.0),
        ).astype(BF16)
        cache_out[i] = cache
        scores = lax.dot_general(
            queries[i], cache, (((1,), (1,)), ((), ())), preferred_element_type=F32
        )
        scores = jnp.where(column <= length, scores * SCORE_SCALE, -jnp.inf)
        top = jnp.max(scores, axis=1, keepdims=True)
        weight = jnp.exp(scores - top)
        weight = (weight / jnp.sum(weight, axis=1, keepdims=True)).astype(BF16)
        out[i] = jnp.dot(
            weight, cache[:, :LATENT_WIDTH], preferred_element_type=F32
        ).astype(BF16)


def attend(tp_index, length, mine, other, queries, fresh):
    n = ATTEND_STEP
    return pl.pallas_call(
        attend_kernel,
        grid=(TRAJ // n,),
        in_specs=[
            smem(),
            smem(),
            pl.BlockSpec((n, 32, LANES), lambda i: (i, 0, 0)),
            pl.BlockSpec((n, 32, LANES), lambda i: (i, 0, 0)),
            pl.BlockSpec((n, 32, LATENT), lambda i: (i, 0, 0)),
            pl.BlockSpec((n, 1, LATENT), lambda i: (i, 0, 0)),
        ],
        out_specs=[
            pl.BlockSpec((n, MAXLEN, LATENT), lambda i: (i, 0, 0)),
            pl.BlockSpec((n, 32, LATENT_WIDTH), lambda i: (i, 0, 0)),
        ],
        out_shape=[
            jax.ShapeDtypeStruct((TRAJ, MAXLEN, LATENT), BF16),
            jax.ShapeDtypeStruct((TRAJ, 32, LATENT_WIDTH), BF16),
        ],
        compiler_params=params(16),
        cost_estimate=cost(2e8, 8e6),
        name="attend",
    )(tp_index, length, mine, other, queries, fresh.reshape(TRAJ, 1, LATENT))


def swap(x, axis):
    return lax.ppermute(x, axis, [(0, 1), (1, 0)])


def z_shift(x, by):
    return lax.ppermute(x, "z", [(i, (i + by) % NZ) for i in range(NZ)])


def plane_shift(x, dx, dy):
    return lax.ppermute(
        x,
        ("xh", "y"),
        [
            (a * NY + b, ((a + dx) % NX) * NY + (b + dy) % NY)
            for a in range(NX)
            for b in range(NY)
        ],
    )


def on_device(
    latent_pages,
    page_table,
    lengths,
    new_place,
    queries,
    fresh_latent,
    hidden_states,
    routing,
    route_weight,
    gate_value,
    gate_scale,
    up_value,
    up_scale,
    down_value,
    down_scale,
):
    xh, z, y, tp = (lax.axis_index(name) for name in ("xh", "z", "y", "tp"))
    tp_index = tp.astype(I32).reshape(1)
    place = jnp.stack([xh, z, y]).astype(I32)

    own = jnp.concatenate(
        [hidden_states, jnp.pad(routing.astype(BF16), ((0, 0), (0, BLOCK - 8)))], axis=1
    )
    up_way, down_way = [own], [own]
    for step in range(4):
        up_way.append(z_shift(up_way[-1], 1))
        if step < 3:
            down_way.append(z_shift(down_way[-1], -1))
    blocks = up_way + down_way[1:]
    behind = [0, 1, 2, 3, 4, -1, -2, -3]

    owner, slot = new_place // TRAJ, new_place % TRAJ
    to_owner = owner[None, :] == jnp.arange(EP, dtype=I32)[:, None]
    mine = lax.dynamic_slice_in_dim(page_table, tp * 2, 2, 1)
    facts = jnp.concatenate([mine, slot[:, None] + 1, lengths[:, None]], axis=1)
    index = jnp.sum(jnp.where(to_owner[:, :, None], facts[None], 0), axis=1)
    index = index - jnp.array([0, 0, 1, 0], I32)[None, :]
    arrived = lax.all_to_all(
        collect(index, latent_pages), ("xh", "z", "y"), split_axis=0, concat_axis=0, tiled=True
    )

    gate, up, down_keep, down_send = scale_panels(
        tp_index, gate_value, gate_scale, up_value, up_scale, down_value, down_scale
    )
    gate_far, up_far = swap(gate, "pool"), swap(up, "pool")
    down_tp = swap(down_send, "tp")
    down_far, down_tp_far = swap(down_keep, "pool"), swap(down_tp, "pool")

    picked = pick_rows(place, blocks)
    tokens = [picked[0]] + [
        plane_shift(picked[dx * NY + dy], dx, dy)
        for dx in range(NX)
        for dy in range(NY)
        if dx or dy
    ]
    act = hidden_units(tokens, gate, gate_far, up, up_far)
    act_tp = swap(act, "tp")
    order = jnp.stack(
        [
            (((xh + dx) % NX) * NZ + (z - b) % NZ) * NY + (y - dy) % NY
            for dx in range(NX)
            for dy in range(NY)
            for b in behind
        ]
    ).astype(I32)
    out_rows = down_rows(order, act, act_tp, [down_keep, down_far, down_tp, down_tp_far])
    returned = lax.all_to_all(
        out_rows, ("xh", "z", "y"), split_axis=0, concat_axis=0, tiled=True
    )
    expert_mix = blend(routing, route_weight, returned)

    labels = arrived[:, 0, LATENT : LATENT + 2].astype(I32)
    taken = labels[:, 0][None, :] == jnp.arange(TRAJ, dtype=I32)[:, None]
    source = jnp.sum(jnp.where(taken, jnp.arange(EP, dtype=I32)[None, :], 0), axis=1)
    length = jnp.sum(jnp.where(taken, labels[:, 1][None, :], 0), axis=1)
    my_half = compact(source, arrived)
    other_half = swap(my_half, "tp")
    new_cache, attention = attend(tp_index, length, my_half, other_half, queries, fresh_latent)
    return new_cache, attention, expert_mix


def solution(mesh):
    grid = Mesh(mesh.devices.reshape(2, NX, NZ, NY, 2), ("pool", "xh", "z", "y", "tp"))
    ep = ("xh", "z", "y")
    rows = ("pool",) + ep
    placed = (
        P(rows, None, None),
        P(rows, None),
        P(rows),
        P(rows),
        P(rows, "tp", None),
        P(rows, None),
        P(rows, None),
        P(rows, None),
        P(rows, None),
        P(ep, None, ("pool", "tp")),
        P(ep, None, ("pool", "tp")),
        P(ep, None, ("pool", "tp")),
        P(ep, None, ("pool", "tp")),
        P(ep, ("pool", "tp"), None),
        P(ep, ("pool", "tp"), None),
    )
    return jax.shard_map(
        on_device,
        mesh=grid,
        in_specs=placed,
        out_specs=(P(rows, None, None), P(rows, "tp", None), P(rows, "tp")),
        check_vma=False,
    )
```

```python
import jax
import jax.numpy as jnp
import numpy as np
from jax import lax
from jax.experimental import pallas as pl
from jax.experimental.pallas import tpu as pltpu
from jax.sharding import Mesh, PartitionSpec as P

F32, BF16, I32 = jnp.float32, jnp.bfloat16, jnp.int32
LATENT_WIDTH = 512
BLOCK = 128
MAXLEN = 64
LATENT = 576
LANES = 640
D = 3584
HALF_D = 1792
TRAJ = 32
CAP = 8
NZ, NY, NX = 8, 4, 2
EP = NZ * NY * NX
SCORE_SCALE = 192.0 ** (-0.5)
MB = 1024 * 1024

SMEM = pltpu.SMEM
PLANE_MAJOR = np.arange(EP, dtype=np.int32).reshape(NX, NZ, NY).transpose(0, 2, 1).reshape(-1)


def whole(shape):
    return pl.BlockSpec(shape, lambda *_: (0,) * len(shape))


def smem():
    return pl.BlockSpec(memory_space=SMEM)


def hbm(*arrays):
    kept = tuple(pltpu.with_memory_space_constraint(x, pltpu.HBM) for x in arrays)
    return kept if len(kept) > 1 else kept[0]


def in_hbm(shape):
    return jax.ShapeDtypeStruct(shape, BF16)


def params(mb):
    return pltpu.CompilerParams(vmem_limit_bytes=mb * MB)


def cost(flops, nbytes):
    return pl.CostEstimate(flops=int(flops), bytes_accessed=int(nbytes), transcendentals=0)


def scaled_blocks(out, value, scale_at):
    for a in range(2):
        for f in range(2):
            rows, cols = slice(a * BLOCK, (a + 1) * BLOCK), slice(f * BLOCK, (f + 1) * BLOCK)
            out[rows, cols] = (value[0, rows, cols].astype(F32) * scale_at(a, f)).astype(BF16)


def wide_kernel(late_ref, gs, us, gv, uv, g_out, u_out):
    step = pl.program_id(0)
    scaled_blocks(g_out, gv, lambda a, f: gs[(step * 2 + a) * 2 + f])
    scaled_blocks(u_out, uv, lambda a, f: us[(step * 2 + a) * 2 + f])


def scale_wide(late, gate_value, gate_scale, up_value, up_scale):
    value = pl.BlockSpec((1, 256, 256), lambda i: (0, i, 0))
    return pl.pallas_call(
        wide_kernel,
        grid=(14,),
        in_specs=[smem(), smem(), smem(), value, value],
        out_specs=[pl.BlockSpec((256, 256), lambda i: (i, 0))] * 2,
        out_shape=[in_hbm((D, 256))] * 2,
        compiler_params=params(16),
        cost_estimate=cost(2e6, 7e6),
        name="scale_wide",
    )(
        late,
        gate_scale.astype(F32).reshape(-1),
        up_scale.astype(F32).reshape(-1),
        *hbm(gate_value, up_value),
    )


def down_panel_kernel(tp_ref, ds, dv, keep_out, send_out):
    step = pl.program_id(0)
    half = jnp.where(step < 7, 1 - tp_ref[0], tp_ref[0])
    column = half * 14 + jnp.where(step < 7, step, step - 7) * 2

    @pl.when(step < 7)
    def _():
        scaled_blocks(send_out, dv, lambda a, f: ds[a * 28 + column + f])

    @pl.when(step >= 7)
    def _():
        scaled_blocks(keep_out, dv, lambda a, f: ds[a * 28 + column + f])


def scale_down(tp_index, down_value, down_scale):
    def value_at(i, t):
        return (0, 0, jnp.where(i < 7, (1 - t[0]) * 7 + i, t[0] * 7 + i - 7))

    return pl.pallas_call(
        down_panel_kernel,
        grid_spec=pltpu.PrefetchScalarGridSpec(
            num_scalar_prefetch=1,
            grid=(14,),
            in_specs=[smem(), pl.BlockSpec((1, 256, 256), value_at)],
            out_specs=[
                pl.BlockSpec((256, 256), lambda i, t: (0, jnp.maximum(i - 7, 0))),
                pl.BlockSpec((256, 256), lambda i, t: (0, jnp.minimum(i, 6))),
            ],
        ),
        out_shape=[in_hbm((256, HALF_D))] * 2,
        compiler_params=params(16),
        cost_estimate=cost(1e6, 4e6),
        name="scale_down",
    )(tp_index, down_scale.astype(F32).reshape(-1), hbm(down_value))


def named_by(routing, experts):
    marks = jnp.zeros((routing.shape[0], experts.shape[1]), F32)
    for k in range(routing.shape[1]):
        marks = marks + (routing[:, k : k + 1] == experts).astype(F32)
    return marks


def earlier(marks):
    n = marks.shape[0]
    lower = (
        lax.broadcasted_iota(I32, (n, n), 0) > lax.broadcasted_iota(I32, (n, n), 1)
    ).astype(BF16)
    return jnp.dot(lower, marks.astype(BF16), preferred_element_type=F32)


def pick_kernel(place_ref, *refs):
    names, blocks, outs, chosen_ref = refs[:NZ], refs[NZ : 2 * NZ], refs[2 * NZ : -1], refs[-1]

    @pl.when(pl.program_id(0) == 0)
    def _():
        xh, z, y = place_ref[0], place_ref[1], place_ref[2]
        column = lax.broadcasted_iota(I32, (1, EP), 1)
        peer, slot = column >> 3, column & 7
        experts = (((peer >> 2) ^ xh) * NZ + z) * NY + (((peer & 3) + y) & 3)
        for b, name in enumerate(names):
            marks = named_by(name[...].astype(F32).astype(I32)[:, :8], experts)
            chosen_ref[b] = jnp.where(earlier(marks) == slot.astype(F32), marks, 0.0).astype(BF16)

    for b, block in enumerate(blocks):
        rows = lax.dot_general(
            chosen_ref[b],
            block[...],
            (((0,), (0,)), ((), ())),
            preferred_element_type=F32,
        ).astype(BF16)
        for r, out in enumerate(outs):
            out[b * CAP : (b + 1) * CAP, :] = rows[r * CAP : (r + 1) * CAP, :]


def pick_rows(place, blocks):
    wide = 896
    return pl.pallas_call(
        pick_kernel,
        grid=(D // wide,),
        in_specs=[smem()]
        + [pl.BlockSpec((TRAJ, BLOCK), lambda i: (0, D // BLOCK))] * NZ
        + [pl.BlockSpec((TRAJ, wide), lambda i: (0, i))] * NZ,
        out_specs=[pl.BlockSpec((NZ * CAP, wide), lambda i: (0, i))] * 8,
        out_shape=[in_hbm((NZ * CAP, D))] * 8,
        scratch_shapes=[pltpu.VMEM((NZ, TRAJ, EP), BF16)],
        compiler_params=params(16),
        cost_estimate=cost(1e9, 6e6),
        name="pick_rows",
    )(place, *blocks, *blocks)


def hidden_kernel(*refs):
    tokens, (g0, g1, u0, u1, out), (acc_g, acc_u) = refs[:8], refs[8:13], refs[13:]
    step = pl.program_id(0)

    @pl.when(step == 0)
    def _():
        acc_g[...] = jnp.zeros_like(acc_g)
        acc_u[...] = jnp.zeros_like(acc_u)

    x = jnp.concatenate([t[...] for t in tokens], axis=0)
    acc_g[:, :256] += jnp.dot(x, g0[...], preferred_element_type=F32)
    acc_u[:, :256] += jnp.dot(x, u0[...], preferred_element_type=F32)
    acc_g[:, 256:] += jnp.dot(x, g1[...], preferred_element_type=F32)
    acc_u[:, 256:] += jnp.dot(x, u1[...], preferred_element_type=F32)

    @pl.when(step == pl.num_programs(0) - 1)
    def _():
        g = acc_g[...]
        out[...] = (g / (1.0 + jnp.exp(-g)) * acc_u[...]).astype(BF16)


def hidden_units(tokens, g0, g1, u0, u1):
    depth = 512
    return pl.pallas_call(
        hidden_kernel,
        grid=(D // depth,),
        in_specs=[pl.BlockSpec((64, depth), lambda k: (0, k))] * 8
        + [pl.BlockSpec((depth, 256), lambda k: (k, 0))] * 4,
        out_specs=whole((512, 512)),
        out_shape=jax.ShapeDtypeStruct((512, 512), BF16),
        scratch_shapes=[pltpu.VMEM((512, 512), F32)] * 2,
        compiler_params=params(24),
        cost_estimate=cost(3.8e9, 12e6),
        name="hidden_units",
    )(*tokens, g0, g1, u0, u1)


def down_kernel(order_ref, h0, h1, w0, w1, w2, w3, out):
    h = jnp.concatenate([h0[...], h1[...]], axis=1)
    w = jnp.concatenate([w0[...], w1[...], w2[...], w3[...]], axis=0)
    rows = jnp.dot(h, w, preferred_element_type=F32)
    for group in range(EP):
        out[order_ref[group]] = rows[group * CAP : (group + 1) * CAP, :].astype(BF16)


def down_rows(order, h0, h1, weights):
    wide = 256
    return pl.pallas_call(
        down_kernel,
        grid=(HALF_D // wide,),
        in_specs=[smem(), whole((512, 512)), whole((512, 512))]
        + [pl.BlockSpec((256, wide), lambda i: (0, i))] * 4,
        out_specs=pl.BlockSpec((EP, CAP, wide), lambda i: (0, 0, i)),
        out_shape=in_hbm((EP, CAP, HALF_D)),
        compiler_params=params(24),
        cost_estimate=cost(1.9e9, 7e6),
        name="down_rows",
    )(order, h0, h1, *weights)


def blend_kernel(routing_ref, weight_ref, rows_ref, out):
    column = lax.broadcasted_iota(I32, (1, EP * CAP), 1)
    experts, slot = column >> 3, column & 7
    routing, weight = routing_ref[...], weight_ref[...]
    marks = jnp.zeros((TRAJ, EP * CAP), F32)
    share = jnp.zeros((TRAJ, EP * CAP), F32)
    for k in range(8):
        hit = routing[:, k : k + 1] == experts
        marks = marks + hit.astype(F32)
        share = share + jnp.where(hit, weight[:, k : k + 1], 0.0)
    share = jnp.where(earlier(marks) == slot.astype(F32), share, 0.0)
    high = share.astype(BF16)
    low = (share - high.astype(F32)).astype(BF16)
    rows = rows_ref[...].reshape(EP * CAP, rows_ref.shape[2])
    out[...] = (
        jnp.dot(high, rows, preferred_element_type=F32)
        + jnp.dot(low, rows, preferred_element_type=F32)
    ).astype(BF16)


def blend(routing, weight, rows):
    wide = 896
    return pl.pallas_call(
        blend_kernel,
        grid=(HALF_D // wide,),
        in_specs=[
            whole((TRAJ, 8)),
            whole((TRAJ, 8)),
            pl.BlockSpec((EP, CAP, wide), lambda i: (0, 0, i)),
        ],
        out_specs=pl.BlockSpec((TRAJ, wide), lambda i: (0, i)),
        out_shape=jax.ShapeDtypeStruct((TRAJ, HALF_D), BF16),
        compiler_params=params(16),
        cost_estimate=cost(1e8, 2e6),
        name="blend",
    )(routing, weight, rows)


def collect_kernel(index_ref, pages, out):
    step = pl.program_id(0)
    lane = lax.broadcasted_iota(I32, (32, LANES - LATENT), 1)
    for i in range(8):
        j = step * 8 + i
        out[i, 0:16, 0:LATENT] = pages[index_ref[j, 0]]
        out[i, 16:32, 0:LATENT] = pages[index_ref[j, 1]]
        slot, length = index_ref[j, 2].astype(F32), index_ref[j, 3].astype(F32)
        out[i, :, LATENT:LANES] = jnp.where(lane == 0, slot, length).astype(BF16)


def collect(index, pages):
    return pl.pallas_call(
        collect_kernel,
        grid=(EP // 8,),
        in_specs=[smem(), whole(pages.shape)],
        out_specs=pl.BlockSpec((8, 32, LANES), lambda i: (i, 0, 0)),
        out_shape=in_hbm((EP, 32, LANES)),
        compiler_params=params(16),
        cost_estimate=cost(1e6, 6e6),
        name="collect",
    )(index, pages)


def regroup_kernel(midway, out):
    out[0] = midway[:, 0]


def regroup(midway):
    return pl.pallas_call(
        regroup_kernel,
        grid=(8,),
        in_specs=[pl.BlockSpec((8, 1, 32, LANES), lambda i: (0, i, 0, 0))],
        out_specs=pl.BlockSpec((1, 8, 32, LANES), lambda i: (i, 0, 0, 0)),
        out_shape=in_hbm((8, 8, 32, LANES)),
        compiler_params=params(8),
        cost_estimate=cost(1e6, 6e6),
        name="regroup",
    )(midway)


def compact_kernel(source_ref, arrived, out):
    step = pl.program_id(0)
    for i in range(8):
        out[i] = arrived[source_ref[step * 8 + i]]


def compact(source, arrived):
    return pl.pallas_call(
        compact_kernel,
        grid=(TRAJ // 8,),
        in_specs=[smem(), whole(arrived.shape)],
        out_specs=pl.BlockSpec((8, 32, LANES), lambda i: (i, 0, 0)),
        out_shape=in_hbm((TRAJ, 32, LANES)),
        compiler_params=params(16),
        cost_estimate=cost(1e6, 4e6),
        name="compact",
    )(source, arrived)


ATTEND_STEP = 8


def attend_kernel(tp_ref, length_ref, mine, other, queries, fresh, cache_out, out):
    step = pl.program_id(0)
    first = tp_ref[0] == 0
    row = lax.broadcasted_iota(I32, (MAXLEN, LATENT), 0).astype(F32).astype(BF16)
    column = lax.broadcasted_iota(I32, (TRAJ, MAXLEN), 1)
    scores = []
    for i in range(ATTEND_STEP):
        length = length_ref[step * ATTEND_STEP + i]
        edge = length.astype(F32).astype(BF16)
        a, b = mine[i, :, :LATENT], other[i, :, :LATENT]
        old = jnp.concatenate([jnp.where(first, a, b), jnp.where(first, b, a)], axis=0)
        new = jnp.broadcast_to(fresh[i], (MAXLEN, LATENT))
        zero = jnp.zeros((), BF16)
        cache = jnp.where(row < edge, old, jnp.where(row == edge, new, zero))
        cache_out[i] = cache
        score = lax.dot_general(
            queries[i], cache, (((1,), (1,)), ((), ())), preferred_element_type=F32
        )
        scores.append(jnp.where(column <= length, score * SCORE_SCALE, -jnp.inf))
    scores = jnp.concatenate(scores, axis=0)
    top = jnp.max(scores, axis=1, keepdims=True)
    weight = jnp.exp(scores - top)
    weight = (weight * (1.0 / jnp.sum(weight, axis=1, keepdims=True))).astype(BF16)
    for i in range(ATTEND_STEP):
        out[i] = jnp.dot(
            weight[i * TRAJ : (i + 1) * TRAJ],
            cache_out[i, :, :LATENT_WIDTH],
            preferred_element_type=F32,
        ).astype(BF16)


def attend(tp_index, length, mine, other, queries, fresh):
    n = ATTEND_STEP
    return pl.pallas_call(
        attend_kernel,
        grid=(TRAJ // n,),
        in_specs=[
            smem(),
            smem(),
            pl.BlockSpec((n, 32, LANES), lambda i: (i, 0, 0)),
            pl.BlockSpec((n, 32, LANES), lambda i: (i, 0, 0)),
            pl.BlockSpec((n, 32, LATENT), lambda i: (i, 0, 0)),
            pl.BlockSpec((n, 1, LATENT), lambda i: (i, 0, 0)),
        ],
        out_specs=[
            pl.BlockSpec((n, MAXLEN, LATENT), lambda i: (i, 0, 0)),
            pl.BlockSpec((n, 32, LATENT_WIDTH), lambda i: (i, 0, 0)),
        ],
        out_shape=[
            jax.ShapeDtypeStruct((TRAJ, MAXLEN, LATENT), BF16),
            jax.ShapeDtypeStruct((TRAJ, 32, LATENT_WIDTH), BF16),
        ],
        compiler_params=params(24),
        cost_estimate=cost(2e8, 8e6),
        name="attend",
    )(tp_index, length, mine, other, hbm(queries), fresh.reshape(TRAJ, 1, LATENT))


def swap(x, axis):
    return lax.ppermute(x, axis, [(0, 1), (1, 0)])


def z_shift(x, by):
    return lax.ppermute(x, "z", [(i, (i + by) % NZ) for i in range(NZ)])


def plane_shift(x, dx, dy):
    return lax.ppermute(
        x,
        ("xh", "y"),
        [
            (a * NY + b, ((a + dx) % NX) * NY + (b + dy) % NY)
            for a in range(NX)
            for b in range(NY)
        ],
    )


def on_device(
    latent_pages,
    page_table,
    lengths,
    new_place,
    queries,
    fresh_latent,
    hidden_states,
    routing,
    route_weight,
    gate_value,
    gate_scale,
    up_value,
    up_scale,
    down_value,
    down_scale,
):
    xh, z, y, tp = (lax.axis_index(name) for name in ("xh", "z", "y", "tp"))
    tp_index = tp.astype(I32).reshape(1)
    place = jnp.stack([xh, z, y]).astype(I32)

    own = jnp.concatenate(
        [hidden_states, jnp.pad(routing.astype(BF16), ((0, 0), (0, BLOCK - 8)))], axis=1
    )
    up_way, down_way = [own, z_shift(own, 1)], [own, z_shift(own, -1)]
    down_keep, down_send = scale_down(tp_index, down_value, down_scale)

    owner, slot = new_place // TRAJ, new_place % TRAJ
    to_owner = owner[None, :] == jnp.asarray(PLANE_MAJOR)[:, None]
    mine = lax.dynamic_slice_in_dim(page_table, tp * 2, 2, 1)
    facts = jnp.concatenate([mine, slot[:, None] + 1, lengths[:, None]], axis=1)
    index = jnp.sum(jnp.where(to_owner[:, :, None], facts[None], 0), axis=1)
    index = index - (jnp.arange(4) == 2).astype(I32)[None, :]
    leaving = collect(index, latent_pages).reshape(8, 8, 32, LANES)
    leaving, up_way[1], down_way[1], down_send = lax.optimization_barrier(
        (leaving, up_way[1], down_way[1], down_send)
    )
    down_tp = swap(down_send, "tp")
    midway = lax.all_to_all(leaving, ("xh", "y"), split_axis=0, concat_axis=0, tiled=True)

    gate, up = scale_wide(tp_index, gate_value, gate_scale, up_value, up_scale)
    gate_far, up_far = swap(gate, "pool"), swap(up, "pool")
    down_far = swap(down_keep, "pool")
    for step in range(1, 4):
        up_way.append(z_shift(up_way[-1], 1))
        if step < 3:
            down_way.append(z_shift(down_way[-1], -1))
    behind = np.array([0, 1, 2, 3, 4, -1, -2, -3], np.int32)

    place, gate_far, up_far, down_far = lax.optimization_barrier(
        (place, gate_far, up_far, down_far)
    )
    picked = pick_rows(place, up_way + down_way[1:])
    tokens = [picked[0]] + [
        plane_shift(picked[dx * NY + dy], dx, dy)
        for dx in range(NX)
        for dy in range(NY)
        if dx or dy
    ]

    midway, tokens[1], tokens[2], tokens[3] = lax.optimization_barrier(
        (midway, tokens[1], tokens[2], tokens[3])
    )
    arrived = lax.all_to_all(regroup(midway), "z", split_axis=0, concat_axis=0, tiled=True)
    down_tp_far = swap(down_tp, "pool")

    act = hidden_units(tokens, gate, gate_far, up, up_far)
    act_tp = swap(act, "tp")
    group = jnp.arange(EP, dtype=I32)
    order = (
        ((xh + (group >> 5)) % NX) * NZ + (z - jnp.tile(jnp.asarray(behind), 8)) % NZ
    ) * NY + (y - (group >> 3)) % NY
    out_rows = down_rows(order, act, act_tp, [down_keep, down_far, down_tp, down_tp_far])
    arrived, out_rows = lax.optimization_barrier((arrived, out_rows))
    returned = lax.all_to_all(
        out_rows, ("xh", "z", "y"), split_axis=0, concat_axis=0, tiled=True
    )
    expert_mix = blend(routing, route_weight, returned)

    arrived = arrived.reshape(EP, 32, LANES)
    labels = arrived[:, 0, LATENT : LATENT + 2].astype(I32)
    taken = labels[:, 0][None, :] == jnp.arange(TRAJ, dtype=I32)[:, None]
    source = jnp.sum(jnp.where(taken, jnp.arange(EP, dtype=I32)[None, :], 0), axis=1)
    length = jnp.sum(jnp.where(taken, labels[:, 1][None, :], 0), axis=1)
    my_half = compact(source, arrived)
    other_half = swap(my_half, "tp")
    new_cache, attention = attend(tp_index, length, my_half, other_half, queries, fresh_latent)
    return new_cache, attention, expert_mix


def solution(mesh):
    grid = Mesh(mesh.devices.reshape(2, NX, NZ, NY, 2), ("pool", "xh", "z", "y", "tp"))
    ep = ("xh", "z", "y")
    rows = ("pool",) + ep
    placed = (
        P(rows, None, None),
        P(rows, None),
        P(rows),
        P(rows),
        P(rows, "tp", None),
        P(rows, None),
        P(rows, None),
        P(rows, None),
        P(rows, None),
        P(ep, None, ("pool", "tp")),
        P(ep, None, ("pool", "tp")),
        P(ep, None, ("pool", "tp")),
        P(ep, None, ("pool", "tp")),
        P(ep, ("pool", "tp"), None),
        P(ep, ("pool", "tp"), None),
    )
    return jax.shard_map(
        on_device,
        mesh=grid,
        in_specs=placed,
        out_specs=(P(rows, None, None), P(rows, "tp", None), P(rows, "tp")),
        check_vma=False,
    )
```

```python
import jax
import jax.numpy as jnp
import numpy as np
from jax import lax
from jax.experimental import pallas as pl
from jax.experimental.pallas import tpu as pltpu
from jax.sharding import Mesh, PartitionSpec as P

F32, BF16, I32 = jnp.float32, jnp.bfloat16, jnp.int32
LATENT_WIDTH = 512
BLOCK = 128
MAXLEN = 64
LATENT = 576
LANES = 640
D = 3584
HALF_D = 1792
TRAJ = 32
CAP = 8
NZ, NY, NX = 8, 4, 2
EP = NZ * NY * NX
SCORE_SCALE = 192.0 ** (-0.5)
MB = 1024 * 1024

SMEM = pltpu.SMEM
PLANE_MAJOR = np.arange(EP, dtype=np.int32).reshape(NX, NZ, NY).transpose(0, 2, 1).reshape(-1)


def whole(shape):
    return pl.BlockSpec(shape, lambda *_: (0,) * len(shape))


def smem():
    return pl.BlockSpec(memory_space=SMEM)


def hbm(*arrays):
    kept = tuple(pltpu.with_memory_space_constraint(x, pltpu.HBM) for x in arrays)
    return kept if len(kept) > 1 else kept[0]


def in_hbm(shape):
    return jax.ShapeDtypeStruct(shape, BF16)


def params(mb):
    return pltpu.CompilerParams(vmem_limit_bytes=mb * MB)


def cost(flops, nbytes):
    return pl.CostEstimate(flops=int(flops), bytes_accessed=int(nbytes), transcendentals=0)


def wide_kernel(scale, value, *rest):
    out = rest[-1]
    first = pl.program_id(0) == 0
    for f in range(2):
        for k in range(14):
            rows, cols = slice(k * BLOCK, (k + 1) * BLOCK), slice(f * BLOCK, (f + 1) * BLOCK)
            by = jnp.where(first, scale[f : f + 1, k : k + 1], scale[f : f + 1, 14 + k : 15 + k])
            out[rows, cols] = (value[0, rows, cols].astype(F32) * by).astype(BF16)


def scale_wide(value, scale, *before):
    return pl.pallas_call(
        wide_kernel,
        grid=(2,),
        in_specs=[whole((2, 28)), pl.BlockSpec((1, D // 2, 256), lambda i: (0, i, 0))]
        + [smem()] * len(before),
        out_specs=pl.BlockSpec((D // 2, 256), lambda i: (i, 0)),
        out_shape=jax.ShapeDtypeStruct((D, 256), BF16),
        compiler_params=params(8),
        cost_estimate=cost(1e6, 4e6),
        name="scale_wide",
    )(scale[0].T.astype(F32), hbm(value), *before)


def narrow_kernel(half_ref, scale, value, *rest):
    out = rest[-1]
    first = half_ref[0] == 0
    for a in range(2):
        for k in range(14):
            rows, cols = slice(a * BLOCK, (a + 1) * BLOCK), slice(k * BLOCK, (k + 1) * BLOCK)
            by = jnp.where(first, scale[a : a + 1, k : k + 1], scale[a : a + 1, 14 + k : 15 + k])
            out[rows, cols] = (value[0, rows, cols].astype(F32) * by).astype(BF16)


def scale_down(half, value, scale, *before):
    return pl.pallas_call(
        narrow_kernel,
        grid_spec=pltpu.PrefetchScalarGridSpec(
            num_scalar_prefetch=1,
            grid=(1,),
            in_specs=[
                pl.BlockSpec((2, 28), lambda i, h: (0, 0)),
                pl.BlockSpec((1, 256, HALF_D), lambda i, h: (0, 0, h[0])),
            ]
            + [smem()] * len(before),
            out_specs=pl.BlockSpec((256, HALF_D), lambda i, h: (0, 0)),
        ),
        out_shape=jax.ShapeDtypeStruct((256, HALF_D), BF16),
        compiler_params=params(8),
        cost_estimate=cost(1e6, 2e6),
        name="scale_down",
    )(half, scale[0].astype(F32), hbm(value), *before)


def named_by(routing, experts):
    marks = jnp.zeros((routing.shape[0], experts.shape[1]), F32)
    for k in range(routing.shape[1]):
        marks = marks + (routing[:, k : k + 1] == experts).astype(F32)
    return marks


def earlier(marks):
    n = marks.shape[0]
    lower = (
        lax.broadcasted_iota(I32, (n, n), 0) > lax.broadcasted_iota(I32, (n, n), 1)
    ).astype(BF16)
    return jnp.dot(lower, marks.astype(BF16), preferred_element_type=F32)


def pick_kernel(place_ref, *refs):
    names, blocks, outs, chosen_ref = refs[:NZ], refs[NZ : 2 * NZ], refs[-9:-1], refs[-1]

    @pl.when(pl.program_id(0) == 0)
    def _():
        xh, z, y = place_ref[0], place_ref[1], place_ref[2]
        column = lax.broadcasted_iota(I32, (1, EP), 1)
        peer, slot = column >> 3, column & 7
        experts = (((peer >> 2) ^ xh) * NZ + z) * NY + (((peer & 3) + y) & 3)
        for b, name in enumerate(names):
            marks = named_by(name[...].astype(F32).astype(I32)[:, :8], experts)
            chosen_ref[b] = jnp.where(earlier(marks) == slot.astype(F32), marks, 0.0).astype(BF16)

    for b, block in enumerate(blocks):
        rows = lax.dot_general(
            chosen_ref[b],
            block[...],
            (((0,), (0,)), ((), ())),
            preferred_element_type=F32,
        ).astype(BF16)
        for r, out in enumerate(outs):
            out[b * CAP : (b + 1) * CAP, :] = rows[r * CAP : (r + 1) * CAP, :]


def pick_rows(place, blocks, *before):
    wide = 896
    return pl.pallas_call(
        pick_kernel,
        grid=(D // wide,),
        in_specs=[smem()]
        + [pl.BlockSpec((TRAJ, BLOCK), lambda i: (0, D // BLOCK))] * NZ
        + [pl.BlockSpec((TRAJ, wide), lambda i: (0, i))] * NZ
        + [smem()] * len(before),
        out_specs=[pl.BlockSpec((NZ * CAP, wide), lambda i: (0, i))] * 8,
        out_shape=[in_hbm((NZ * CAP, D))] * 8,
        scratch_shapes=[pltpu.VMEM((NZ, TRAJ, EP), BF16)],
        compiler_params=params(10),
        cost_estimate=cost(1e9, 6e6),
        name="pick_rows",
    )(place, *blocks, *blocks, *before)


def hidden_kernel(*refs):
    tokens, (g0, g1, u0, u1, out), (x,) = refs[:8], refs[8:13], refs[13:]
    for r, token in enumerate(tokens):
        x[r * 64 : (r + 1) * 64, :] = token[...]
    for half in range(2):
        rows = slice(half * 256, (half + 1) * 256)
        for n, (gate, up) in enumerate(((g0, u0), (g1, u1))):
            g = jnp.dot(x[rows, :], gate[...], preferred_element_type=F32)
            u = jnp.dot(x[rows, :], up[...], preferred_element_type=F32)
            out[rows, n * 256 : (n + 1) * 256] = (g / (1.0 + jnp.exp(-g)) * u).astype(BF16)


def hidden_units(tokens, g0, g1, u0, u1):
    vmem = pl.BlockSpec(memory_space=pltpu.VMEM)
    return pl.pallas_call(
        hidden_kernel,
        in_specs=[vmem] * 12,
        out_specs=vmem,
        out_shape=jax.ShapeDtypeStruct((512, 512), BF16),
        scratch_shapes=[pltpu.VMEM((512, D), BF16)],
        compiler_params=params(10),
        cost_estimate=cost(3.8e9, 12e6),
        name="hidden_units",
    )(*tokens, g0, g1, u0, u1)


def down_kernel(order_ref, h0, h1, w0, w1, w2, w3, out):
    h = jnp.concatenate([h0[...], h1[...]], axis=1)
    for c in range(HALF_D // 256):
        cols = slice(c * 256, (c + 1) * 256)
        w = jnp.concatenate([p[:, cols] for p in (w0, w1, w2, w3)], axis=0)
        rows = jnp.dot(h, w, preferred_element_type=F32)
        for group in range(EP):
            out[order_ref[group], :, cols] = rows[group * CAP : (group + 1) * CAP, :].astype(BF16)


def down_rows(order, h0, h1, weights):
    vmem = pl.BlockSpec(memory_space=pltpu.VMEM)
    return pl.pallas_call(
        down_kernel,
        in_specs=[smem()] + [vmem] * 6,
        out_specs=vmem,
        out_shape=jax.ShapeDtypeStruct((EP, CAP, HALF_D), BF16),
        compiler_params=params(10),
        cost_estimate=cost(1.9e9, 7e6),
        name="down_rows",
    )(order, h0, h1, *weights)


def blend_kernel(routing_ref, weight_ref, rows_ref, out):
    column = lax.broadcasted_iota(I32, (1, EP * CAP), 1)
    experts, slot = column >> 3, column & 7
    routing, weight = routing_ref[...], weight_ref[...]
    marks = jnp.zeros((TRAJ, EP * CAP), F32)
    share = jnp.zeros((TRAJ, EP * CAP), F32)
    for k in range(8):
        hit = routing[:, k : k + 1] == experts
        marks = marks + hit.astype(F32)
        share = share + jnp.where(hit, weight[:, k : k + 1], 0.0)
    share = jnp.where(earlier(marks) == slot.astype(F32), share, 0.0)
    high = share.astype(BF16)
    low = (share - high.astype(F32)).astype(BF16)
    rows = rows_ref[...].reshape(EP * CAP, rows_ref.shape[2])
    out[...] = (
        jnp.dot(high, rows, preferred_element_type=F32)
        + jnp.dot(low, rows, preferred_element_type=F32)
    ).astype(BF16)


def blend(routing, weight, rows):
    wide = 896
    return pl.pallas_call(
        blend_kernel,
        grid=(HALF_D // wide,),
        in_specs=[
            whole((TRAJ, 8)),
            whole((TRAJ, 8)),
            pl.BlockSpec((EP, CAP, wide), lambda i: (0, 0, i)),
        ],
        out_specs=pl.BlockSpec((TRAJ, wide), lambda i: (0, i)),
        out_shape=jax.ShapeDtypeStruct((TRAJ, HALF_D), BF16),
        compiler_params=params(10),
        cost_estimate=cost(1e8, 2e6),
        name="blend",
    )(routing, weight, rows)


def collect_kernel(index_ref, pages, *rest):
    out = rest[-1]
    step = pl.program_id(0)
    lane = lax.broadcasted_iota(I32, (32, LANES - LATENT), 1)
    for i in range(8):
        j = step * 8 + i
        out[i, 0:16, 0:LATENT] = pages[index_ref[j, 0]]
        out[i, 16:32, 0:LATENT] = pages[index_ref[j, 1]]
        slot, length = index_ref[j, 2].astype(F32), index_ref[j, 3].astype(F32)
        out[i, :, LATENT:LANES] = jnp.where(lane == 0, slot, length).astype(BF16)


def collect(index, pages, *before):
    return pl.pallas_call(
        collect_kernel,
        grid=(EP // 8,),
        in_specs=[smem(), whole(pages.shape)] + [smem()] * len(before),
        out_specs=pl.BlockSpec((8, 32, LANES), lambda i: (i, 0, 0)),
        out_shape=pltpu.HBM((EP, 32, LANES), BF16),
        compiler_params=params(10),
        cost_estimate=cost(1e6, 6e6),
        name="collect",
    )(index, pages, *before)


def regroup_kernel(midway, *rest):
    out = rest[-1]
    out[0] = midway[:, 0]


def regroup(midway, *before):
    return pl.pallas_call(
        regroup_kernel,
        grid=(8,),
        in_specs=[pl.BlockSpec((8, 1, 32, LANES), lambda i: (0, i, 0, 0))] + [smem()] * len(before),
        out_specs=pl.BlockSpec((1, 8, 32, LANES), lambda i: (i, 0, 0, 0)),
        out_shape=pltpu.HBM((8, 8, 32, LANES), BF16),
        compiler_params=params(8),
        cost_estimate=cost(1e6, 6e6),
        name="regroup",
    )(hbm(midway), *before)


def compact_kernel(source_ref, arrived, *rest):
    out = rest[-1]
    step = pl.program_id(0)
    for i in range(8):
        out[i] = arrived[source_ref[step * 8 + i]]


def compact(source, arrived, *before):
    return pl.pallas_call(
        compact_kernel,
        grid=(TRAJ // 8,),
        in_specs=[smem(), whole(arrived.shape)] + [smem()] * len(before),
        out_specs=pl.BlockSpec((8, 32, LANES), lambda i: (i, 0, 0)),
        out_shape=in_hbm((TRAJ, 32, LANES)),
        compiler_params=params(10),
        cost_estimate=cost(1e6, 4e6),
        name="compact",
    )(source, hbm(arrived), *before)


ATTEND_STEP = 8


def attend_kernel(tp_ref, length_ref, mine, other, queries, fresh, cache_out, out):
    step = pl.program_id(0)
    first = tp_ref[0] == 0
    row = lax.broadcasted_iota(I32, (MAXLEN, LATENT), 0).astype(F32).astype(BF16)
    column = lax.broadcasted_iota(I32, (TRAJ, MAXLEN), 1)
    scores = []
    for i in range(ATTEND_STEP):
        length = length_ref[step * ATTEND_STEP + i]
        edge = length.astype(F32).astype(BF16)
        a, b = mine[i, :, :LATENT], other[i, :, :LATENT]
        old = jnp.concatenate([jnp.where(first, a, b), jnp.where(first, b, a)], axis=0)
        new = jnp.broadcast_to(fresh[i], (MAXLEN, LATENT))
        zero = jnp.zeros((), BF16)
        cache = jnp.where(row < edge, old, jnp.where(row == edge, new, zero))
        cache_out[i] = cache
        score = lax.dot_general(
            queries[i], cache, (((1,), (1,)), ((), ())), preferred_element_type=F32
        )
        scores.append(jnp.where(column <= length, score * SCORE_SCALE, -jnp.inf))
    scores = jnp.concatenate(scores, axis=0)
    top = jnp.max(scores, axis=1, keepdims=True)
    weight = jnp.exp(scores - top)
    weight = (weight * (1.0 / jnp.sum(weight, axis=1, keepdims=True))).astype(BF16)
    for i in range(ATTEND_STEP):
        out[i] = jnp.dot(
            weight[i * TRAJ : (i + 1) * TRAJ],
            cache_out[i, :, :LATENT_WIDTH],
            preferred_element_type=F32,
        ).astype(BF16)


def attend(tp_index, length, mine, other, queries, fresh):
    n = ATTEND_STEP
    return pl.pallas_call(
        attend_kernel,
        grid=(TRAJ // n,),
        in_specs=[
            smem(),
            smem(),
            pl.BlockSpec((n, 32, LANES), lambda i: (i, 0, 0)),
            pl.BlockSpec((n, 32, LANES), lambda i: (i, 0, 0)),
            pl.BlockSpec((n, 32, LATENT), lambda i: (i, 0, 0)),
            pl.BlockSpec((n, 1, LATENT), lambda i: (i, 0, 0)),
        ],
        out_specs=[
            pl.BlockSpec((n, MAXLEN, LATENT), lambda i: (i, 0, 0)),
            pl.BlockSpec((n, 32, LATENT_WIDTH), lambda i: (i, 0, 0)),
        ],
        out_shape=[
            jax.ShapeDtypeStruct((TRAJ, MAXLEN, LATENT), BF16),
            jax.ShapeDtypeStruct((TRAJ, 32, LATENT_WIDTH), BF16),
        ],
        compiler_params=params(10),
        cost_estimate=cost(2e8, 8e6),
        name="attend",
    )(tp_index, length, mine, other, hbm(queries), fresh.reshape(TRAJ, 1, LATENT))


def once_kernel(*refs):
    refs[-1][0] = 0.0


def once(*arrays):
    return pl.pallas_call(
        once_kernel,
        in_specs=[pl.BlockSpec(memory_space=pl.ANY)] * len(arrays),
        out_specs=smem(),
        out_shape=jax.ShapeDtypeStruct((1,), F32),
        compiler_params=params(1),
        cost_estimate=cost(1, 4),
        name="once",
    )(*arrays)


def swap(x, axis):
    return lax.ppermute(x, axis, [(0, 1), (1, 0)])


def z_shift(x, by):
    return lax.ppermute(x, "z", [(i, (i + by) % NZ) for i in range(NZ)])


def plane_shift(x, dx, dy):
    return lax.ppermute(
        x,
        ("xh", "y"),
        [
            (a * NY + b, ((a + dx) % NX) * NY + (b + dy) % NY)
            for a in range(NX)
            for b in range(NY)
        ],
    )


def on_device(
    latent_pages,
    page_table,
    lengths,
    new_place,
    queries,
    fresh_latent,
    hidden_states,
    routing,
    route_weight,
    gate_value,
    gate_scale,
    up_value,
    up_scale,
    down_value,
    down_scale,
):
    xh, z, y, tp = (lax.axis_index(name) for name in ("xh", "z", "y", "tp"))
    tp_index = tp.astype(I32).reshape(1)
    place = jnp.stack([xh, z, y]).astype(I32)

    own = jnp.concatenate(
        [hidden_states, jnp.pad(routing.astype(BF16), ((0, 0), (0, BLOCK - 8)))], axis=1
    )
    up_way, down_way = [own, z_shift(own, 1)], [own, z_shift(own, -1)]
    down_send = scale_down(1 - tp_index, down_value, down_scale)
    down_tp = swap(down_send, "tp")

    owner, slot = new_place // TRAJ, new_place % TRAJ
    to_owner = owner[None, :] == jnp.asarray(PLANE_MAJOR)[:, None]
    mine = lax.dynamic_slice_in_dim(page_table, tp * 2, 2, 1)
    facts = jnp.concatenate([mine, slot[:, None] + 1, lengths[:, None]], axis=1)
    index = jnp.sum(jnp.where(to_owner[:, :, None], facts[None], 0), axis=1)
    index = index - (jnp.arange(4) == 2).astype(I32)[None, :]
    leaving = collect(index, latent_pages, once(up_way[1], down_way[1], down_send)).reshape(8, 8, 32, LANES)
    midway = lax.all_to_all(leaving, ("xh", "y"), split_axis=0, concat_axis=0, tiled=True)
    for step in range(1, 4):
        up_way.append(z_shift(up_way[-1], 1))
        if step < 3:
            down_way.append(z_shift(down_way[-1], -1))
    behind = np.array([0, 1, 2, 3, 4, -1, -2, -3], np.int32)

    gate = scale_wide(gate_value, gate_scale, once(up_way[1], down_way[1]))
    up = scale_wide(up_value, up_scale, once(up_way[2], down_way[2]))
    down_keep = scale_down(tp_index, down_value, down_scale, once(up_way[2], down_way[2]))
    gate_far, up_far = swap(gate, "pool"), swap(up, "pool")
    down_far, down_tp_far = swap(down_keep, "pool"), swap(down_tp, "pool")

    midway = regroup(
        midway, once(up_way[4], down_way[3], gate_far, up_far, down_far, down_tp)
    )
    picked = pick_rows(
        place, up_way + down_way[1:], once(down_tp_far)
    )
    tokens = [picked[0]] + [
        plane_shift(picked[dx * NY + dy], dx, dy)
        for dx in range(NX)
        for dy in range(NY)
        if dx or dy
    ]

    arrived = lax.all_to_all(midway, "z", split_axis=0, concat_axis=0, tiled=True)

    act = hidden_units(tokens, gate, gate_far, up, up_far)
    act_tp = swap(act, "tp")
    group = jnp.arange(EP, dtype=I32)
    order = (
        ((xh + (group >> 5)) % NX) * NZ + (z - jnp.tile(jnp.asarray(behind), 8)) % NZ
    ) * NY + (y - (group >> 3)) % NY
    out_rows = down_rows(order, act, act_tp, [down_keep, down_far, down_tp, down_tp_far])
    returned = lax.all_to_all(
        out_rows, ("xh", "z", "y"), split_axis=0, concat_axis=0, tiled=True
    )
    expert_mix = blend(routing, route_weight, returned)

    arrived = arrived.reshape(EP, 32, LANES)
    labels = arrived[:, 0, LATENT : LATENT + 2].astype(I32)
    taken = labels[:, 0][None, :] == jnp.arange(TRAJ, dtype=I32)[:, None]
    source = jnp.sum(jnp.where(taken, jnp.arange(EP, dtype=I32)[None, :], 0), axis=1)
    length = jnp.sum(jnp.where(taken, labels[:, 1][None, :], 0), axis=1)
    my_half = compact(source, arrived, once(out_rows))
    other_half = swap(my_half, "tp")
    new_cache, attention = attend(tp_index, length, my_half, other_half, queries, fresh_latent)
    return new_cache, attention, expert_mix


def solution(mesh):
    grid = Mesh(mesh.devices.reshape(2, NX, NZ, NY, 2), ("pool", "xh", "z", "y", "tp"))
    ep = ("xh", "z", "y")
    rows = ("pool",) + ep
    placed = (
        P(rows, None, None),
        P(rows, None),
        P(rows),
        P(rows),
        P(rows, "tp", None),
        P(rows, None),
        P(rows, None),
        P(rows, None),
        P(rows, None),
        P(ep, None, ("pool", "tp")),
        P(ep, None, ("pool", "tp")),
        P(ep, None, ("pool", "tp")),
        P(ep, None, ("pool", "tp")),
        P(ep, ("pool", "tp"), None),
        P(ep, ("pool", "tp"), None),
    )
    return jax.shard_map(
        on_device,
        mesh=grid,
        in_specs=placed,
        out_specs=(P(rows, None, None), P(rows, "tp", None), P(rows, "tp")),
        check_vma=False,
    )
```

```python
import jax
import jax.numpy as jnp
import numpy as np
from jax import lax
from jax.experimental import pallas as pl
from jax.experimental.pallas import tpu as pltpu
from jax.sharding import Mesh, PartitionSpec as P

F32, BF16, I32 = jnp.float32, jnp.bfloat16, jnp.int32
LATENT_WIDTH = 512
BLOCK = 128
MAXLEN = 64
LATENT = 576
LANES = 640
D = 3584
HALF_D = 1792
TRAJ = 32
CAP = 8
NZ, NY, NX = 8, 4, 2
EP = NZ * NY * NX
SCORE_SCALE = 192.0 ** (-0.5)
MB = 1024 * 1024

SMEM = pltpu.SMEM
PLANE_MAJOR = np.arange(EP, dtype=np.int32).reshape(NX, NZ, NY).transpose(0, 2, 1).reshape(-1)


def whole(shape):
    return pl.BlockSpec(shape, lambda *_: (0,) * len(shape))


def smem():
    return pl.BlockSpec(memory_space=SMEM)


def hbm(*arrays):
    kept = tuple(pltpu.with_memory_space_constraint(x, pltpu.HBM) for x in arrays)
    return kept if len(kept) > 1 else kept[0]


def in_hbm(shape):
    return jax.ShapeDtypeStruct(shape, BF16)


def params(mb):
    return pltpu.CompilerParams(vmem_limit_bytes=mb * MB)


def cost(flops, nbytes):
    return pl.CostEstimate(flops=int(flops), bytes_accessed=int(nbytes), transcendentals=0)


def wide_kernel(scale, value, *rest):
    out = rest[-1]
    first = pl.program_id(0) == 0
    for f in range(2):
        for k in range(14):
            rows, cols = slice(k * BLOCK, (k + 1) * BLOCK), slice(f * BLOCK, (f + 1) * BLOCK)
            by = jnp.where(first, scale[f : f + 1, k : k + 1], scale[f : f + 1, 14 + k : 15 + k])
            out[rows, cols] = (value[0, rows, cols].astype(F32) * by).astype(BF16)


def scale_wide(value, scale, *before):
    return pl.pallas_call(
        wide_kernel,
        grid=(2,),
        in_specs=[whole((2, 28)), pl.BlockSpec((1, D // 2, 256), lambda i: (0, i, 0))]
        + [smem()] * len(before),
        out_specs=pl.BlockSpec((D // 2, 256), lambda i: (i, 0)),
        out_shape=jax.ShapeDtypeStruct((D, 256), BF16),
        compiler_params=params(8),
        cost_estimate=cost(1e6, 4e6),
        name="scale_wide",
    )(scale[0].T.astype(F32), hbm(value), *before)


def narrow_kernel(half_ref, scale, value, *rest):
    out = rest[-1]
    first = half_ref[0] == 0
    for a in range(2):
        for k in range(14):
            rows, cols = slice(a * BLOCK, (a + 1) * BLOCK), slice(k * BLOCK, (k + 1) * BLOCK)
            by = jnp.where(first, scale[a : a + 1, k : k + 1], scale[a : a + 1, 14 + k : 15 + k])
            out[rows, cols] = (value[0, rows, cols].astype(F32) * by).astype(BF16)


def scale_down(half, value, scale, *before):
    return pl.pallas_call(
        narrow_kernel,
        grid_spec=pltpu.PrefetchScalarGridSpec(
            num_scalar_prefetch=1,
            grid=(1,),
            in_specs=[
                pl.BlockSpec((2, 28), lambda i, h: (0, 0)),
                pl.BlockSpec((1, 256, HALF_D), lambda i, h: (0, 0, h[0])),
            ]
            + [smem()] * len(before),
            out_specs=pl.BlockSpec((256, HALF_D), lambda i, h: (0, 0)),
        ),
        out_shape=jax.ShapeDtypeStruct((256, HALF_D), BF16),
        compiler_params=params(8),
        cost_estimate=cost(1e6, 2e6),
        name="scale_down",
    )(half, scale[0].astype(F32), hbm(value), *before)


def named_by(routing, experts):
    marks = jnp.zeros((routing.shape[0], experts.shape[1]), F32)
    for k in range(routing.shape[1]):
        marks = marks + (routing[:, k : k + 1] == experts).astype(F32)
    return marks


def earlier(marks):
    n = marks.shape[0]
    lower = (
        lax.broadcasted_iota(I32, (n, n), 0) > lax.broadcasted_iota(I32, (n, n), 1)
    ).astype(BF16)
    return jnp.dot(lower, marks.astype(BF16), preferred_element_type=F32)


def pick_kernel(place_ref, *refs):
    names, blocks, outs, chosen_ref = refs[:NZ], refs[NZ : 2 * NZ], refs[-9:-1], refs[-1]

    @pl.when(pl.program_id(0) == 0)
    def _():
        xh, z, y = place_ref[0], place_ref[1], place_ref[2]
        column = lax.broadcasted_iota(I32, (1, EP), 1)
        peer, slot = column >> 3, column & 7
        experts = (((peer >> 2) ^ xh) * NZ + z) * NY + (((peer & 3) + y) & 3)
        for b, name in enumerate(names):
            marks = named_by(name[...].astype(F32).astype(I32)[:, :8], experts)
            chosen_ref[b] = jnp.where(earlier(marks) == slot.astype(F32), marks, 0.0).astype(BF16)

    for b, block in enumerate(blocks):
        rows = lax.dot_general(
            chosen_ref[b],
            block[...],
            (((0,), (0,)), ((), ())),
            preferred_element_type=F32,
        ).astype(BF16)
        for r, out in enumerate(outs):
            out[b * CAP : (b + 1) * CAP, :] = rows[r * CAP : (r + 1) * CAP, :]


def pick_rows(place, blocks, *before):
    wide = 896
    return pl.pallas_call(
        pick_kernel,
        grid=(D // wide,),
        in_specs=[smem()]
        + [pl.BlockSpec((TRAJ, BLOCK), lambda i: (0, D // BLOCK))] * NZ
        + [pl.BlockSpec((TRAJ, wide), lambda i: (0, i))] * NZ
        + [smem()] * len(before),
        out_specs=[pl.BlockSpec((NZ * CAP, wide), lambda i: (0, i))] * 8,
        out_shape=[in_hbm((NZ * CAP, D))] * 8,
        scratch_shapes=[pltpu.VMEM((NZ, TRAJ, EP), BF16)],
        compiler_params=params(10),
        cost_estimate=cost(1e9, 6e6),
        name="pick_rows",
    )(place, *blocks, *blocks, *before)


PEER_ORDER = (4, 1, 5, 2, 6, 3, 7, 0)


def hidden_kernel(*refs):
    tokens, (gate, up, out, x) = refs[:8], refs[8:]
    for r, token in zip(PEER_ORDER, tokens):
        x[r * 64 : (r + 1) * 64, :] = token[...]
    for half in range(2):
        rows = slice(half * 256, (half + 1) * 256)
        g = jnp.dot(x[rows, :], gate[...], preferred_element_type=F32)
        u = jnp.dot(x[rows, :], up[...], preferred_element_type=F32)
        out[rows, :] = (g / (1.0 + jnp.exp(-g)) * u).astype(BF16)


def hidden_units(tokens, gate, up):
    vmem = pl.BlockSpec(memory_space=pltpu.VMEM)
    return pl.pallas_call(
        hidden_kernel,
        in_specs=[vmem] * 10,
        out_specs=vmem,
        out_shape=jax.ShapeDtypeStruct((512, 256), BF16),
        scratch_shapes=[pltpu.VMEM((512, D), BF16)],
        compiler_params=params(10),
        cost_estimate=cost(1.9e9, 8e6),
        name="hidden_units",
    )(*[tokens[r] for r in PEER_ORDER], gate, up)


def down_kernel(order_ref, h0, h1, h2, h3, w0, w1, w2, w3, out):
    h = jnp.concatenate([part[...] for part in (h0, h1, h2, h3)], axis=1)
    for c in range(HALF_D // 256):
        cols = slice(c * 256, (c + 1) * 256)
        w = jnp.concatenate([p[:, cols] for p in (w0, w1, w2, w3)], axis=0)
        rows = jnp.dot(h, w, preferred_element_type=F32)
        for group in range(EP):
            out[order_ref[group], :, cols] = rows[group * CAP : (group + 1) * CAP, :].astype(BF16)


def down_rows(order, parts, weights):
    vmem = pl.BlockSpec(memory_space=pltpu.VMEM)
    return pl.pallas_call(
        down_kernel,
        in_specs=[smem()] + [vmem] * 8,
        out_specs=vmem,
        out_shape=jax.ShapeDtypeStruct((EP, CAP, HALF_D), BF16),
        compiler_params=params(10),
        cost_estimate=cost(1.9e9, 7e6),
        name="down_rows",
    )(order, *parts, *weights)


def blend_kernel(routing_ref, weight_ref, rows_ref, out):
    column = lax.broadcasted_iota(I32, (1, EP * CAP), 1)
    experts, slot = column >> 3, column & 7
    routing, weight = routing_ref[...], weight_ref[...]
    marks = jnp.zeros((TRAJ, EP * CAP), F32)
    share = jnp.zeros((TRAJ, EP * CAP), F32)
    for k in range(8):
        hit = routing[:, k : k + 1] == experts
        marks = marks + hit.astype(F32)
        share = share + jnp.where(hit, weight[:, k : k + 1], 0.0)
    share = jnp.where(earlier(marks) == slot.astype(F32), share, 0.0)
    high = share.astype(BF16)
    low = (share - high.astype(F32)).astype(BF16)
    rows = rows_ref[...].reshape(EP * CAP, rows_ref.shape[2])
    out[...] = (
        jnp.dot(high, rows, preferred_element_type=F32)
        + jnp.dot(low, rows, preferred_element_type=F32)
    ).astype(BF16)


def blend(routing, weight, rows):
    wide = 896
    return pl.pallas_call(
        blend_kernel,
        grid=(HALF_D // wide,),
        in_specs=[
            whole((TRAJ, 8)),
            whole((TRAJ, 8)),
            pl.BlockSpec((EP, CAP, wide), lambda i: (0, 0, i)),
        ],
        out_specs=pl.BlockSpec((TRAJ, wide), lambda i: (0, i)),
        out_shape=jax.ShapeDtypeStruct((TRAJ, HALF_D), BF16),
        compiler_params=params(10),
        cost_estimate=cost(1e8, 2e6),
        name="blend",
    )(routing, weight, rows)


def collect_kernel(index_ref, pages, *rest):
    out = rest[-1]
    step = pl.program_id(0)
    lane = lax.broadcasted_iota(I32, (32, LANES - LATENT), 1)
    for i in range(8):
        j = step * 8 + i
        out[i, 0:16, 0:LATENT] = pages[index_ref[j, 0]]
        out[i, 16:32, 0:LATENT] = pages[index_ref[j, 1]]
        slot, length = index_ref[j, 2].astype(F32), index_ref[j, 3].astype(F32)
        out[i, :, LATENT:LANES] = jnp.where(lane == 0, slot, length).astype(BF16)


def collect(index, pages, *before):
    return pl.pallas_call(
        collect_kernel,
        grid=(EP // 8,),
        in_specs=[smem(), whole(pages.shape)] + [smem()] * len(before),
        out_specs=pl.BlockSpec((8, 32, LANES), lambda i: (i, 0, 0)),
        out_shape=pltpu.HBM((EP, 32, LANES), BF16),
        compiler_params=params(10),
        cost_estimate=cost(1e6, 6e6),
        name="collect",
    )(index, pages, *before)


def regroup_kernel(midway, *rest):
    out = rest[-1]
    out[0] = midway[:, 0]


def regroup(midway, *before):
    return pl.pallas_call(
        regroup_kernel,
        grid=(8,),
        in_specs=[pl.BlockSpec((8, 1, 32, LANES), lambda i: (0, i, 0, 0))] + [smem()] * len(before),
        out_specs=pl.BlockSpec((1, 8, 32, LANES), lambda i: (i, 0, 0, 0)),
        out_shape=pltpu.HBM((8, 8, 32, LANES), BF16),
        compiler_params=params(8),
        cost_estimate=cost(1e6, 6e6),
        name="regroup",
    )(hbm(midway), *before)


def compact_kernel(source_ref, arrived, *rest):
    out = rest[-1]
    step = pl.program_id(0)
    for i in range(8):
        out[i] = arrived[source_ref[step * 8 + i]]


def compact(source, arrived, *before):
    return pl.pallas_call(
        compact_kernel,
        grid=(TRAJ // 8,),
        in_specs=[smem(), whole(arrived.shape)] + [smem()] * len(before),
        out_specs=pl.BlockSpec((8, 32, LANES), lambda i: (i, 0, 0)),
        out_shape=in_hbm((TRAJ, 32, LANES)),
        compiler_params=params(10),
        cost_estimate=cost(1e6, 4e6),
        name="compact",
    )(source, hbm(arrived), *before)


ATTEND_STEP = 8


def attend_kernel(tp_ref, length_ref, mine, other, queries, fresh, cache_out, out):
    step = pl.program_id(0)
    first = tp_ref[0] == 0
    row = lax.broadcasted_iota(I32, (MAXLEN, LATENT), 0).astype(F32).astype(BF16)
    column = lax.broadcasted_iota(I32, (TRAJ, MAXLEN), 1)
    scores = []
    for i in range(ATTEND_STEP):
        length = length_ref[step * ATTEND_STEP + i]
        edge = length.astype(F32).astype(BF16)
        a, b = mine[i, :, :LATENT], other[i, :, :LATENT]
        old = jnp.concatenate([jnp.where(first, a, b), jnp.where(first, b, a)], axis=0)
        new = jnp.broadcast_to(fresh[i], (MAXLEN, LATENT))
        zero = jnp.zeros((), BF16)
        cache = jnp.where(row < edge, old, jnp.where(row == edge, new, zero))
        cache_out[i] = cache
        score = lax.dot_general(
            queries[i], cache, (((1,), (1,)), ((), ())), preferred_element_type=F32
        )
        scores.append(jnp.where(column <= length, score * SCORE_SCALE, -jnp.inf))
    scores = jnp.concatenate(scores, axis=0)
    top = jnp.max(scores, axis=1, keepdims=True)
    weight = jnp.exp(scores - top)
    weight = (weight * (1.0 / jnp.sum(weight, axis=1, keepdims=True))).astype(BF16)
    for i in range(ATTEND_STEP):
        out[i] = jnp.dot(
            weight[i * TRAJ : (i + 1) * TRAJ],
            cache_out[i, :, :LATENT_WIDTH],
            preferred_element_type=F32,
        ).astype(BF16)


def attend(tp_index, length, mine, other, queries, fresh):
    n = ATTEND_STEP
    return pl.pallas_call(
        attend_kernel,
        grid=(TRAJ // n,),
        in_specs=[
            smem(),
            smem(),
            pl.BlockSpec((n, 32, LANES), lambda i: (i, 0, 0)),
            pl.BlockSpec((n, 32, LANES), lambda i: (i, 0, 0)),
            pl.BlockSpec((n, 32, LATENT), lambda i: (i, 0, 0)),
            pl.BlockSpec((n, 1, LATENT), lambda i: (i, 0, 0)),
        ],
        out_specs=[
            pl.BlockSpec((n, MAXLEN, LATENT), lambda i: (i, 0, 0)),
            pl.BlockSpec((n, 32, LATENT_WIDTH), lambda i: (i, 0, 0)),
        ],
        out_shape=[
            jax.ShapeDtypeStruct((TRAJ, MAXLEN, LATENT), BF16),
            jax.ShapeDtypeStruct((TRAJ, 32, LATENT_WIDTH), BF16),
        ],
        compiler_params=params(10),
        cost_estimate=cost(2e8, 8e6),
        name="attend",
    )(tp_index, length, mine, other, hbm(queries), fresh.reshape(TRAJ, 1, LATENT))


def once_kernel(*refs):
    refs[-1][0] = 0.0


def once(*arrays):
    return pl.pallas_call(
        once_kernel,
        in_specs=[pl.BlockSpec(memory_space=pl.ANY)] * len(arrays),
        out_specs=smem(),
        out_shape=jax.ShapeDtypeStruct((1,), F32),
        compiler_params=params(1),
        cost_estimate=cost(1, 4),
        name="once",
    )(*arrays)


def swap(x, axis):
    return lax.ppermute(x, axis, [(0, 1), (1, 0)])


def z_shift(x, by):
    return lax.ppermute(x, "z", [(i, (i + by) % NZ) for i in range(NZ)])


def plane_shift(x, dx, dy):
    return lax.ppermute(
        x,
        ("xh", "y"),
        [
            (a * NY + b, ((a + dx) % NX) * NY + (b + dy) % NY)
            for a in range(NX)
            for b in range(NY)
        ],
    )


def on_device(
    latent_pages,
    page_table,
    lengths,
    new_place,
    queries,
    fresh_latent,
    hidden_states,
    routing,
    route_weight,
    gate_value,
    gate_scale,
    up_value,
    up_scale,
    down_value,
    down_scale,
):
    xh, z, y, tp = (lax.axis_index(name) for name in ("xh", "z", "y", "tp"))
    tp_index = tp.astype(I32).reshape(1)
    place = jnp.stack([xh, z, y]).astype(I32)

    own = jnp.concatenate(
        [hidden_states, jnp.pad(routing.astype(BF16), ((0, 0), (0, BLOCK - 8)))], axis=1
    )
    up_way, down_way = [own, z_shift(own, 1)], [own, z_shift(own, -1)]
    down_send = scale_down(1 - tp_index, down_value, down_scale)
    down_tp = swap(down_send, "tp")

    owner, slot = new_place // TRAJ, new_place % TRAJ
    to_owner = owner[None, :] == jnp.asarray(PLANE_MAJOR)[:, None]
    mine = lax.dynamic_slice_in_dim(page_table, tp * 2, 2, 1)
    facts = jnp.concatenate([mine, slot[:, None] + 1, lengths[:, None]], axis=1)
    index = jnp.sum(jnp.where(to_owner[:, :, None], facts[None], 0), axis=1)
    index = index - (jnp.arange(4) == 2).astype(I32)[None, :]
    leaving = collect(index, latent_pages, once(up_way[1], down_way[1])).reshape(8, 8, 32, LANES)
    midway = lax.all_to_all(leaving, ("xh", "y"), split_axis=0, concat_axis=0, tiled=True)
    for step in range(1, 4):
        up_way.append(z_shift(up_way[-1], 1))
        if step < 3:
            down_way.append(z_shift(down_way[-1], -1))
    behind = np.array([0, 1, 2, 3, 4, -1, -2, -3], np.int32)

    gate = scale_wide(gate_value, gate_scale, once(up_way[1], down_way[1]))
    up = scale_wide(up_value, up_scale, once(up_way[2], down_way[2], down_tp))
    down_keep = scale_down(tp_index, down_value, down_scale, once(up_way[2], down_way[2]))
    gate_far, up_far = swap(gate, "pool"), swap(up, "pool")
    down_far, down_tp_far = swap(down_keep, "pool"), swap(down_tp, "pool")

    midway = regroup(
        midway, once(up_way[4], down_way[3], gate_far, up_far, down_far)
    )
    picked = pick_rows(
        place, up_way + down_way[1:], once(down_tp_far)
    )
    tokens = list(picked)
    for peer in PEER_ORDER[:7]:
        tokens[peer] = plane_shift(picked[peer], peer // NY, peer % NY)

    arrived = lax.all_to_all(midway, "z", split_axis=0, concat_axis=0, tiled=True)

    act, act_far = hidden_units(tokens, gate, up), hidden_units(tokens, gate_far, up_far)
    act_tp, act_tp_far = swap(act, "tp"), swap(act_far, "tp")
    group = jnp.arange(EP, dtype=I32)
    order = (
        ((xh + (group >> 5)) % NX) * NZ + (z - jnp.tile(jnp.asarray(behind), 8)) % NZ
    ) * NY + (y - (group >> 3)) % NY
    out_rows = down_rows(
        order,
        [act, act_far, act_tp, act_tp_far],
        [down_keep, down_far, down_tp, down_tp_far],
    )
    returned = lax.all_to_all(
        out_rows, ("xh", "z", "y"), split_axis=0, concat_axis=0, tiled=True
    )
    expert_mix = blend(routing, route_weight, returned)

    arrived = arrived.reshape(EP, 32, LANES)
    labels = arrived[:, 0, LATENT : LATENT + 2].astype(I32)
    taken = labels[:, 0][None, :] == jnp.arange(TRAJ, dtype=I32)[:, None]
    source = jnp.sum(jnp.where(taken, jnp.arange(EP, dtype=I32)[None, :], 0), axis=1)
    length = jnp.sum(jnp.where(taken, labels[:, 1][None, :], 0), axis=1)
    my_half = compact(source, arrived, once(out_rows))
    other_half = swap(my_half, "tp")
    new_cache, attention = attend(tp_index, length, my_half, other_half, queries, fresh_latent)
    return new_cache, attention, expert_mix


def solution(mesh):
    grid = Mesh(mesh.devices.reshape(2, NX, NZ, NY, 2), ("pool", "xh", "z", "y", "tp"))
    ep = ("xh", "z", "y")
    rows = ("pool",) + ep
    placed = (
        P(rows, None, None),
        P(rows, None),
        P(rows),
        P(rows),
        P(rows, "tp", None),
        P(rows, None),
        P(rows, None),
        P(rows, None),
        P(rows, None),
        P(ep, None, ("pool", "tp")),
        P(ep, None, ("pool", "tp")),
        P(ep, None, ("pool", "tp")),
        P(ep, None, ("pool", "tp")),
        P(ep, ("pool", "tp"), None),
        P(ep, ("pool", "tp"), None),
    )
    return jax.shard_map(
        on_device,
        mesh=grid,
        in_specs=placed,
        out_specs=(P(rows, None, None), P(rows, "tp", None), P(rows, "tp")),
        check_vma=False,
    )
```

```python
import jax
import jax.numpy as jnp
import numpy as np
from jax import lax
from jax.experimental import pallas as pl
from jax.experimental.pallas import tpu as pltpu
from jax.sharding import Mesh, PartitionSpec as P

F32, BF16, I32 = jnp.float32, jnp.bfloat16, jnp.int32
LATENT_WIDTH = 512
BLOCK = 128
MAXLEN = 64
LATENT = 576
LANES = 640
D = 3584
HALF_D = 1792
TRAJ = 32
CAP = 8
NZ, NY, NX = 8, 4, 2
EP = NZ * NY * NX
SCORE_SCALE = 192.0 ** (-0.5)
MB = 1024 * 1024

SMEM = pltpu.SMEM
PLANE_MAJOR = np.arange(EP, dtype=np.int32).reshape(NX, NZ, NY).transpose(0, 2, 1).reshape(-1)


def whole(shape):
    return pl.BlockSpec(shape, lambda *_: (0,) * len(shape))


def smem():
    return pl.BlockSpec(memory_space=SMEM)


def hbm(*arrays):
    kept = tuple(pltpu.with_memory_space_constraint(x, pltpu.HBM) for x in arrays)
    return kept if len(kept) > 1 else kept[0]


def in_hbm(shape):
    return jax.ShapeDtypeStruct(shape, BF16)


def params(mb):
    return pltpu.CompilerParams(vmem_limit_bytes=mb * MB)


def cost(flops, nbytes):
    return pl.CostEstimate(flops=int(flops), bytes_accessed=int(nbytes), transcendentals=0)


def wide_kernel(scale, value, *rest):
    out = rest[-1]
    first = pl.program_id(0) == 0
    for f in range(2):
        for k in range(14):
            rows, cols = slice(k * BLOCK, (k + 1) * BLOCK), slice(f * BLOCK, (f + 1) * BLOCK)
            by = jnp.where(first, scale[f : f + 1, k : k + 1], scale[f : f + 1, 14 + k : 15 + k])
            out[rows, cols] = (value[0, rows, cols].astype(F32) * by).astype(BF16)


def scale_wide(value, scale, *before):
    return pl.pallas_call(
        wide_kernel,
        grid=(2,),
        in_specs=[whole((2, 28)), pl.BlockSpec((1, D // 2, 256), lambda i: (0, i, 0))]
        + [smem()] * len(before),
        out_specs=pl.BlockSpec((D // 2, 256), lambda i: (i, 0)),
        out_shape=jax.ShapeDtypeStruct((D, 256), BF16),
        compiler_params=params(8),
        cost_estimate=cost(1e6, 4e6),
        name="scale_wide",
    )(scale[0].T.astype(F32), hbm(value), *before)


def narrow_kernel(half_ref, scale, value, *rest):
    out = rest[-1]
    first = half_ref[0] == 0
    for a in range(2):
        for k in range(14):
            rows, cols = slice(a * BLOCK, (a + 1) * BLOCK), slice(k * BLOCK, (k + 1) * BLOCK)
            by = jnp.where(first, scale[a : a + 1, k : k + 1], scale[a : a + 1, 14 + k : 15 + k])
            out[rows, cols] = (value[0, rows, cols].astype(F32) * by).astype(BF16)


def scale_down(half, value, scale, *before):
    return pl.pallas_call(
        narrow_kernel,
        grid_spec=pltpu.PrefetchScalarGridSpec(
            num_scalar_prefetch=1,
            grid=(1,),
            in_specs=[
                pl.BlockSpec((2, 28), lambda i, h: (0, 0)),
                pl.BlockSpec((1, 256, HALF_D), lambda i, h: (0, 0, h[0])),
            ]
            + [smem()] * len(before),
            out_specs=pl.BlockSpec((256, HALF_D), lambda i, h: (0, 0)),
        ),
        out_shape=jax.ShapeDtypeStruct((256, HALF_D), BF16),
        compiler_params=params(8),
        cost_estimate=cost(1e6, 2e6),
        name="scale_down",
    )(half, scale[0].astype(F32), hbm(value), *before)


def named_by(routing, experts):
    marks = jnp.zeros((routing.shape[0], experts.shape[1]), F32)
    for k in range(routing.shape[1]):
        marks = marks + (routing[:, k : k + 1] == experts).astype(F32)
    return marks


def earlier(marks):
    n = marks.shape[0]
    lower = (
        lax.broadcasted_iota(I32, (n, n), 0) > lax.broadcasted_iota(I32, (n, n), 1)
    ).astype(BF16)
    return jnp.dot(lower, marks.astype(BF16), preferred_element_type=F32)


def pick_kernel(place_ref, *refs):
    blocks, outs = refs[:NZ], refs[NZ:]
    xh, z, y = place_ref[0], place_ref[1], place_ref[2]
    column = lax.broadcasted_iota(I32, (1, EP), 1)
    peer, slot = column >> 3, column & 7
    experts = (((peer >> 2) ^ xh) * NZ + z) * NY + (((peer & 3) + y) & 3)
    for b, block in enumerate(blocks):
        marks = named_by(block[:, D : D + 8].astype(F32).astype(I32), experts)
        chosen = jnp.where(earlier(marks) == slot.astype(F32), marks, 0.0).astype(BF16)
        rows = lax.dot_general(
            chosen, block[:, :D], (((0,), (0,)), ((), ())), preferred_element_type=F32
        ).astype(BF16)
        for r, out in enumerate(outs):
            out[b * CAP : (b + 1) * CAP, :] = rows[r * CAP : (r + 1) * CAP, :]


def pick_rows(place, blocks):
    vmem = pl.BlockSpec(memory_space=pltpu.VMEM)
    return pl.pallas_call(
        pick_kernel,
        in_specs=[smem()] + [vmem] * NZ,
        out_specs=[vmem] * 8,
        out_shape=[jax.ShapeDtypeStruct((NZ * CAP, D), BF16)] * 8,
        compiler_params=params(6),
        cost_estimate=cost(1e9, 6e6),
        name="pick_rows",
    )(place, *blocks)


PEER_ORDER = (4, 1, 5, 2, 6, 3, 7, 0)


def hidden_kernel(*refs):
    tokens, (gate, up, out, x) = refs[:8], refs[8:]
    for r, token in zip(PEER_ORDER, tokens):
        x[r * 64 : (r + 1) * 64, :] = token[...]
    for half in range(2):
        rows = slice(half * 256, (half + 1) * 256)
        g = jnp.dot(x[rows, :], gate[...], preferred_element_type=F32)
        u = jnp.dot(x[rows, :], up[...], preferred_element_type=F32)
        out[rows, :] = (g / (1.0 + jnp.exp(-g)) * u).astype(BF16)


def hidden_units(tokens, gate, up):
    vmem = pl.BlockSpec(memory_space=pltpu.VMEM)
    return pl.pallas_call(
        hidden_kernel,
        in_specs=[vmem] * 10,
        out_specs=vmem,
        out_shape=jax.ShapeDtypeStruct((512, 256), BF16),
        scratch_shapes=[pltpu.VMEM((512, D), BF16)],
        compiler_params=params(10),
        cost_estimate=cost(1.9e9, 8e6),
        name="hidden_units",
    )(*[tokens[r] for r in PEER_ORDER], gate, up)


def down_kernel(order_ref, h0, h1, h2, h3, w0, w1, w2, w3, out):
    h = jnp.concatenate([part[...] for part in (h0, h1, h2, h3)], axis=1)
    for c in range(HALF_D // 256):
        cols = slice(c * 256, (c + 1) * 256)
        w = jnp.concatenate([p[:, cols] for p in (w0, w1, w2, w3)], axis=0)
        rows = jnp.dot(h, w, preferred_element_type=F32)
        for group in range(EP):
            out[order_ref[group], :, cols] = rows[group * CAP : (group + 1) * CAP, :].astype(BF16)


def down_rows(order, parts, weights):
    vmem = pl.BlockSpec(memory_space=pltpu.VMEM)
    return pl.pallas_call(
        down_kernel,
        in_specs=[smem()] + [vmem] * 8,
        out_specs=vmem,
        out_shape=jax.ShapeDtypeStruct((EP, CAP, HALF_D), BF16),
        compiler_params=params(10),
        cost_estimate=cost(1.9e9, 7e6),
        name="down_rows",
    )(order, *parts, *weights)


def blend_kernel(routing_ref, weight_ref, rows_ref, out):
    column = lax.broadcasted_iota(I32, (1, EP * CAP), 1)
    experts, slot = column >> 3, column & 7
    routing, weight = routing_ref[...], weight_ref[...]
    marks = jnp.zeros((TRAJ, EP * CAP), F32)
    share = jnp.zeros((TRAJ, EP * CAP), F32)
    for k in range(8):
        hit = routing[:, k : k + 1] == experts
        marks = marks + hit.astype(F32)
        share = share + jnp.where(hit, weight[:, k : k + 1], 0.0)
    share = jnp.where(earlier(marks) == slot.astype(F32), share, 0.0)
    high = share.astype(BF16)
    low = (share - high.astype(F32)).astype(BF16)
    rows = rows_ref[...].reshape(EP * CAP, rows_ref.shape[2])
    out[...] = (
        jnp.dot(high, rows, preferred_element_type=F32)
        + jnp.dot(low, rows, preferred_element_type=F32)
    ).astype(BF16)


def blend(routing, weight, rows):
    wide = 896
    return pl.pallas_call(
        blend_kernel,
        grid=(HALF_D // wide,),
        in_specs=[
            whole((TRAJ, 8)),
            whole((TRAJ, 8)),
            pl.BlockSpec((EP, CAP, wide), lambda i: (0, 0, i)),
        ],
        out_specs=pl.BlockSpec((TRAJ, wide), lambda i: (0, i)),
        out_shape=jax.ShapeDtypeStruct((TRAJ, HALF_D), BF16),
        compiler_params=params(10),
        cost_estimate=cost(1e8, 2e6),
        name="blend",
    )(routing, weight, rows)


def collect_kernel(index_ref, pages, *rest):
    out = rest[-1]
    step = pl.program_id(0)
    lane = lax.broadcasted_iota(I32, (32, LANES - LATENT), 1)
    for i in range(8):
        j = step * 8 + i
        out[i, 0:16, 0:LATENT] = pages[index_ref[j, 0]]
        out[i, 16:32, 0:LATENT] = pages[index_ref[j, 1]]
        slot, length = index_ref[j, 2].astype(F32), index_ref[j, 3].astype(F32)
        out[i, :, LATENT:LANES] = jnp.where(lane == 0, slot, length).astype(BF16)


def collect(index, pages, *before):
    return pl.pallas_call(
        collect_kernel,
        grid=(EP // 8,),
        in_specs=[smem(), whole(pages.shape)] + [smem()] * len(before),
        out_specs=pl.BlockSpec((8, 32, LANES), lambda i: (i, 0, 0)),
        out_shape=pltpu.HBM((EP, 32, LANES), BF16),
        compiler_params=params(10),
        cost_estimate=cost(1e6, 6e6),
        name="collect",
    )(index, pages, *before)


def regroup_kernel(midway, *rest):
    out = rest[-1]
    for i in range(4):
        out[i] = midway[:, i]


def regroup(midway, *before):
    return pl.pallas_call(
        regroup_kernel,
        grid=(2,),
        in_specs=[pl.BlockSpec((8, 4, 32, LANES), lambda i: (0, i, 0, 0))] + [smem()] * len(before),
        out_specs=pl.BlockSpec((4, 8, 32, LANES), lambda i: (i, 0, 0, 0)),
        out_shape=pltpu.HBM((8, 8, 32, LANES), BF16),
        compiler_params=params(8),
        cost_estimate=cost(1e6, 6e6),
        name="regroup",
    )(hbm(midway), *before)


def compact_kernel(source_ref, arrived, *rest):
    out = rest[-1]
    step = pl.program_id(0)
    for i in range(8):
        out[i] = arrived[source_ref[step * 8 + i]]


def compact(source, arrived, *before):
    return pl.pallas_call(
        compact_kernel,
        grid=(TRAJ // 8,),
        in_specs=[smem(), whole(arrived.shape)] + [smem()] * len(before),
        out_specs=pl.BlockSpec((8, 32, LANES), lambda i: (i, 0, 0)),
        out_shape=in_hbm((TRAJ, 32, LANES)),
        compiler_params=params(10),
        cost_estimate=cost(1e6, 4e6),
        name="compact",
    )(source, hbm(arrived), *before)


ATTEND_STEP = 8


def attend_kernel(tp_ref, length_ref, mine, other, queries, fresh, cache_out, out):
    step = pl.program_id(0)
    first = tp_ref[0] == 0
    row = lax.broadcasted_iota(I32, (MAXLEN, LATENT), 0).astype(F32).astype(BF16)
    column = lax.broadcasted_iota(I32, (TRAJ, MAXLEN), 1)
    scores = []
    for i in range(ATTEND_STEP):
        length = length_ref[step * ATTEND_STEP + i]
        edge = length.astype(F32).astype(BF16)
        a, b = mine[i, :, :LATENT], other[i, :, :LATENT]
        old = jnp.concatenate([jnp.where(first, a, b), jnp.where(first, b, a)], axis=0)
        new = jnp.broadcast_to(fresh[i], (MAXLEN, LATENT))
        zero = jnp.zeros((), BF16)
        cache = jnp.where(row < edge, old, jnp.where(row == edge, new, zero))
        cache_out[i] = cache
        score = lax.dot_general(
            queries[i], cache, (((1,), (1,)), ((), ())), preferred_element_type=F32
        )
        scores.append(jnp.where(column <= length, score * SCORE_SCALE, -jnp.inf))
    scores = jnp.concatenate(scores, axis=0)
    top = jnp.max(scores, axis=1, keepdims=True)
    weight = jnp.exp(scores - top)
    weight = (weight * (1.0 / jnp.sum(weight, axis=1, keepdims=True))).astype(BF16)
    for i in range(ATTEND_STEP):
        out[i] = jnp.dot(
            weight[i * TRAJ : (i + 1) * TRAJ],
            cache_out[i, :, :LATENT_WIDTH],
            preferred_element_type=F32,
        ).astype(BF16)


def attend(tp_index, length, mine, other, queries, fresh):
    n = ATTEND_STEP
    return pl.pallas_call(
        attend_kernel,
        grid=(TRAJ // n,),
        in_specs=[
            smem(),
            smem(),
            pl.BlockSpec((n, 32, LANES), lambda i: (i, 0, 0)),
            pl.BlockSpec((n, 32, LANES), lambda i: (i, 0, 0)),
            pl.BlockSpec((n, 32, LATENT), lambda i: (i, 0, 0)),
            pl.BlockSpec((n, 1, LATENT), lambda i: (i, 0, 0)),
        ],
        out_specs=[
            pl.BlockSpec((n, MAXLEN, LATENT), lambda i: (i, 0, 0)),
            pl.BlockSpec((n, 32, LATENT_WIDTH), lambda i: (i, 0, 0)),
        ],
        out_shape=[
            jax.ShapeDtypeStruct((TRAJ, MAXLEN, LATENT), BF16),
            jax.ShapeDtypeStruct((TRAJ, 32, LATENT_WIDTH), BF16),
        ],
        compiler_params=params(10),
        cost_estimate=cost(2e8, 8e6),
        name="attend",
    )(tp_index, length, mine, other, hbm(queries), fresh.reshape(TRAJ, 1, LATENT))


def once_kernel(*refs):
    refs[-1][0] = 0.0


def once(*arrays):
    return pl.pallas_call(
        once_kernel,
        in_specs=[pl.BlockSpec(memory_space=pl.ANY)] * len(arrays),
        out_specs=smem(),
        out_shape=jax.ShapeDtypeStruct((1,), F32),
        compiler_params=params(1),
        cost_estimate=cost(1, 4),
        name="once",
    )(*arrays)


def swap(x, axis):
    return lax.ppermute(x, axis, [(0, 1), (1, 0)])


def z_shift(x, by):
    return lax.ppermute(x, "z", [(i, (i + by) % NZ) for i in range(NZ)])


def plane_shift(x, dx, dy):
    return lax.ppermute(
        x,
        ("xh", "y"),
        [
            (a * NY + b, ((a + dx) % NX) * NY + (b + dy) % NY)
            for a in range(NX)
            for b in range(NY)
        ],
    )


def on_device(
    latent_pages,
    page_table,
    lengths,
    new_place,
    queries,
    fresh_latent,
    hidden_states,
    routing,
    route_weight,
    gate_value,
    gate_scale,
    up_value,
    up_scale,
    down_value,
    down_scale,
):
    xh, z, y, tp = (lax.axis_index(name) for name in ("xh", "z", "y", "tp"))
    tp_index = tp.astype(I32).reshape(1)
    place = jnp.stack([xh, z, y]).astype(I32)

    own = jnp.concatenate(
        [hidden_states, jnp.pad(routing.astype(BF16), ((0, 0), (0, BLOCK - 8)))], axis=1
    )
    up_way, down_way = [own, z_shift(own, 1)], [own, z_shift(own, -1)]
    down_send = scale_down(1 - tp_index, down_value, down_scale)
    down_tp = swap(down_send, "tp")

    owner, slot = new_place // TRAJ, new_place % TRAJ
    to_owner = owner[None, :] == jnp.asarray(PLANE_MAJOR)[:, None]
    mine = lax.dynamic_slice_in_dim(page_table, tp * 2, 2, 1)
    facts = jnp.concatenate([mine, slot[:, None] + 1, lengths[:, None]], axis=1)
    index = jnp.sum(jnp.where(to_owner[:, :, None], facts[None], 0), axis=1)
    index = index - (jnp.arange(4) == 2).astype(I32)[None, :]
    leaving = collect(index, latent_pages, once(up_way[1], down_way[1])).reshape(8, 8, 32, LANES)
    midway = lax.all_to_all(leaving, ("xh", "y"), split_axis=0, concat_axis=0, tiled=True)
    for step in range(1, 4):
        up_way.append(z_shift(up_way[-1], 1))
        if step < 3:
            down_way.append(z_shift(down_way[-1], -1))
    behind = np.array([0, 1, 2, 3, 4, -1, -2, -3], np.int32)

    gate = scale_wide(gate_value, gate_scale, once(up_way[1], down_way[1]))
    up = scale_wide(up_value, up_scale, once(up_way[2], down_way[2], down_tp))
    gate_far, up_far = swap(gate, "pool"), swap(up, "pool")

    midway = regroup(
        midway, once(up_way[4], down_way[3], gate_far, up_far)
    )
    picked = pick_rows(place, up_way + down_way[1:])
    tokens = list(picked)
    for peer in PEER_ORDER[:7]:
        tokens[peer] = plane_shift(picked[peer], peer // NY, peer % NY)

    down_keep = scale_down(tp_index, down_value, down_scale, once(picked[5]))
    down_far, down_tp_far = swap(down_keep, "pool"), swap(down_tp, "pool")

    arrived = lax.all_to_all(midway, "z", split_axis=0, concat_axis=0, tiled=True)

    act, act_far = hidden_units(tokens, gate, up), hidden_units(tokens, gate_far, up_far)
    act_tp, act_tp_far = swap(act, "tp"), swap(act_far, "tp")
    group = jnp.arange(EP, dtype=I32)
    order = (
        ((xh + (group >> 5)) % NX) * NZ + (z - jnp.tile(jnp.asarray(behind), 8)) % NZ
    ) * NY + (y - (group >> 3)) % NY
    out_rows = down_rows(
        order,
        [act, act_far, act_tp, act_tp_far],
        [down_keep, down_far, down_tp, down_tp_far],
    )
    returned = lax.all_to_all(
        out_rows, ("xh", "z", "y"), split_axis=0, concat_axis=0, tiled=True
    )
    expert_mix = blend(routing, route_weight, returned)

    arrived = arrived.reshape(EP, 32, LANES)
    labels = arrived[:, 0, LATENT : LATENT + 2].astype(I32)
    taken = labels[:, 0][None, :] == jnp.arange(TRAJ, dtype=I32)[:, None]
    source = jnp.sum(jnp.where(taken, jnp.arange(EP, dtype=I32)[None, :], 0), axis=1)
    length = jnp.sum(jnp.where(taken, labels[:, 1][None, :], 0), axis=1)
    my_half = compact(source, arrived, once(out_rows))
    other_half = swap(my_half, "tp")
    new_cache, attention = attend(tp_index, length, my_half, other_half, queries, fresh_latent)
    return new_cache, attention, expert_mix


def solution(mesh):
    grid = Mesh(mesh.devices.reshape(2, NX, NZ, NY, 2), ("pool", "xh", "z", "y", "tp"))
    ep = ("xh", "z", "y")
    rows = ("pool",) + ep
    placed = (
        P(rows, None, None),
        P(rows, None),
        P(rows),
        P(rows),
        P(rows, "tp", None),
        P(rows, None),
        P(rows, None),
        P(rows, None),
        P(rows, None),
        P(ep, None, ("pool", "tp")),
        P(ep, None, ("pool", "tp")),
        P(ep, None, ("pool", "tp")),
        P(ep, None, ("pool", "tp")),
        P(ep, ("pool", "tp"), None),
        P(ep, ("pool", "tp"), None),
    )
    return jax.shard_map(
        on_device,
        mesh=grid,
        in_specs=placed,
        out_specs=(P(rows, None, None), P(rows, "tp", None), P(rows, "tp")),
        check_vma=False,
    )
```

```python
import functools

import jax
import jax.numpy as jnp
import numpy as np
from jax import lax
from jax.experimental import pallas as pl
from jax.experimental.pallas import tpu as pltpu
from jax.sharding import Mesh, PartitionSpec as P

F32, BF16, I32 = jnp.float32, jnp.bfloat16, jnp.int32
LATENT_WIDTH = 512
BLOCK = 128
MAXLEN = 64
LATENT = 576
LANES = 640
D = 3584
HALF_D = 1792
TRAJ = 32
CAP = 8
NZ, NY, NX = 8, 4, 2
EP = NZ * NY * NX
SCORE_SCALE = 192.0 ** (-0.5)
MB = 1024 * 1024

SMEM = pltpu.SMEM
PLANE_MAJOR = np.arange(EP, dtype=np.int32).reshape(NX, NZ, NY).transpose(0, 2, 1).reshape(-1)


def whole(shape):
    return pl.BlockSpec(shape, lambda *_: (0,) * len(shape))


def smem():
    return pl.BlockSpec(memory_space=SMEM)


def hbm(*arrays):
    kept = tuple(pltpu.with_memory_space_constraint(x, pltpu.HBM) for x in arrays)
    return kept if len(kept) > 1 else kept[0]


def in_hbm(shape):
    return jax.ShapeDtypeStruct(shape, BF16)


def params(mb):
    return pltpu.CompilerParams(vmem_limit_bytes=mb * MB)


def cost(flops, nbytes):
    return pl.CostEstimate(flops=int(flops), bytes_accessed=int(nbytes), transcendentals=0)


def wide_kernel(scale, value, *rest):
    out = rest[-1]
    first = pl.program_id(0) == 0
    for f in range(2):
        for k in range(14):
            rows, cols = slice(k * BLOCK, (k + 1) * BLOCK), slice(f * BLOCK, (f + 1) * BLOCK)
            by = jnp.where(first, scale[f : f + 1, k : k + 1], scale[f : f + 1, 14 + k : 15 + k])
            out[rows, cols] = (value[0, rows, cols].astype(F32) * by).astype(BF16)


def scale_wide(value, scale, *before):
    return pl.pallas_call(
        wide_kernel,
        grid=(2,),
        in_specs=[whole((2, 28)), pl.BlockSpec((1, D // 2, 256), lambda i: (0, i, 0))]
        + [smem()] * len(before),
        out_specs=pl.BlockSpec((D // 2, 256), lambda i: (i, 0)),
        out_shape=jax.ShapeDtypeStruct((D, 256), BF16),
        compiler_params=params(8),
        cost_estimate=cost(1e6, 4e6),
        name="scale_wide",
    )(scale[0].T.astype(F32), hbm(value), *before)


def narrow_kernel(half_ref, scale, value, *rest):
    out = rest[-1]
    first = half_ref[0] == 0
    for a in range(2):
        for k in range(14):
            rows, cols = slice(a * BLOCK, (a + 1) * BLOCK), slice(k * BLOCK, (k + 1) * BLOCK)
            by = jnp.where(first, scale[a : a + 1, k : k + 1], scale[a : a + 1, 14 + k : 15 + k])
            out[rows, cols] = (value[0, rows, cols].astype(F32) * by).astype(BF16)


def scale_down(half, value, scale, *before):
    return pl.pallas_call(
        narrow_kernel,
        grid_spec=pltpu.PrefetchScalarGridSpec(
            num_scalar_prefetch=1,
            grid=(1,),
            in_specs=[
                pl.BlockSpec((2, 28), lambda i, h: (0, 0)),
                pl.BlockSpec((1, 256, HALF_D), lambda i, h: (0, 0, h[0])),
            ]
            + [smem()] * len(before),
            out_specs=pl.BlockSpec((256, HALF_D), lambda i, h: (0, 0)),
        ),
        out_shape=jax.ShapeDtypeStruct((256, HALF_D), BF16),
        compiler_params=params(8),
        cost_estimate=cost(1e6, 2e6),
        name="scale_down",
    )(half, scale[0].astype(F32), hbm(value), *before)


def named_by(routing, experts):
    marks = jnp.zeros((routing.shape[0], experts.shape[1]), F32)
    for k in range(routing.shape[1]):
        marks = marks + (routing[:, k : k + 1] == experts).astype(F32)
    return marks


def earlier(marks):
    n = marks.shape[0]
    lower = (
        lax.broadcasted_iota(I32, (n, n), 0) > lax.broadcasted_iota(I32, (n, n), 1)
    ).astype(BF16)
    return jnp.dot(lower, marks.astype(BF16), preferred_element_type=F32)


def pick_kernel(place_ref, *refs):
    blocks, outs = refs[:NZ], refs[NZ:]
    xh, z, y = place_ref[0], place_ref[1], place_ref[2]
    column = lax.broadcasted_iota(I32, (1, EP), 1)
    peer, slot = column >> 3, column & 7
    experts = (((peer >> 2) ^ xh) * NZ + z) * NY + (((peer & 3) + y) & 3)
    for b, block in enumerate(blocks):
        marks = named_by(block[:, D : D + 8].astype(F32).astype(I32), experts)
        chosen = jnp.where(earlier(marks) == slot.astype(F32), marks, 0.0).astype(BF16)
        rows = lax.dot_general(
            chosen, block[:, :D], (((0,), (0,)), ((), ())), preferred_element_type=F32
        ).astype(BF16)
        for r, out in enumerate(outs):
            out[b * CAP : (b + 1) * CAP, :] = rows[r * CAP : (r + 1) * CAP, :]


def pick_rows(place, blocks):
    vmem = pl.BlockSpec(memory_space=pltpu.VMEM)
    return pl.pallas_call(
        pick_kernel,
        in_specs=[smem()] + [vmem] * NZ,
        out_specs=[vmem] * 8,
        out_shape=[jax.ShapeDtypeStruct((NZ * CAP, D), BF16)] * 8,
        compiler_params=params(6),
        cost_estimate=cost(1e9, 6e6),
        name="pick_rows",
    )(place, *blocks)


PEER_ORDER = (0, 4, 1, 5, 2, 6, 3, 7)


def hidden_kernel(*refs):
    tokens, (g0, g1, u0, u1, out, x) = refs[:4], refs[4:]
    for n, token in enumerate(tokens):
        x[n * 64 : (n + 1) * 64, :] = token[...]
    for n, (gate, up) in enumerate(((g0, u0), (g1, u1))):
        g = jnp.dot(x[...], gate[...], preferred_element_type=F32)
        u = jnp.dot(x[...], up[...], preferred_element_type=F32)
        out[:, n * 256 : (n + 1) * 256] = (g / (1.0 + jnp.exp(-g)) * u).astype(BF16)


def hidden_units(tokens, panels):
    vmem = pl.BlockSpec(memory_space=pltpu.VMEM)
    return pl.pallas_call(
        hidden_kernel,
        in_specs=[vmem] * 8,
        out_specs=vmem,
        out_shape=jax.ShapeDtypeStruct((256, 512), BF16),
        scratch_shapes=[pltpu.VMEM((256, D), BF16)],
        compiler_params=params(8),
        cost_estimate=cost(1.9e9, 8e6),
        name="hidden_units",
    )(*tokens, *panels)


def down_kernel(order_ref, a0, a1, b0, b1, w0, w1, w2, w3, out):
    h = jnp.concatenate(
        [
            jnp.concatenate([a0[...], a1[...]], axis=1),
            jnp.concatenate([b0[...], b1[...]], axis=1),
        ],
        axis=0,
    )
    for c in range(HALF_D // 256):
        cols = slice(c * 256, (c + 1) * 256)
        w = jnp.concatenate([p[:, cols] for p in (w0, w1, w2, w3)], axis=0)
        rows = jnp.dot(h, w, preferred_element_type=F32)
        for group in range(EP):
            out[order_ref[group], :, cols] = rows[group * CAP : (group + 1) * CAP, :].astype(BF16)


def down_rows(order, parts, weights):
    vmem = pl.BlockSpec(memory_space=pltpu.VMEM)
    return pl.pallas_call(
        down_kernel,
        in_specs=[smem()] + [vmem] * 8,
        out_specs=vmem,
        out_shape=jax.ShapeDtypeStruct((EP, CAP, HALF_D), BF16),
        compiler_params=params(10),
        cost_estimate=cost(1.9e9, 7e6),
        name="down_rows",
    )(order, *parts, *weights)


def blend_kernel(late_ref, routing_ref, weight_ref, rows_ref, out, done):
    done[0] = 0.0
    column = lax.broadcasted_iota(I32, (1, EP * CAP), 1)
    experts, slot = column >> 3, column & 7
    routing, weight = routing_ref[...], weight_ref[...]
    marks = jnp.zeros((TRAJ, EP * CAP), F32)
    share = jnp.zeros((TRAJ, EP * CAP), F32)
    for k in range(8):
        hit = routing[:, k : k + 1] == experts
        marks = marks + hit.astype(F32)
        share = share + jnp.where(hit, weight[:, k : k + 1], 0.0)
    share = jnp.where(earlier(marks) == slot.astype(F32), share, 0.0)
    high = share.astype(BF16)
    low = (share - high.astype(F32)).astype(BF16)
    rows = rows_ref[...].reshape(EP * CAP, rows_ref.shape[2])
    out[...] = (
        jnp.dot(high, rows, preferred_element_type=F32)
        + jnp.dot(low, rows, preferred_element_type=F32)
    ).astype(BF16)


def blend(late, routing, weight, rows):
    wide = 896
    return pl.pallas_call(
        blend_kernel,
        grid=(HALF_D // wide,),
        in_specs=[
            smem(),
            whole((TRAJ, 8)),
            whole((TRAJ, 8)),
            pl.BlockSpec((EP, CAP, wide), lambda i: (0, 0, i)),
        ],
        out_specs=[pl.BlockSpec((TRAJ, wide), lambda i: (0, i)), smem()],
        out_shape=[
            jax.ShapeDtypeStruct((TRAJ, HALF_D), BF16),
            jax.ShapeDtypeStruct((1,), F32),
        ],
        compiler_params=params(10),
        cost_estimate=cost(1e8, 2e6),
        name="blend",
    )(late, routing, weight, rows)


def collect_kernel(index_ref, pages, *rest):
    out = rest[-1]
    step = pl.program_id(0)
    lane = lax.broadcasted_iota(I32, (32, LANES - LATENT), 1)
    for i in range(16):
        j = step * 16 + i
        out[i, 0:16, 0:LATENT] = pages[index_ref[j, 0]]
        out[i, 16:32, 0:LATENT] = pages[index_ref[j, 1]]
        slot, length = index_ref[j, 2].astype(F32), index_ref[j, 3].astype(F32)
        out[i, :, LATENT:LANES] = jnp.where(lane == 0, slot, length).astype(BF16)


def collect(index, pages, *before):
    return pl.pallas_call(
        collect_kernel,
        grid=(EP // 16,),
        in_specs=[smem(), whole(pages.shape)] + [smem()] * len(before),
        out_specs=pl.BlockSpec((16, 32, LANES), lambda i: (i, 0, 0)),
        out_shape=pltpu.HBM((EP, 32, LANES), BF16),
        compiler_params=params(10),
        cost_estimate=cost(1e6, 6e6),
        name="collect",
    )(index, pages, *before)


def regroup_kernel(midway, *rest):
    out = rest[-1]
    for i in range(4):
        out[i] = midway[:, i]


def regroup(midway, *before):
    return pl.pallas_call(
        regroup_kernel,
        grid=(2,),
        in_specs=[pl.BlockSpec((8, 4, 32, LANES), lambda i: (0, i, 0, 0))] + [smem()] * len(before),
        out_specs=pl.BlockSpec((4, 8, 32, LANES), lambda i: (i, 0, 0, 0)),
        out_shape=pltpu.HBM((8, 8, 32, LANES), BF16),
        compiler_params=params(8),
        cost_estimate=cost(1e6, 6e6),
        name="regroup",
    )(hbm(midway), *before)


def compact_kernel(source_ref, arrived, late_ref, first, second):
    for s in range(TRAJ // 2):
        first[s] = arrived[source_ref[s]]
        second[s] = arrived[source_ref[TRAJ // 2 + s]]


def compact(source, arrived, late):
    half = (TRAJ // 2, 32, LANES)
    return pl.pallas_call(
        compact_kernel,
        grid=(1,),
        in_specs=[smem(), whole(arrived.shape), smem()],
        out_specs=[whole(half)] * 2,
        out_shape=[in_hbm(half)] * 2,
        compiler_params=params(10),
        cost_estimate=cost(1e6, 4e6),
        name="compact",
    )(source, hbm(arrived), late)


ATTEND_STEP = 8


def attend_kernel(start, late_ref, tp_ref, length_ref, mine, other, queries, fresh, *rest):
    cache_out, out, done = rest[-3:]
    done[0] = 0.0
    step = pl.program_id(0) + start
    first = tp_ref[0] == 0
    row = lax.broadcasted_iota(I32, (MAXLEN, LATENT), 0).astype(F32).astype(BF16)
    column = lax.broadcasted_iota(I32, (TRAJ, MAXLEN), 1)
    scores = []
    for i in range(ATTEND_STEP):
        length = length_ref[step * ATTEND_STEP + i]
        edge = length.astype(F32).astype(BF16)
        a, b = mine[i, :, :LATENT], other[i, :, :LATENT]
        old = jnp.concatenate([jnp.where(first, a, b), jnp.where(first, b, a)], axis=0)
        new = jnp.broadcast_to(fresh[i], (MAXLEN, LATENT))
        zero = jnp.zeros((), BF16)
        cache = jnp.where(row < edge, old, jnp.where(row == edge, new, zero))
        cache_out[i] = cache
        score = lax.dot_general(
            queries[i], cache, (((1,), (1,)), ((), ())), preferred_element_type=F32
        )
        scores.append(jnp.where(column <= length, score * SCORE_SCALE, -jnp.inf))
    scores = jnp.concatenate(scores, axis=0)
    top = jnp.max(scores, axis=1, keepdims=True)
    weight = jnp.exp(scores - top)
    weight = (weight * (1.0 / jnp.sum(weight, axis=1, keepdims=True))).astype(BF16)
    for i in range(ATTEND_STEP):
        out[i] = jnp.dot(
            weight[i * TRAJ : (i + 1) * TRAJ],
            cache_out[i, :, :LATENT_WIDTH],
            preferred_element_type=F32,
        ).astype(BF16)


def attend(half, late, tp_index, length, mine, other, queries, fresh, *so_far):
    n = ATTEND_STEP
    start = half * (TRAJ // 2 // n)
    there = pl.BlockSpec(memory_space=pl.ANY)
    return pl.pallas_call(
        functools.partial(attend_kernel, start),
        grid=(TRAJ // 2 // n,),
        in_specs=[
            smem(),
            smem(),
            smem(),
            pl.BlockSpec((n, 32, LANES), lambda i: (i, 0, 0)),
            pl.BlockSpec((n, 32, LANES), lambda i: (i, 0, 0)),
            pl.BlockSpec((n, 32, LATENT), lambda i: (i + start, 0, 0)),
            pl.BlockSpec((n, 1, LATENT), lambda i: (i + start, 0, 0)),
        ]
        + [there] * len(so_far),
        out_specs=[
            pl.BlockSpec((n, MAXLEN, LATENT), lambda i: (i + start, 0, 0)),
            pl.BlockSpec((n, 32, LATENT_WIDTH), lambda i: (i + start, 0, 0)),
            smem(),
        ],
        out_shape=[
            jax.ShapeDtypeStruct((TRAJ, MAXLEN, LATENT), BF16),
            jax.ShapeDtypeStruct((TRAJ, 32, LATENT_WIDTH), BF16),
            jax.ShapeDtypeStruct((1,), F32),
        ],
        input_output_aliases={7 + k: k for k in range(len(so_far))},
        compiler_params=params(10),
        cost_estimate=cost(1e8, 4e6),
        name="attend",
    )(late, tp_index, length, mine, other, hbm(queries), fresh, *so_far)


def once_kernel(*refs):
    refs[-1][0] = 0.0


def once(*arrays):
    return pl.pallas_call(
        once_kernel,
        in_specs=[pl.BlockSpec(memory_space=pl.ANY)] * len(arrays),
        out_specs=smem(),
        out_shape=jax.ShapeDtypeStruct((1,), F32),
        compiler_params=params(1),
        cost_estimate=cost(1, 4),
        name="once",
    )(*arrays)


def swap(x, axis):
    return lax.ppermute(x, axis, [(0, 1), (1, 0)])


def z_shift(x, by):
    return lax.ppermute(x, "z", [(i, (i + by) % NZ) for i in range(NZ)])


def plane_shift(x, dx, dy):
    return lax.ppermute(
        x,
        ("xh", "y"),
        [
            (a * NY + b, ((a + dx) % NX) * NY + (b + dy) % NY)
            for a in range(NX)
            for b in range(NY)
        ],
    )


def on_device(
    latent_pages,
    page_table,
    lengths,
    new_place,
    queries,
    fresh_latent,
    hidden_states,
    routing,
    route_weight,
    gate_value,
    gate_scale,
    up_value,
    up_scale,
    down_value,
    down_scale,
):
    xh, z, y, tp = (lax.axis_index(name) for name in ("xh", "z", "y", "tp"))
    tp_index = tp.astype(I32).reshape(1)
    place = jnp.stack([xh, z, y]).astype(I32)

    own = jnp.concatenate(
        [hidden_states, jnp.pad(routing.astype(BF16), ((0, 0), (0, BLOCK - 8)))], axis=1
    )
    up_way, down_way = [own, z_shift(own, 1)], [own, z_shift(own, -1)]
    down_send = scale_down(1 - tp_index, down_value, down_scale)
    down_tp = swap(down_send, "tp")

    owner, slot = new_place // TRAJ, new_place % TRAJ
    to_owner = owner[None, :] == jnp.asarray(PLANE_MAJOR)[:, None]
    mine = lax.dynamic_slice_in_dim(page_table, tp * 2, 2, 1)
    facts = jnp.concatenate([mine, slot[:, None] + 1, lengths[:, None]], axis=1)
    index = jnp.sum(jnp.where(to_owner[:, :, None], facts[None], 0), axis=1)
    index = index - (jnp.arange(4) == 2).astype(I32)[None, :]
    leaving = collect(index, latent_pages, once(up_way[1], down_way[1])).reshape(8, 8, 32, LANES)
    midway = lax.all_to_all(leaving, ("xh", "y"), split_axis=0, concat_axis=0, tiled=True)
    for step in range(1, 4):
        up_way.append(z_shift(up_way[-1], 1))
        if step < 3:
            down_way.append(z_shift(down_way[-1], -1))
    behind = np.array([0, 1, 2, 3, 4, -1, -2, -3], np.int32)

    gate = scale_wide(gate_value, gate_scale, once(up_way[1], down_way[1]))
    up = scale_wide(up_value, up_scale, once(up_way[2], down_way[2], down_tp))
    gate_far, up_far = swap(gate, "pool"), swap(up, "pool")

    midway = regroup(
        midway, once(up_way[4], down_way[3], gate_far, up_far)
    )
    picked = pick_rows(place, up_way + down_way[1:])
    tokens = list(picked)
    for peer in PEER_ORDER[1:]:
        tokens[peer] = plane_shift(picked[peer], peer // NY, peer % NY)

    down_keep = scale_down(tp_index, down_value, down_scale, once(picked[5]))
    down_far, down_tp_far = swap(down_keep, "pool"), swap(down_tp, "pool")

    arrived = lax.all_to_all(midway, "z", split_axis=0, concat_axis=0, tiled=True)

    panels = (gate, gate_far, up, up_far)
    act = hidden_units([tokens[peer] for peer in PEER_ORDER[:4]], panels)
    act_tp = swap(act, "tp")
    act_late = hidden_units([tokens[peer] for peer in PEER_ORDER[4:]], panels)
    act_late_tp = swap(act_late, "tp")
    peer = jnp.asarray(np.repeat(np.array(PEER_ORDER, np.int32), 8))
    order = (
        ((xh + (peer >> 2)) % NX) * NZ + (z - jnp.asarray(np.tile(behind, 8))) % NZ
    ) * NY + (y - peer) % NY
    out_rows = down_rows(
        order,
        [act, act_tp, act_late, act_late_tp],
        [down_keep, down_far, down_tp, down_tp_far],
    )
    returned = lax.all_to_all(
        out_rows, ("xh", "z", "y"), split_axis=0, concat_axis=0, tiled=True
    )

    arrived = arrived.reshape(EP, 32, LANES)
    labels = arrived[:, 0, LATENT : LATENT + 2].astype(I32)
    taken = labels[:, 0][None, :] == jnp.arange(TRAJ, dtype=I32)[:, None]
    source = jnp.sum(jnp.where(taken, jnp.arange(EP, dtype=I32)[None, :], 0), axis=1)
    length = jnp.sum(jnp.where(taken, labels[:, 1][None, :], 0), axis=1)
    fresh = fresh_latent.reshape(TRAJ, 1, LATENT)
    late = once(out_rows)
    halves = compact(source, arrived, late)
    others = [swap(part, "tp") for part in halves]
    so_far = attend(0, late, tp_index, length, halves[0], others[0], queries, fresh)
    expert_mix, late = blend(so_far[2], routing, route_weight, returned)
    new_cache, attention, _ = attend(
        1, late, tp_index, length, halves[1], others[1], queries, fresh, *so_far[:2]
    )
    return new_cache, attention, expert_mix


def solution(mesh):
    grid = Mesh(mesh.devices.reshape(2, NX, NZ, NY, 2), ("pool", "xh", "z", "y", "tp"))
    ep = ("xh", "z", "y")
    rows = ("pool",) + ep
    placed = (
        P(rows, None, None),
        P(rows, None),
        P(rows),
        P(rows),
        P(rows, "tp", None),
        P(rows, None),
        P(rows, None),
        P(rows, None),
        P(rows, None),
        P(ep, None, ("pool", "tp")),
        P(ep, None, ("pool", "tp")),
        P(ep, None, ("pool", "tp")),
        P(ep, None, ("pool", "tp")),
        P(ep, ("pool", "tp"), None),
        P(ep, ("pool", "tp"), None),
    )
    return jax.shard_map(
        on_device,
        mesh=grid,
        in_specs=placed,
        out_specs=(P(rows, None, None), P(rows, "tp", None), P(rows, "tp")),
        check_vma=False,
    )
```

```python
import functools

import jax
import jax.numpy as jnp
import numpy as np
from jax import lax
from jax.experimental import pallas as pl
from jax.experimental.pallas import tpu as pltpu
from jax.sharding import Mesh, PartitionSpec as P

F32, BF16, I32 = jnp.float32, jnp.bfloat16, jnp.int32
LATENT_WIDTH = 512
BLOCK = 128
MAXLEN = 64
LATENT = 576
LANES = 640
D = 3584
HALF_D = 1792
TRAJ = 32
CAP = 8
NZ, NY, NX = 8, 4, 2
EP = NZ * NY * NX
SCORE_SCALE = 192.0 ** (-0.5)
MB = 1024 * 1024

SMEM = pltpu.SMEM
PLANE_MAJOR = np.arange(EP, dtype=np.int32).reshape(NX, NZ, NY).transpose(0, 2, 1).reshape(-1)


def whole(shape):
    return pl.BlockSpec(shape, lambda *_: (0,) * len(shape))


def smem():
    return pl.BlockSpec(memory_space=SMEM)


def hbm(*arrays):
    kept = tuple(pltpu.with_memory_space_constraint(x, pltpu.HBM) for x in arrays)
    return kept if len(kept) > 1 else kept[0]


def in_hbm(shape):
    return jax.ShapeDtypeStruct(shape, BF16)


def params(mb):
    return pltpu.CompilerParams(vmem_limit_bytes=mb * MB)


def cost(flops, nbytes):
    return pl.CostEstimate(flops=int(flops), bytes_accessed=int(nbytes), transcendentals=0)


def wide_kernel(scale, value, *rest):
    out = rest[-1]
    first = pl.program_id(0) == 0
    for f in range(2):
        for k in range(14):
            rows, cols = slice(k * BLOCK, (k + 1) * BLOCK), slice(f * BLOCK, (f + 1) * BLOCK)
            by = jnp.where(first, scale[f : f + 1, k : k + 1], scale[f : f + 1, 14 + k : 15 + k])
            out[rows, cols] = (value[0, rows, cols].astype(F32) * by).astype(BF16)


def scale_wide(value, scale, *before):
    return pl.pallas_call(
        wide_kernel,
        grid=(2,),
        in_specs=[whole((2, 28)), pl.BlockSpec((1, D // 2, 256), lambda i: (0, i, 0))]
        + [smem()] * len(before),
        out_specs=pl.BlockSpec((D // 2, 256), lambda i: (i, 0)),
        out_shape=jax.ShapeDtypeStruct((D, 256), BF16),
        compiler_params=params(8),
        cost_estimate=cost(1e6, 4e6),
        name="scale_wide",
    )(scale[0].T.astype(F32), hbm(value), *before)


def narrow_kernel(half_ref, scale, value, *rest):
    out = rest[-1]
    first = half_ref[0] == 0
    for a in range(2):
        for k in range(14):
            rows, cols = slice(a * BLOCK, (a + 1) * BLOCK), slice(k * BLOCK, (k + 1) * BLOCK)
            by = jnp.where(first, scale[a : a + 1, k : k + 1], scale[a : a + 1, 14 + k : 15 + k])
            out[rows, cols] = (value[0, rows, cols].astype(F32) * by).astype(BF16)


def scale_down(half, value, scale, *before):
    return pl.pallas_call(
        narrow_kernel,
        grid_spec=pltpu.PrefetchScalarGridSpec(
            num_scalar_prefetch=1,
            grid=(1,),
            in_specs=[
                pl.BlockSpec((2, 28), lambda i, h: (0, 0)),
                pl.BlockSpec((1, 256, HALF_D), lambda i, h: (0, 0, h[0])),
            ]
            + [smem()] * len(before),
            out_specs=pl.BlockSpec((256, HALF_D), lambda i, h: (0, 0)),
        ),
        out_shape=jax.ShapeDtypeStruct((256, HALF_D), BF16),
        compiler_params=params(8),
        cost_estimate=cost(1e6, 2e6),
        name="scale_down",
    )(half, scale[0].astype(F32), hbm(value), *before)


def named_by(routing, experts):
    marks = jnp.zeros((routing.shape[0], experts.shape[1]), F32)
    for k in range(routing.shape[1]):
        marks = marks + (routing[:, k : k + 1] == experts).astype(F32)
    return marks


def earlier(marks):
    n = marks.shape[0]
    lower = (
        lax.broadcasted_iota(I32, (n, n), 0) > lax.broadcasted_iota(I32, (n, n), 1)
    ).astype(BF16)
    return jnp.dot(lower, marks.astype(BF16), preferred_element_type=F32)


def pick_kernel(place_ref, *refs):
    blocks, outs = refs[:NZ], refs[NZ:]
    xh, z, y = place_ref[0], place_ref[1], place_ref[2]
    column = lax.broadcasted_iota(I32, (1, EP), 1)
    peer, slot = column >> 3, column & 7
    experts = (((peer >> 2) ^ xh) * NZ + z) * NY + (((peer & 3) + y) & 3)
    for b, block in enumerate(blocks):
        marks = named_by(block[:, D : D + 8].astype(F32).astype(I32), experts)
        chosen = jnp.where(earlier(marks) == slot.astype(F32), marks, 0.0).astype(BF16)
        rows = lax.dot_general(
            chosen, block[:, :D], (((0,), (0,)), ((), ())), preferred_element_type=F32
        ).astype(BF16)
        for r, out in enumerate(outs):
            out[b * CAP : (b + 1) * CAP, :] = rows[r * CAP : (r + 1) * CAP, :]


def pick_rows(place, blocks):
    vmem = pl.BlockSpec(memory_space=pltpu.VMEM)
    return pl.pallas_call(
        pick_kernel,
        in_specs=[smem()] + [vmem] * NZ,
        out_specs=[vmem] * 8,
        out_shape=[jax.ShapeDtypeStruct((NZ * CAP, D), BF16)] * 8,
        compiler_params=params(6),
        cost_estimate=cost(1e9, 6e6),
        name="pick_rows",
    )(place, *blocks)


PEER_ORDER = (4, 1, 5, 2, 6, 3, 7, 0)


def hidden_kernel(*refs):
    tokens, (gate, up, out, x) = refs[:8], refs[8:]
    for r, token in zip(PEER_ORDER, tokens):
        x[r * 64 : (r + 1) * 64, :] = token[...]
    for half in range(2):
        rows = slice(half * 256, (half + 1) * 256)
        g = jnp.dot(x[rows, :], gate[...], preferred_element_type=F32)
        u = jnp.dot(x[rows, :], up[...], preferred_element_type=F32)
        out[rows, :] = (g / (1.0 + jnp.exp(-g)) * u).astype(BF16)


def hidden_units(tokens, gate, up):
    vmem = pl.BlockSpec(memory_space=pltpu.VMEM)
    return pl.pallas_call(
        hidden_kernel,
        in_specs=[vmem] * 10,
        out_specs=vmem,
        out_shape=jax.ShapeDtypeStruct((512, 256), BF16),
        scratch_shapes=[pltpu.VMEM((512, D), BF16)],
        compiler_params=params(10),
        cost_estimate=cost(1.9e9, 8e6),
        name="hidden_units",
    )(*[tokens[r] for r in PEER_ORDER], gate, up)


def down_kernel(order_ref, h0, h1, h2, h3, w0, w1, w2, w3, out):
    h = jnp.concatenate([part[...] for part in (h0, h1, h2, h3)], axis=1)
    for c in range(HALF_D // 256):
        cols = slice(c * 256, (c + 1) * 256)
        w = jnp.concatenate([p[:, cols] for p in (w0, w1, w2, w3)], axis=0)
        rows = jnp.dot(h, w, preferred_element_type=F32)
        for group in range(EP):
            out[order_ref[group], :, cols] = rows[group * CAP : (group + 1) * CAP, :].astype(BF16)


def down_rows(order, parts, weights):
    vmem = pl.BlockSpec(memory_space=pltpu.VMEM)
    return pl.pallas_call(
        down_kernel,
        in_specs=[smem()] + [vmem] * 8,
        out_specs=vmem,
        out_shape=jax.ShapeDtypeStruct((EP, CAP, HALF_D), BF16),
        compiler_params=params(10),
        cost_estimate=cost(1.9e9, 7e6),
        name="down_rows",
    )(order, *parts, *weights)


def blend_kernel(late_ref, routing_ref, weight_ref, rows_ref, out, done):
    done[0] = 0.0
    column = lax.broadcasted_iota(I32, (1, EP * CAP), 1)
    experts, slot = column >> 3, column & 7
    routing, weight = routing_ref[...], weight_ref[...]
    marks = jnp.zeros((TRAJ, EP * CAP), F32)
    share = jnp.zeros((TRAJ, EP * CAP), F32)
    for k in range(8):
        hit = routing[:, k : k + 1] == experts
        marks = marks + hit.astype(F32)
        share = share + jnp.where(hit, weight[:, k : k + 1], 0.0)
    share = jnp.where(earlier(marks) == slot.astype(F32), share, 0.0)
    high = share.astype(BF16)
    low = (share - high.astype(F32)).astype(BF16)
    rows = rows_ref[...].reshape(EP * CAP, rows_ref.shape[2])
    out[...] = (
        jnp.dot(high, rows, preferred_element_type=F32)
        + jnp.dot(low, rows, preferred_element_type=F32)
    ).astype(BF16)


def blend(late, routing, weight, rows):
    wide = 896
    return pl.pallas_call(
        blend_kernel,
        grid=(HALF_D // wide,),
        in_specs=[
            smem(),
            whole((TRAJ, 8)),
            whole((TRAJ, 8)),
            pl.BlockSpec((EP, CAP, wide), lambda i: (0, 0, i)),
        ],
        out_specs=[pl.BlockSpec((TRAJ, wide), lambda i: (0, i)), smem()],
        out_shape=[
            jax.ShapeDtypeStruct((TRAJ, HALF_D), BF16),
            jax.ShapeDtypeStruct((1,), F32),
        ],
        compiler_params=params(10),
        cost_estimate=cost(1e8, 2e6),
        name="blend",
    )(late, routing, weight, rows)


def collect_kernel(index_ref, pages, *rest):
    out = rest[-1]
    step = pl.program_id(0)
    lane = lax.broadcasted_iota(I32, (32, LANES - LATENT), 1)
    for i in range(16):
        j = step * 16 + i
        out[i, 0:16, 0:LATENT] = pages[index_ref[j, 0]]
        out[i, 16:32, 0:LATENT] = pages[index_ref[j, 1]]
        slot, length = index_ref[j, 2].astype(F32), index_ref[j, 3].astype(F32)
        out[i, :, LATENT:LANES] = jnp.where(lane == 0, slot, length).astype(BF16)


def collect(index, pages, *before):
    return pl.pallas_call(
        collect_kernel,
        grid=(EP // 16,),
        in_specs=[smem(), whole(pages.shape)] + [smem()] * len(before),
        out_specs=pl.BlockSpec((16, 32, LANES), lambda i: (i, 0, 0)),
        out_shape=pltpu.HBM((EP, 32, LANES), BF16),
        compiler_params=params(10),
        cost_estimate=cost(1e6, 6e6),
        name="collect",
    )(index, pages, *before)


def regroup_kernel(midway, *rest):
    out = rest[-1]
    for i in range(4):
        out[i] = midway[:, i]


def regroup(midway, *before):
    return pl.pallas_call(
        regroup_kernel,
        grid=(2,),
        in_specs=[pl.BlockSpec((8, 4, 32, LANES), lambda i: (0, i, 0, 0))] + [smem()] * len(before),
        out_specs=pl.BlockSpec((4, 8, 32, LANES), lambda i: (i, 0, 0, 0)),
        out_shape=pltpu.HBM((8, 8, 32, LANES), BF16),
        compiler_params=params(8),
        cost_estimate=cost(1e6, 6e6),
        name="regroup",
    )(hbm(midway), *before)


def compact_kernel(source_ref, arrived, late_ref, first, second):
    for s in range(TRAJ // 2):
        first[s] = arrived[source_ref[s]]
        second[s] = arrived[source_ref[TRAJ // 2 + s]]


def compact(source, arrived, late):
    half = (TRAJ // 2, 32, LANES)
    return pl.pallas_call(
        compact_kernel,
        grid=(1,),
        in_specs=[smem(), whole(arrived.shape), smem()],
        out_specs=[whole(half)] * 2,
        out_shape=[in_hbm(half)] * 2,
        compiler_params=params(10),
        cost_estimate=cost(1e6, 4e6),
        name="compact",
    )(source, hbm(arrived), late)


ATTEND_STEP = 8


def attend_kernel(start, late_ref, tp_ref, length_ref, mine, other, queries, fresh, *rest):
    cache_out, out, done = rest[-3:]
    done[0] = 0.0
    step = pl.program_id(0) + start
    first = tp_ref[0] == 0
    row = lax.broadcasted_iota(I32, (MAXLEN, LATENT), 0).astype(F32).astype(BF16)
    column = lax.broadcasted_iota(I32, (TRAJ, MAXLEN), 1)
    scores = []
    for i in range(ATTEND_STEP):
        length = length_ref[step * ATTEND_STEP + i]
        edge = length.astype(F32).astype(BF16)
        a, b = mine[i, :, :LATENT], other[i, :, :LATENT]
        old = jnp.concatenate([jnp.where(first, a, b), jnp.where(first, b, a)], axis=0)
        new = jnp.broadcast_to(fresh[i], (MAXLEN, LATENT))
        zero = jnp.zeros((), BF16)
        cache = jnp.where(row < edge, old, jnp.where(row == edge, new, zero))
        cache_out[i] = cache
        score = lax.dot_general(
            queries[i], cache, (((1,), (1,)), ((), ())), preferred_element_type=F32
        )
        scores.append(jnp.where(column <= length, score * SCORE_SCALE, -jnp.inf))
    scores = jnp.concatenate(scores, axis=0)
    top = jnp.max(scores, axis=1, keepdims=True)
    weight = jnp.exp(scores - top)
    weight = (weight * (1.0 / jnp.sum(weight, axis=1, keepdims=True))).astype(BF16)
    for i in range(ATTEND_STEP):
        out[i] = jnp.dot(
            weight[i * TRAJ : (i + 1) * TRAJ],
            cache_out[i, :, :LATENT_WIDTH],
            preferred_element_type=F32,
        ).astype(BF16)


def attend(half, late, tp_index, length, mine, other, queries, fresh, *so_far):
    n = ATTEND_STEP
    start = half * (TRAJ // 2 // n)
    there = pl.BlockSpec(memory_space=pl.ANY)
    return pl.pallas_call(
        functools.partial(attend_kernel, start),
        grid=(TRAJ // 2 // n,),
        in_specs=[
            smem(),
            smem(),
            smem(),
            pl.BlockSpec((n, 32, LANES), lambda i: (i, 0, 0)),
            pl.BlockSpec((n, 32, LANES), lambda i: (i, 0, 0)),
            pl.BlockSpec((n, 32, LATENT), lambda i: (i + start, 0, 0)),
            pl.BlockSpec((n, 1, LATENT), lambda i: (i + start, 0, 0)),
        ]
        + [there] * len(so_far),
        out_specs=[
            pl.BlockSpec((n, MAXLEN, LATENT), lambda i: (i + start, 0, 0)),
            pl.BlockSpec((n, 32, LATENT_WIDTH), lambda i: (i + start, 0, 0)),
            smem(),
        ],
        out_shape=[
            jax.ShapeDtypeStruct((TRAJ, MAXLEN, LATENT), BF16),
            jax.ShapeDtypeStruct((TRAJ, 32, LATENT_WIDTH), BF16),
            jax.ShapeDtypeStruct((1,), F32),
        ],
        input_output_aliases={7 + k: k for k in range(len(so_far))},
        compiler_params=params(10),
        cost_estimate=cost(1e8, 4e6),
        name="attend",
    )(late, tp_index, length, mine, other, hbm(queries), fresh, *so_far)


def once_kernel(*refs):
    refs[-1][0] = 0.0


def once(*arrays):
    return pl.pallas_call(
        once_kernel,
        in_specs=[pl.BlockSpec(memory_space=pl.ANY)] * len(arrays),
        out_specs=smem(),
        out_shape=jax.ShapeDtypeStruct((1,), F32),
        compiler_params=params(1),
        cost_estimate=cost(1, 4),
        name="once",
    )(*arrays)


def swap(x, axis):
    return lax.ppermute(x, axis, [(0, 1), (1, 0)])


def z_shift(x, by):
    return lax.ppermute(x, "z", [(i, (i + by) % NZ) for i in range(NZ)])


def plane_shift(x, dx, dy):
    return lax.ppermute(
        x,
        ("xh", "y"),
        [
            (a * NY + b, ((a + dx) % NX) * NY + (b + dy) % NY)
            for a in range(NX)
            for b in range(NY)
        ],
    )


def on_device(
    latent_pages,
    page_table,
    lengths,
    new_place,
    queries,
    fresh_latent,
    hidden_states,
    routing,
    route_weight,
    gate_value,
    gate_scale,
    up_value,
    up_scale,
    down_value,
    down_scale,
):
    xh, z, y, tp = (lax.axis_index(name) for name in ("xh", "z", "y", "tp"))
    tp_index = tp.astype(I32).reshape(1)
    place = jnp.stack([xh, z, y]).astype(I32)

    own = jnp.concatenate(
        [hidden_states, jnp.pad(routing.astype(BF16), ((0, 0), (0, BLOCK - 8)))], axis=1
    )
    up_way, down_way = [own, z_shift(own, 1)], [own, z_shift(own, -1)]
    down_send = scale_down(1 - tp_index, down_value, down_scale)
    down_tp = swap(down_send, "tp")

    owner, slot = new_place // TRAJ, new_place % TRAJ
    to_owner = owner[None, :] == jnp.asarray(PLANE_MAJOR)[:, None]
    mine = lax.dynamic_slice_in_dim(page_table, tp * 2, 2, 1)
    facts = jnp.concatenate([mine, slot[:, None] + 1, lengths[:, None]], axis=1)
    index = jnp.sum(jnp.where(to_owner[:, :, None], facts[None], 0), axis=1)
    index = index - (jnp.arange(4) == 2).astype(I32)[None, :]
    leaving = collect(index, latent_pages, once(up_way[1], down_way[1])).reshape(8, 8, 32, LANES)
    midway = lax.all_to_all(leaving, ("xh", "y"), split_axis=0, concat_axis=0, tiled=True)
    for step in range(1, 4):
        up_way.append(z_shift(up_way[-1], 1))
        if step < 3:
            down_way.append(z_shift(down_way[-1], -1))
    behind = np.array([0, 1, 2, 3, 4, -1, -2, -3], np.int32)

    gate = scale_wide(gate_value, gate_scale, once(up_way[1], down_way[1]))
    up = scale_wide(up_value, up_scale, once(up_way[2], down_way[2], down_tp))
    gate_far, up_far = swap(gate, "pool"), swap(up, "pool")

    midway = regroup(
        midway, once(up_way[4], down_way[3], gate_far, up_far)
    )
    picked = pick_rows(place, up_way + down_way[1:])
    tokens = list(picked)
    for peer in PEER_ORDER[:7]:
        tokens[peer] = plane_shift(picked[peer], peer // NY, peer % NY)

    down_keep = scale_down(tp_index, down_value, down_scale, once(picked[5]))
    down_far, down_tp_far = swap(down_keep, "pool"), swap(down_tp, "pool")

    arrived = lax.all_to_all(midway, "z", split_axis=0, concat_axis=0, tiled=True)

    act, act_far = hidden_units(tokens, gate, up), hidden_units(tokens, gate_far, up_far)
    act_tp, act_tp_far = swap(act, "tp"), swap(act_far, "tp")
    group = jnp.arange(EP, dtype=I32)
    order = (
        ((xh + (group >> 5)) % NX) * NZ + (z - jnp.tile(jnp.asarray(behind), 8)) % NZ
    ) * NY + (y - (group >> 3)) % NY
    out_rows = down_rows(
        order,
        [act, act_far, act_tp, act_tp_far],
        [down_keep, down_far, down_tp, down_tp_far],
    )
    returned = lax.all_to_all(
        out_rows, ("xh", "z", "y"), split_axis=0, concat_axis=0, tiled=True
    )

    arrived = arrived.reshape(EP, 32, LANES)
    labels = arrived[:, 0, LATENT : LATENT + 2].astype(I32)
    taken = labels[:, 0][None, :] == jnp.arange(TRAJ, dtype=I32)[:, None]
    source = jnp.sum(jnp.where(taken, jnp.arange(EP, dtype=I32)[None, :], 0), axis=1)
    length = jnp.sum(jnp.where(taken, labels[:, 1][None, :], 0), axis=1)
    fresh = fresh_latent.reshape(TRAJ, 1, LATENT)
    late = once(out_rows)
    halves = compact(source, arrived, late)
    others = [swap(part, "tp") for part in halves]
    so_far = attend(0, late, tp_index, length, halves[0], others[0], queries, fresh)
    expert_mix, late = blend(so_far[2], routing, route_weight, returned)
    new_cache, attention, _ = attend(
        1, late, tp_index, length, halves[1], others[1], queries, fresh, *so_far[:2]
    )
    return new_cache, attention, expert_mix


def solution(mesh):
    grid = Mesh(mesh.devices.reshape(2, NX, NZ, NY, 2), ("pool", "xh", "z", "y", "tp"))
    ep = ("xh", "z", "y")
    rows = ("pool",) + ep
    placed = (
        P(rows, None, None),
        P(rows, None),
        P(rows),
        P(rows),
        P(rows, "tp", None),
        P(rows, None),
        P(rows, None),
        P(rows, None),
        P(rows, None),
        P(ep, None, ("pool", "tp")),
        P(ep, None, ("pool", "tp")),
        P(ep, None, ("pool", "tp")),
        P(ep, None, ("pool", "tp")),
        P(ep, ("pool", "tp"), None),
        P(ep, ("pool", "tp"), None),
    )
    return jax.shard_map(
        on_device,
        mesh=grid,
        in_specs=placed,
        out_specs=(P(rows, None, None), P(rows, "tp", None), P(rows, "tp")),
        check_vma=False,
    )
```

```python
import functools

import jax
import jax.numpy as jnp
import numpy as np
from jax import lax
from jax.experimental import pallas as pl
from jax.experimental.pallas import tpu as pltpu
from jax.sharding import Mesh, PartitionSpec as P

F32, BF16, I32 = jnp.float32, jnp.bfloat16, jnp.int32
LATENT_WIDTH = 512
BLOCK = 128
MAXLEN = 64
LATENT = 576
LANES = 640
D = 3584
HALF_D = 1792
TRAJ = 32
CAP = 8
NZ, NY, NX = 8, 4, 2
EP = NZ * NY * NX
SCORE_SCALE = 192.0 ** (-0.5)
MB = 1024 * 1024

SMEM = pltpu.SMEM
PLANE_MAJOR = np.arange(EP, dtype=np.int32).reshape(NX, NZ, NY).transpose(0, 2, 1).reshape(-1)


def whole(shape):
    return pl.BlockSpec(shape, lambda *_: (0,) * len(shape))


def smem():
    return pl.BlockSpec(memory_space=SMEM)


def hbm(*arrays):
    kept = tuple(pltpu.with_memory_space_constraint(x, pltpu.HBM) for x in arrays)
    return kept if len(kept) > 1 else kept[0]


def in_hbm(shape):
    return jax.ShapeDtypeStruct(shape, BF16)


def params(mb):
    return pltpu.CompilerParams(vmem_limit_bytes=mb * MB)


def cost(flops, nbytes):
    return pl.CostEstimate(flops=int(flops), bytes_accessed=int(nbytes), transcendentals=0)


def wide_kernel(scale, value, *rest):
    out = rest[-1]
    first = pl.program_id(0) == 0
    for f in range(2):
        for k in range(14):
            rows, cols = slice(k * BLOCK, (k + 1) * BLOCK), slice(f * BLOCK, (f + 1) * BLOCK)
            by = jnp.where(first, scale[f : f + 1, k : k + 1], scale[f : f + 1, 14 + k : 15 + k])
            out[rows, cols] = (value[0, rows, cols].astype(F32) * by).astype(BF16)


def scale_wide(value, scale, *before):
    return pl.pallas_call(
        wide_kernel,
        grid=(2,),
        in_specs=[whole((2, 28)), pl.BlockSpec((1, D // 2, 256), lambda i: (0, i, 0))]
        + [smem()] * len(before),
        out_specs=pl.BlockSpec((D // 2, 256), lambda i: (i, 0)),
        out_shape=jax.ShapeDtypeStruct((D, 256), BF16),
        compiler_params=params(8),
        cost_estimate=cost(1e6, 4e6),
        name="scale_wide",
    )(scale[0].T.astype(F32), hbm(value), *before)


def narrow_kernel(half_ref, scale, value, *rest):
    out = rest[-1]
    first = half_ref[0] == 0
    for a in range(2):
        for k in range(14):
            rows, cols = slice(a * BLOCK, (a + 1) * BLOCK), slice(k * BLOCK, (k + 1) * BLOCK)
            by = jnp.where(first, scale[a : a + 1, k : k + 1], scale[a : a + 1, 14 + k : 15 + k])
            out[rows, cols] = (value[0, rows, cols].astype(F32) * by).astype(BF16)


def scale_down(half, value, scale, *before):
    return pl.pallas_call(
        narrow_kernel,
        grid_spec=pltpu.PrefetchScalarGridSpec(
            num_scalar_prefetch=1,
            grid=(1,),
            in_specs=[
                pl.BlockSpec((2, 28), lambda i, h: (0, 0)),
                pl.BlockSpec((1, 256, HALF_D), lambda i, h: (0, 0, h[0])),
            ]
            + [smem()] * len(before),
            out_specs=pl.BlockSpec((256, HALF_D), lambda i, h: (0, 0)),
        ),
        out_shape=jax.ShapeDtypeStruct((256, HALF_D), BF16),
        compiler_params=params(8),
        cost_estimate=cost(1e6, 2e6),
        name="scale_down",
    )(half, scale[0].astype(F32), hbm(value), *before)


def named_by(routing, experts):
    marks = jnp.zeros((routing.shape[0], experts.shape[1]), F32)
    for k in range(routing.shape[1]):
        marks = marks + (routing[:, k : k + 1] == experts).astype(F32)
    return marks


def earlier(marks):
    n = marks.shape[0]
    lower = (
        lax.broadcasted_iota(I32, (n, n), 0) > lax.broadcasted_iota(I32, (n, n), 1)
    ).astype(BF16)
    return jnp.dot(lower, marks.astype(BF16), preferred_element_type=F32)


def pick_kernel(place_ref, *refs):
    blocks, outs = refs[:NZ], refs[NZ:]
    xh, z, y = place_ref[0], place_ref[1], place_ref[2]
    column = lax.broadcasted_iota(I32, (1, EP), 1)
    peer, slot = column >> 3, column & 7
    experts = (((peer >> 2) ^ xh) * NZ + z) * NY + (((peer & 3) + y) & 3)
    for b, block in enumerate(blocks):
        marks = named_by(block[:, D : D + 8].astype(F32).astype(I32), experts)
        chosen = jnp.where(earlier(marks) == slot.astype(F32), marks, 0.0).astype(BF16)
        rows = lax.dot_general(
            chosen, block[:, :D], (((0,), (0,)), ((), ())), preferred_element_type=F32
        ).astype(BF16)
        for r, out in enumerate(outs):
            out[b * CAP : (b + 1) * CAP, :] = rows[r * CAP : (r + 1) * CAP, :]


def pick_rows(place, blocks):
    vmem = pl.BlockSpec(memory_space=pltpu.VMEM)
    return pl.pallas_call(
        pick_kernel,
        in_specs=[smem()] + [vmem] * NZ,
        out_specs=[vmem] * 8,
        out_shape=[jax.ShapeDtypeStruct((NZ * CAP, D), BF16)] * 8,
        compiler_params=params(6),
        cost_estimate=cost(1e9, 6e6),
        name="pick_rows",
    )(place, *blocks)


PEER_ORDER = (4, 5, 6, 7, 1, 2, 3, 0)


def hidden_kernel(*refs):
    tokens, (gate, up, out, x) = refs[:8], refs[8:]
    for r, token in zip(PEER_ORDER, tokens):
        x[r * 64 : (r + 1) * 64, :] = token[...]
    for half in range(2):
        rows = slice(half * 256, (half + 1) * 256)
        g = jnp.dot(x[rows, :], gate[...], preferred_element_type=F32)
        u = jnp.dot(x[rows, :], up[...], preferred_element_type=F32)
        out[rows, :] = (g / (1.0 + jnp.exp(-g)) * u).astype(BF16)


def hidden_units(tokens, gate, up):
    vmem = pl.BlockSpec(memory_space=pltpu.VMEM)
    return pl.pallas_call(
        hidden_kernel,
        in_specs=[vmem] * 10,
        out_specs=vmem,
        out_shape=jax.ShapeDtypeStruct((512, 256), BF16),
        scratch_shapes=[pltpu.VMEM((512, D), BF16)],
        compiler_params=params(10),
        cost_estimate=cost(1.9e9, 8e6),
        name="hidden_units",
    )(*[tokens[r] for r in PEER_ORDER], gate, up)


def down_kernel(order_ref, h0, h1, h2, h3, w0, w1, w2, w3, out):
    h = jnp.concatenate([part[...] for part in (h0, h1, h2, h3)], axis=1)
    for c in range(HALF_D // 256):
        cols = slice(c * 256, (c + 1) * 256)
        w = jnp.concatenate([p[:, cols] for p in (w0, w1, w2, w3)], axis=0)
        rows = jnp.dot(h, w, preferred_element_type=F32)
        for group in range(EP):
            out[order_ref[group], :, cols] = rows[group * CAP : (group + 1) * CAP, :].astype(BF16)


def down_rows(order, parts, weights):
    vmem = pl.BlockSpec(memory_space=pltpu.VMEM)
    return pl.pallas_call(
        down_kernel,
        in_specs=[smem()] + [vmem] * 8,
        out_specs=vmem,
        out_shape=jax.ShapeDtypeStruct((EP, CAP, HALF_D), BF16),
        compiler_params=params(10),
        cost_estimate=cost(1.9e9, 7e6),
        name="down_rows",
    )(order, *parts, *weights)


def blend_kernel(late_ref, routing_ref, weight_ref, rows_ref, out, done):
    done[0] = 0.0
    column = lax.broadcasted_iota(I32, (1, EP * CAP), 1)
    experts, slot = column >> 3, column & 7
    routing, weight = routing_ref[...], weight_ref[...]
    marks = jnp.zeros((TRAJ, EP * CAP), F32)
    share = jnp.zeros((TRAJ, EP * CAP), F32)
    for k in range(8):
        hit = routing[:, k : k + 1] == experts
        marks = marks + hit.astype(F32)
        share = share + jnp.where(hit, weight[:, k : k + 1], 0.0)
    share = jnp.where(earlier(marks) == slot.astype(F32), share, 0.0)
    high = share.astype(BF16)
    low = (share - high.astype(F32)).astype(BF16)
    rows = rows_ref[...].reshape(EP * CAP, rows_ref.shape[2])
    out[...] = (
        jnp.dot(high, rows, preferred_element_type=F32)
        + jnp.dot(low, rows, preferred_element_type=F32)
    ).astype(BF16)


def blend(late, routing, weight, rows):
    wide = 896
    return pl.pallas_call(
        blend_kernel,
        grid=(HALF_D // wide,),
        in_specs=[
            smem(),
            whole((TRAJ, 8)),
            whole((TRAJ, 8)),
            pl.BlockSpec((EP, CAP, wide), lambda i: (0, 0, i)),
        ],
        out_specs=[pl.BlockSpec((TRAJ, wide), lambda i: (0, i)), smem()],
        out_shape=[
            jax.ShapeDtypeStruct((TRAJ, HALF_D), BF16),
            jax.ShapeDtypeStruct((1,), F32),
        ],
        compiler_params=params(10),
        cost_estimate=cost(1e8, 2e6),
        name="blend",
    )(late, routing, weight, rows)


def collect_kernel(index_ref, pages, *rest):
    out = rest[-1]
    step = pl.program_id(0)
    lane = lax.broadcasted_iota(I32, (32, LANES - LATENT), 1)
    for i in range(16):
        j = step * 16 + i
        out[i, 0:16, 0:LATENT] = pages[index_ref[j, 0]]
        out[i, 16:32, 0:LATENT] = pages[index_ref[j, 1]]
        slot, length = index_ref[j, 2].astype(F32), index_ref[j, 3].astype(F32)
        out[i, :, LATENT:LANES] = jnp.where(lane == 0, slot, length).astype(BF16)


def collect(index, pages, *before):
    return pl.pallas_call(
        collect_kernel,
        grid=(EP // 16,),
        in_specs=[smem(), whole(pages.shape)] + [smem()] * len(before),
        out_specs=pl.BlockSpec((16, 32, LANES), lambda i: (i, 0, 0)),
        out_shape=pltpu.HBM((EP, 32, LANES), BF16),
        compiler_params=params(10),
        cost_estimate=cost(1e6, 6e6),
        name="collect",
    )(index, pages, *before)


def regroup_kernel(midway, *rest):
    out = rest[-1]
    for i in range(4):
        out[i] = midway[:, i]


def regroup(midway, *before):
    return pl.pallas_call(
        regroup_kernel,
        grid=(2,),
        in_specs=[pl.BlockSpec((8, 4, 32, LANES), lambda i: (0, i, 0, 0))] + [smem()] * len(before),
        out_specs=pl.BlockSpec((4, 8, 32, LANES), lambda i: (i, 0, 0, 0)),
        out_shape=pltpu.HBM((8, 8, 32, LANES), BF16),
        compiler_params=params(8),
        cost_estimate=cost(1e6, 6e6),
        name="regroup",
    )(hbm(midway), *before)


def compact_kernel(source_ref, arrived, late_ref, first, second):
    step = pl.program_id(0) * 8
    for s in range(8):
        first[s] = arrived[source_ref[step + s]]
        second[s] = arrived[source_ref[TRAJ // 2 + step + s]]


def compact(source, arrived, late):
    half = (TRAJ // 2, 32, LANES)
    return pl.pallas_call(
        compact_kernel,
        grid=(2,),
        in_specs=[smem(), whole(arrived.shape), smem()],
        out_specs=[pl.BlockSpec((8, 32, LANES), lambda i: (i, 0, 0))] * 2,
        out_shape=[in_hbm(half)] * 2,
        compiler_params=params(10),
        cost_estimate=cost(1e6, 4e6),
        name="compact",
    )(source, hbm(arrived), late)


ATTEND_STEP = 8


def attend_kernel(start, late_ref, tp_ref, length_ref, mine, other, queries, fresh, *rest):
    cache_out, out, done = rest[-3:]
    done[0] = 0.0
    step = pl.program_id(0) + start
    first = tp_ref[0] == 0
    row = lax.broadcasted_iota(I32, (MAXLEN, LATENT), 0).astype(F32).astype(BF16)
    column = lax.broadcasted_iota(I32, (TRAJ, MAXLEN), 1)
    scores = []
    for i in range(ATTEND_STEP):
        length = length_ref[step * ATTEND_STEP + i]
        edge = length.astype(F32).astype(BF16)
        a, b = mine[i, :, :LATENT], other[i, :, :LATENT]
        old = jnp.concatenate([jnp.where(first, a, b), jnp.where(first, b, a)], axis=0)
        new = jnp.broadcast_to(fresh[i], (MAXLEN, LATENT))
        zero = jnp.zeros((), BF16)
        cache = jnp.where(row < edge, old, jnp.where(row == edge, new, zero))
        cache_out[i] = cache
        score = lax.dot_general(
            queries[i], cache, (((1,), (1,)), ((), ())), preferred_element_type=F32
        )
        scores.append(jnp.where(column <= length, score * SCORE_SCALE, -jnp.inf))
    scores = jnp.concatenate(scores, axis=0)
    top = jnp.max(scores, axis=1, keepdims=True)
    weight = jnp.exp(scores - top)
    weight = (weight * (1.0 / jnp.sum(weight, axis=1, keepdims=True))).astype(BF16)
    for i in range(ATTEND_STEP):
        out[i] = jnp.dot(
            weight[i * TRAJ : (i + 1) * TRAJ],
            cache_out[i, :, :LATENT_WIDTH],
            preferred_element_type=F32,
        ).astype(BF16)


def attend(half, late, tp_index, length, mine, other, queries, fresh, *so_far):
    n = ATTEND_STEP
    start = half * (TRAJ // 2 // n)
    there = pl.BlockSpec(memory_space=pl.ANY)
    return pl.pallas_call(
        functools.partial(attend_kernel, start),
        grid=(TRAJ // 2 // n,),
        in_specs=[
            smem(),
            smem(),
            smem(),
            pl.BlockSpec((n, 32, LANES), lambda i: (i, 0, 0)),
            pl.BlockSpec((n, 32, LANES), lambda i: (i, 0, 0)),
            pl.BlockSpec((n, 32, LATENT), lambda i: (i + start, 0, 0)),
            pl.BlockSpec((n, 1, LATENT), lambda i: (i + start, 0, 0)),
        ]
        + [there] * len(so_far),
        out_specs=[
            pl.BlockSpec((n, MAXLEN, LATENT), lambda i: (i + start, 0, 0)),
            pl.BlockSpec((n, 32, LATENT_WIDTH), lambda i: (i + start, 0, 0)),
            smem(),
        ],
        out_shape=[
            jax.ShapeDtypeStruct((TRAJ, MAXLEN, LATENT), BF16),
            jax.ShapeDtypeStruct((TRAJ, 32, LATENT_WIDTH), BF16),
            jax.ShapeDtypeStruct((1,), F32),
        ],
        input_output_aliases={7 + k: k for k in range(len(so_far))},
        compiler_params=params(10),
        cost_estimate=cost(1e8, 4e6),
        name="attend",
    )(late, tp_index, length, mine, other, hbm(queries), fresh, *so_far)


def once_kernel(*refs):
    refs[-1][0] = 0.0


def once(*arrays):
    return pl.pallas_call(
        once_kernel,
        in_specs=[pl.BlockSpec(memory_space=pl.ANY)] * len(arrays),
        out_specs=smem(),
        out_shape=jax.ShapeDtypeStruct((1,), F32),
        compiler_params=params(1),
        cost_estimate=cost(1, 4),
        name="once",
    )(*arrays)


def swap(x, axis):
    return lax.ppermute(x, axis, [(0, 1), (1, 0)])


def z_shift(x, by):
    return lax.ppermute(x, "z", [(i, (i + by) % NZ) for i in range(NZ)])


def plane_shift(x, dx, dy):
    return lax.ppermute(
        x,
        ("xh", "y"),
        [
            (a * NY + b, ((a + dx) % NX) * NY + (b + dy) % NY)
            for a in range(NX)
            for b in range(NY)
        ],
    )


def on_device(
    latent_pages,
    page_table,
    lengths,
    new_place,
    queries,
    fresh_latent,
    hidden_states,
    routing,
    route_weight,
    gate_value,
    gate_scale,
    up_value,
    up_scale,
    down_value,
    down_scale,
):
    xh, z, y, tp = (lax.axis_index(name) for name in ("xh", "z", "y", "tp"))
    tp_index = tp.astype(I32).reshape(1)
    place = jnp.stack([xh, z, y]).astype(I32)

    own = jnp.concatenate(
        [hidden_states, jnp.pad(routing.astype(BF16), ((0, 0), (0, BLOCK - 8)))], axis=1
    )
    up_way, down_way = [own, z_shift(own, 1)], [own, z_shift(own, -1)]
    down_send = scale_down(1 - tp_index, down_value, down_scale)
    down_tp = swap(down_send, "tp")

    owner, slot = new_place // TRAJ, new_place % TRAJ
    to_owner = owner[None, :] == jnp.asarray(PLANE_MAJOR)[:, None]
    mine = lax.dynamic_slice_in_dim(page_table, tp * 2, 2, 1)
    facts = jnp.concatenate([mine, slot[:, None] + 1, lengths[:, None]], axis=1)
    index = jnp.sum(jnp.where(to_owner[:, :, None], facts[None], 0), axis=1)
    index = index - (jnp.arange(4) == 2).astype(I32)[None, :]
    leaving = collect(index, latent_pages, once(up_way[1], down_way[1])).reshape(8, 8, 32, LANES)
    midway = lax.all_to_all(leaving, ("xh", "y"), split_axis=0, concat_axis=0, tiled=True)
    for step in range(1, 4):
        up_way.append(z_shift(up_way[-1], 1))
        if step < 3:
            down_way.append(z_shift(down_way[-1], -1))
    behind = np.array([0, 1, 2, 3, 4, -1, -2, -3], np.int32)

    gate = scale_wide(gate_value, gate_scale, once(up_way[1], down_way[1]))
    up = scale_wide(up_value, up_scale, once(up_way[2], down_way[2], down_tp))
    gate_far, up_far = swap(gate, "pool"), swap(up, "pool")

    midway = regroup(
        midway, once(up_way[4], down_way[3], gate_far, up_far)
    )
    picked = pick_rows(place, up_way + down_way[1:])
    tokens = list(picked)
    for peer in PEER_ORDER[:7]:
        tokens[peer] = plane_shift(picked[peer], peer // NY, peer % NY)

    down_keep = scale_down(tp_index, down_value, down_scale, once(picked[5]))
    down_far, down_tp_far = swap(down_keep, "pool"), swap(down_tp, "pool")

    arrived = lax.all_to_all(midway, "z", split_axis=0, concat_axis=0, tiled=True)

    act, act_far = hidden_units(tokens, gate, up), hidden_units(tokens, gate_far, up_far)
    act_tp, act_tp_far = swap(act, "tp"), swap(act_far, "tp")
    group = jnp.arange(EP, dtype=I32)
    order = (
        ((xh + (group >> 5)) % NX) * NZ + (z - jnp.tile(jnp.asarray(behind), 8)) % NZ
    ) * NY + (y - (group >> 3)) % NY
    out_rows = down_rows(
        order,
        [act, act_far, act_tp, act_tp_far],
        [down_keep, down_far, down_tp, down_tp_far],
    )
    returned = lax.all_to_all(
        out_rows, ("xh", "z", "y"), split_axis=0, concat_axis=0, tiled=True
    )

    arrived = arrived.reshape(EP, 32, LANES)
    labels = arrived[:, 0, LATENT : LATENT + 2].astype(I32)
    taken = labels[:, 0][None, :] == jnp.arange(TRAJ, dtype=I32)[:, None]
    source = jnp.sum(jnp.where(taken, jnp.arange(EP, dtype=I32)[None, :], 0), axis=1)
    length = jnp.sum(jnp.where(taken, labels[:, 1][None, :], 0), axis=1)
    fresh = fresh_latent.reshape(TRAJ, 1, LATENT)
    late = once(out_rows)
    halves = compact(source, arrived, late)
    others = [swap(part, "tp") for part in halves]
    so_far = attend(0, late, tp_index, length, halves[0], others[0], queries, fresh)
    expert_mix, late = blend(so_far[2], routing, route_weight, returned)
    new_cache, attention, _ = attend(
        1, late, tp_index, length, halves[1], others[1], queries, fresh, *so_far[:2]
    )
    return new_cache, attention, expert_mix


def solution(mesh):
    grid = Mesh(mesh.devices.reshape(2, NX, NZ, NY, 2), ("pool", "xh", "z", "y", "tp"))
    ep = ("xh", "z", "y")
    rows = ("pool",) + ep
    placed = (
        P(rows, None, None),
        P(rows, None),
        P(rows),
        P(rows),
        P(rows, "tp", None),
        P(rows, None),
        P(rows, None),
        P(rows, None),
        P(rows, None),
        P(ep, None, ("pool", "tp")),
        P(ep, None, ("pool", "tp")),
        P(ep, None, ("pool", "tp")),
        P(ep, None, ("pool", "tp")),
        P(ep, ("pool", "tp"), None),
        P(ep, ("pool", "tp"), None),
    )
    return jax.shard_map(
        on_device,
        mesh=grid,
        in_specs=placed,
        out_specs=(P(rows, None, None), P(rows, "tp", None), P(rows, "tp")),
        check_vma=False,
    )
```

```python
import functools

import jax
import jax.numpy as jnp
import numpy as np
from jax import lax
from jax.experimental import pallas as pl
from jax.experimental.pallas import tpu as pltpu
from jax.sharding import Mesh, PartitionSpec as P

F32, BF16, I32 = jnp.float32, jnp.bfloat16, jnp.int32
LATENT_WIDTH = 512
BLOCK = 128
MAXLEN = 64
LATENT = 576
LANES = 640
D = 3584
HALF_D = 1792
TRAJ = 32
CAP = 8
NZ, NY, NX = 8, 4, 2
EP = NZ * NY * NX
SCORE_SCALE = 192.0 ** (-0.5)
MB = 1024 * 1024

SMEM = pltpu.SMEM
PLANE_MAJOR = np.arange(EP, dtype=np.int32).reshape(NX, NZ, NY).transpose(0, 2, 1).reshape(-1)


def whole(shape):
    return pl.BlockSpec(shape, lambda *_: (0,) * len(shape))


def smem():
    return pl.BlockSpec(memory_space=SMEM)


def hbm(*arrays):
    kept = tuple(pltpu.with_memory_space_constraint(x, pltpu.HBM) for x in arrays)
    return kept if len(kept) > 1 else kept[0]


def in_hbm(shape):
    return jax.ShapeDtypeStruct(shape, BF16)


def params(mb):
    return pltpu.CompilerParams(vmem_limit_bytes=mb * MB)


def cost(flops, nbytes):
    return pl.CostEstimate(flops=int(flops), bytes_accessed=int(nbytes), transcendentals=0)


def wide_kernel(scale, value, *rest):
    out = rest[-1]
    first = pl.program_id(0) == 0
    for f in range(2):
        for k in range(14):
            rows, cols = slice(k * BLOCK, (k + 1) * BLOCK), slice(f * BLOCK, (f + 1) * BLOCK)
            by = jnp.where(first, scale[f : f + 1, k : k + 1], scale[f : f + 1, 14 + k : 15 + k])
            out[rows, cols] = (value[0, rows, cols].astype(F32) * by).astype(BF16)


def scale_wide(value, scale, *before):
    return pl.pallas_call(
        wide_kernel,
        grid=(2,),
        in_specs=[whole((2, 28)), pl.BlockSpec((1, D // 2, 256), lambda i: (0, i, 0))]
        + [smem()] * len(before),
        out_specs=pl.BlockSpec((D // 2, 256), lambda i: (i, 0)),
        out_shape=jax.ShapeDtypeStruct((D, 256), BF16),
        compiler_params=params(8),
        cost_estimate=cost(1e6, 4e6),
        name="scale_wide",
    )(scale[0].T.astype(F32), hbm(value), *before)


def narrow_kernel(half_ref, scale, value, *rest):
    out = rest[-1]
    first = half_ref[0] == 0
    for a in range(2):
        for k in range(14):
            rows, cols = slice(a * BLOCK, (a + 1) * BLOCK), slice(k * BLOCK, (k + 1) * BLOCK)
            by = jnp.where(first, scale[a : a + 1, k : k + 1], scale[a : a + 1, 14 + k : 15 + k])
            out[rows, cols] = (value[0, rows, cols].astype(F32) * by).astype(BF16)


def scale_down(half, value, scale, *before):
    return pl.pallas_call(
        narrow_kernel,
        grid_spec=pltpu.PrefetchScalarGridSpec(
            num_scalar_prefetch=1,
            grid=(1,),
            in_specs=[
                pl.BlockSpec((2, 28), lambda i, h: (0, 0)),
                pl.BlockSpec((1, 256, HALF_D), lambda i, h: (0, 0, h[0])),
            ]
            + [smem()] * len(before),
            out_specs=pl.BlockSpec((256, HALF_D), lambda i, h: (0, 0)),
        ),
        out_shape=jax.ShapeDtypeStruct((256, HALF_D), BF16),
        compiler_params=params(8),
        cost_estimate=cost(1e6, 2e6),
        name="scale_down",
    )(half, scale[0].astype(F32), hbm(value), *before)


def named_by(routing, experts):
    marks = jnp.zeros((routing.shape[0], experts.shape[1]), F32)
    for k in range(routing.shape[1]):
        marks = marks + (routing[:, k : k + 1] == experts).astype(F32)
    return marks


def earlier(marks):
    n = marks.shape[0]
    lower = (
        lax.broadcasted_iota(I32, (n, n), 0) > lax.broadcasted_iota(I32, (n, n), 1)
    ).astype(BF16)
    return jnp.dot(lower, marks.astype(BF16), preferred_element_type=F32)


def pick_kernel(place_ref, *refs):
    blocks, outs = refs[:NZ], refs[NZ:]
    xh, z, y = place_ref[0], place_ref[1], place_ref[2]
    column = lax.broadcasted_iota(I32, (1, EP), 1)
    peer, slot = column >> 3, column & 7
    experts = (((peer >> 2) ^ xh) * NZ + z) * NY + (((peer & 3) + y) & 3)
    for b, block in enumerate(blocks):
        marks = named_by(block[:, D : D + 8].astype(F32).astype(I32), experts)
        chosen = jnp.where(earlier(marks) == slot.astype(F32), marks, 0.0).astype(BF16)
        rows = lax.dot_general(
            chosen, block[:, :D], (((0,), (0,)), ((), ())), preferred_element_type=F32
        ).astype(BF16)
        for r, out in enumerate(outs):
            out[b * CAP : (b + 1) * CAP, :] = rows[r * CAP : (r + 1) * CAP, :]


def pick_rows(place, blocks):
    vmem = pl.BlockSpec(memory_space=pltpu.VMEM)
    return pl.pallas_call(
        pick_kernel,
        in_specs=[smem()] + [vmem] * NZ,
        out_specs=[vmem] * 8,
        out_shape=[jax.ShapeDtypeStruct((NZ * CAP, D), BF16)] * 8,
        compiler_params=params(6),
        cost_estimate=cost(1e9, 6e6),
        name="pick_rows",
    )(place, *blocks)


PEER_ORDER = (4, 1, 5, 2, 7, 6, 3, 0)


def hidden_kernel(*refs):
    tokens, (gate, up, out, x) = refs[:8], refs[8:]
    for r, token in zip(PEER_ORDER, tokens):
        x[r * 64 : (r + 1) * 64, :] = token[...]
    for half in range(2):
        rows = slice(half * 256, (half + 1) * 256)
        g = jnp.dot(x[rows, :], gate[...], preferred_element_type=F32)
        u = jnp.dot(x[rows, :], up[...], preferred_element_type=F32)
        out[rows, :] = (g / (1.0 + jnp.exp(-g)) * u).astype(BF16)


def hidden_units(tokens, gate, up):
    vmem = pl.BlockSpec(memory_space=pltpu.VMEM)
    return pl.pallas_call(
        hidden_kernel,
        in_specs=[vmem] * 10,
        out_specs=vmem,
        out_shape=jax.ShapeDtypeStruct((512, 256), BF16),
        scratch_shapes=[pltpu.VMEM((512, D), BF16)],
        compiler_params=params(10),
        cost_estimate=cost(1.9e9, 8e6),
        name="hidden_units",
    )(*[tokens[r] for r in PEER_ORDER], gate, up)


def down_kernel(order_ref, h0, h1, h2, h3, w0, w1, w2, w3, out):
    h = jnp.concatenate([part[...] for part in (h0, h1, h2, h3)], axis=1)
    for c in range(HALF_D // 256):
        cols = slice(c * 256, (c + 1) * 256)
        w = jnp.concatenate([p[:, cols] for p in (w0, w1, w2, w3)], axis=0)
        rows = jnp.dot(h, w, preferred_element_type=F32)
        for group in range(EP):
            out[order_ref[group], :, cols] = rows[group * CAP : (group + 1) * CAP, :].astype(BF16)


def down_rows(order, parts, weights):
    vmem = pl.BlockSpec(memory_space=pltpu.VMEM)
    return pl.pallas_call(
        down_kernel,
        in_specs=[smem()] + [vmem] * 8,
        out_specs=vmem,
        out_shape=jax.ShapeDtypeStruct((EP, CAP, HALF_D), BF16),
        compiler_params=params(10),
        cost_estimate=cost(1.9e9, 7e6),
        name="down_rows",
    )(order, *parts, *weights)


def blend_kernel(late_ref, routing_ref, weight_ref, rows_ref, out, done):
    done[0] = 0.0
    column = lax.broadcasted_iota(I32, (1, EP * CAP), 1)
    experts, slot = column >> 3, column & 7
    routing, weight = routing_ref[...], weight_ref[...]
    marks = jnp.zeros((TRAJ, EP * CAP), F32)
    share = jnp.zeros((TRAJ, EP * CAP), F32)
    for k in range(8):
        hit = routing[:, k : k + 1] == experts
        marks = marks + hit.astype(F32)
        share = share + jnp.where(hit, weight[:, k : k + 1], 0.0)
    share = jnp.where(earlier(marks) == slot.astype(F32), share, 0.0)
    high = share.astype(BF16)
    low = (share - high.astype(F32)).astype(BF16)
    rows = rows_ref[...].reshape(EP * CAP, rows_ref.shape[2])
    out[...] = (
        jnp.dot(high, rows, preferred_element_type=F32)
        + jnp.dot(low, rows, preferred_element_type=F32)
    ).astype(BF16)


def blend(late, routing, weight, rows):
    wide = 896
    return pl.pallas_call(
        blend_kernel,
        grid=(HALF_D // wide,),
        in_specs=[
            smem(),
            whole((TRAJ, 8)),
            whole((TRAJ, 8)),
            pl.BlockSpec((EP, CAP, wide), lambda i: (0, 0, i)),
        ],
        out_specs=[pl.BlockSpec((TRAJ, wide), lambda i: (0, i)), smem()],
        out_shape=[
            jax.ShapeDtypeStruct((TRAJ, HALF_D), BF16),
            jax.ShapeDtypeStruct((1,), F32),
        ],
        compiler_params=params(10),
        cost_estimate=cost(1e8, 2e6),
        name="blend",
    )(late, routing, weight, rows)


def collect_kernel(index_ref, pages, *rest):
    out = rest[-1]
    step = pl.program_id(0)
    lane = lax.broadcasted_iota(I32, (32, LANES - LATENT), 1)
    for i in range(16):
        j = step * 16 + i
        out[i, 0:16, 0:LATENT] = pages[index_ref[j, 0]]
        out[i, 16:32, 0:LATENT] = pages[index_ref[j, 1]]
        slot, length = index_ref[j, 2].astype(F32), index_ref[j, 3].astype(F32)
        out[i, :, LATENT:LANES] = jnp.where(lane == 0, slot, length).astype(BF16)


def collect(index, pages, *before):
    return pl.pallas_call(
        collect_kernel,
        grid=(EP // 16,),
        in_specs=[smem(), whole(pages.shape)] + [smem()] * len(before),
        out_specs=pl.BlockSpec((16, 32, LANES), lambda i: (i, 0, 0)),
        out_shape=pltpu.HBM((EP, 32, LANES), BF16),
        compiler_params=params(10),
        cost_estimate=cost(1e6, 6e6),
        name="collect",
    )(index, pages, *before)


def regroup_kernel(midway, *rest):
    out = rest[-1]
    for i in range(4):
        out[i] = midway[:, i]


def regroup(midway, *before):
    return pl.pallas_call(
        regroup_kernel,
        grid=(2,),
        in_specs=[pl.BlockSpec((8, 4, 32, LANES), lambda i: (0, i, 0, 0))] + [smem()] * len(before),
        out_specs=pl.BlockSpec((4, 8, 32, LANES), lambda i: (i, 0, 0, 0)),
        out_shape=pltpu.HBM((8, 8, 32, LANES), BF16),
        compiler_params=params(8),
        cost_estimate=cost(1e6, 6e6),
        name="regroup",
    )(hbm(midway), *before)


def compact_kernel(source_ref, arrived, late_ref, first, second):
    for s in range(TRAJ // 2):
        first[s] = arrived[source_ref[s]]
        second[s] = arrived[source_ref[TRAJ // 2 + s]]


def compact(source, arrived, late):
    half = (TRAJ // 2, 32, LANES)
    return pl.pallas_call(
        compact_kernel,
        grid=(1,),
        in_specs=[smem(), whole(arrived.shape), smem()],
        out_specs=[whole(half)] * 2,
        out_shape=[in_hbm(half)] * 2,
        compiler_params=params(10),
        cost_estimate=cost(1e6, 4e6),
        name="compact",
    )(source, hbm(arrived), late)


ATTEND_STEP = 8


def attend_kernel(start, late_ref, tp_ref, length_ref, mine, other, queries, fresh, *rest):
    cache_out, out, done = rest[-3:]
    done[0] = 0.0
    step = pl.program_id(0) + start
    first = tp_ref[0] == 0
    row = lax.broadcasted_iota(I32, (MAXLEN, LATENT), 0).astype(F32).astype(BF16)
    column = lax.broadcasted_iota(I32, (TRAJ, MAXLEN), 1)
    scores = []
    for i in range(ATTEND_STEP):
        length = length_ref[step * ATTEND_STEP + i]
        edge = length.astype(F32).astype(BF16)
        a, b = mine[i, :, :LATENT], other[i, :, :LATENT]
        old = jnp.concatenate([jnp.where(first, a, b), jnp.where(first, b, a)], axis=0)
        new = jnp.broadcast_to(fresh[i], (MAXLEN, LATENT))
        zero = jnp.zeros((), BF16)
        cache = jnp.where(row < edge, old, jnp.where(row == edge, new, zero))
        cache_out[i] = cache
        score = lax.dot_general(
            queries[i], cache, (((1,), (1,)), ((), ())), preferred_element_type=F32
        )
        scores.append(jnp.where(column <= length, score * SCORE_SCALE, -jnp.inf))
    scores = jnp.concatenate(scores, axis=0)
    top = jnp.max(scores, axis=1, keepdims=True)
    weight = jnp.exp(scores - top)
    weight = (weight * (1.0 / jnp.sum(weight, axis=1, keepdims=True))).astype(BF16)
    for i in range(ATTEND_STEP):
        out[i] = jnp.dot(
            weight[i * TRAJ : (i + 1) * TRAJ],
            cache_out[i, :, :LATENT_WIDTH],
            preferred_element_type=F32,
        ).astype(BF16)


def attend(half, late, tp_index, length, mine, other, queries, fresh, *so_far):
    n = ATTEND_STEP
    start = half * (TRAJ // 2 // n)
    there = pl.BlockSpec(memory_space=pl.ANY)
    return pl.pallas_call(
        functools.partial(attend_kernel, start),
        grid=(TRAJ // 2 // n,),
        in_specs=[
            smem(),
            smem(),
            smem(),
            pl.BlockSpec((n, 32, LANES), lambda i: (i, 0, 0)),
            pl.BlockSpec((n, 32, LANES), lambda i: (i, 0, 0)),
            pl.BlockSpec((n, 32, LATENT), lambda i: (i + start, 0, 0)),
            pl.BlockSpec((n, 1, LATENT), lambda i: (i + start, 0, 0)),
        ]
        + [there] * len(so_far),
        out_specs=[
            pl.BlockSpec((n, MAXLEN, LATENT), lambda i: (i + start, 0, 0)),
            pl.BlockSpec((n, 32, LATENT_WIDTH), lambda i: (i + start, 0, 0)),
            smem(),
        ],
        out_shape=[
            jax.ShapeDtypeStruct((TRAJ, MAXLEN, LATENT), BF16),
            jax.ShapeDtypeStruct((TRAJ, 32, LATENT_WIDTH), BF16),
            jax.ShapeDtypeStruct((1,), F32),
        ],
        input_output_aliases={7 + k: k for k in range(len(so_far))},
        compiler_params=params(10),
        cost_estimate=cost(1e8, 4e6),
        name="attend",
    )(late, tp_index, length, mine, other, hbm(queries), fresh, *so_far)


def once_kernel(*refs):
    refs[-1][0] = 0.0


def once(*arrays):
    return pl.pallas_call(
        once_kernel,
        in_specs=[pl.BlockSpec(memory_space=pl.ANY)] * len(arrays),
        out_specs=smem(),
        out_shape=jax.ShapeDtypeStruct((1,), F32),
        compiler_params=params(1),
        cost_estimate=cost(1, 4),
        name="once",
    )(*arrays)


def swap(x, axis):
    return lax.ppermute(x, axis, [(0, 1), (1, 0)])


def z_shift(x, by):
    return lax.ppermute(x, "z", [(i, (i + by) % NZ) for i in range(NZ)])


def plane_shift(x, dx, dy):
    return lax.ppermute(
        x,
        ("xh", "y"),
        [
            (a * NY + b, ((a + dx) % NX) * NY + (b + dy) % NY)
            for a in range(NX)
            for b in range(NY)
        ],
    )


def on_device(
    latent_pages,
    page_table,
    lengths,
    new_place,
    queries,
    fresh_latent,
    hidden_states,
    routing,
    route_weight,
    gate_value,
    gate_scale,
    up_value,
    up_scale,
    down_value,
    down_scale,
):
    xh, z, y, tp = (lax.axis_index(name) for name in ("xh", "z", "y", "tp"))
    tp_index = tp.astype(I32).reshape(1)
    place = jnp.stack([xh, z, y]).astype(I32)

    own = jnp.concatenate(
        [hidden_states, jnp.pad(routing.astype(BF16), ((0, 0), (0, BLOCK - 8)))], axis=1
    )
    up_way, down_way = [own, z_shift(own, 1)], [own, z_shift(own, -1)]
    down_send = scale_down(1 - tp_index, down_value, down_scale)
    down_tp = swap(down_send, "tp")

    owner, slot = new_place // TRAJ, new_place % TRAJ
    to_owner = owner[None, :] == jnp.asarray(PLANE_MAJOR)[:, None]
    mine = lax.dynamic_slice_in_dim(page_table, tp * 2, 2, 1)
    facts = jnp.concatenate([mine, slot[:, None] + 1, lengths[:, None]], axis=1)
    index = jnp.sum(jnp.where(to_owner[:, :, None], facts[None], 0), axis=1)
    index = index - (jnp.arange(4) == 2).astype(I32)[None, :]
    leaving = collect(index, latent_pages, once(up_way[1], down_way[1])).reshape(8, 8, 32, LANES)
    midway = lax.all_to_all(leaving, ("xh", "y"), split_axis=0, concat_axis=0, tiled=True)
    for step in range(1, 4):
        up_way.append(z_shift(up_way[-1], 1))
        if step < 3:
            down_way.append(z_shift(down_way[-1], -1))
    behind = np.array([0, 1, 2, 3, 4, -1, -2, -3], np.int32)

    gate = scale_wide(gate_value, gate_scale, once(up_way[1], down_way[1]))
    up = scale_wide(up_value, up_scale, once(up_way[2], down_way[2], down_tp))
    gate_far, up_far = swap(gate, "pool"), swap(up, "pool")

    midway = regroup(
        midway, once(up_way[4], down_way[3], gate_far, up_far)
    )
    picked = pick_rows(place, up_way + down_way[1:])
    tokens = list(picked)
    for peer in PEER_ORDER[:7]:
        tokens[peer] = plane_shift(picked[peer], peer // NY, peer % NY)

    down_keep = scale_down(tp_index, down_value, down_scale, once(picked[5]))
    down_far, down_tp_far = swap(down_keep, "pool"), swap(down_tp, "pool")

    arrived = lax.all_to_all(midway, "z", split_axis=0, concat_axis=0, tiled=True)

    act, act_far = hidden_units(tokens, gate, up), hidden_units(tokens, gate_far, up_far)
    act_tp, act_tp_far = swap(act, "tp"), swap(act_far, "tp")
    group = jnp.arange(EP, dtype=I32)
    order = (
        ((xh + (group >> 5)) % NX) * NZ + (z - jnp.tile(jnp.asarray(behind), 8)) % NZ
    ) * NY + (y - (group >> 3)) % NY
    out_rows = down_rows(
        order,
        [act, act_far, act_tp, act_tp_far],
        [down_keep, down_far, down_tp, down_tp_far],
    )
    returned = lax.all_to_all(
        out_rows, ("xh", "z", "y"), split_axis=0, concat_axis=0, tiled=True
    )

    arrived = arrived.reshape(EP, 32, LANES)
    labels = arrived[:, 0, LATENT : LATENT + 2].astype(I32)
    taken = labels[:, 0][None, :] == jnp.arange(TRAJ, dtype=I32)[:, None]
    source = jnp.sum(jnp.where(taken, jnp.arange(EP, dtype=I32)[None, :], 0), axis=1)
    length = jnp.sum(jnp.where(taken, labels[:, 1][None, :], 0), axis=1)
    fresh = fresh_latent.reshape(TRAJ, 1, LATENT)
    late = once(out_rows)
    halves = compact(source, arrived, late)
    others = [swap(part, "tp") for part in halves]
    so_far = attend(0, late, tp_index, length, halves[0], others[0], queries, fresh)
    expert_mix, late = blend(so_far[2], routing, route_weight, returned)
    new_cache, attention, _ = attend(
        1, late, tp_index, length, halves[1], others[1], queries, fresh, *so_far[:2]
    )
    return new_cache, attention, expert_mix


def solution(mesh):
    grid = Mesh(mesh.devices.reshape(2, NX, NZ, NY, 2), ("pool", "xh", "z", "y", "tp"))
    ep = ("xh", "z", "y")
    rows = ("pool",) + ep
    placed = (
        P(rows, None, None),
        P(rows, None),
        P(rows),
        P(rows),
        P(rows, "tp", None),
        P(rows, None),
        P(rows, None),
        P(rows, None),
        P(rows, None),
        P(ep, None, ("pool", "tp")),
        P(ep, None, ("pool", "tp")),
        P(ep, None, ("pool", "tp")),
        P(ep, None, ("pool", "tp")),
        P(ep, ("pool", "tp"), None),
        P(ep, ("pool", "tp"), None),
    )
    return jax.shard_map(
        on_device,
        mesh=grid,
        in_specs=placed,
        out_specs=(P(rows, None, None), P(rows, "tp", None), P(rows, "tp")),
        check_vma=False,
    )
```
